128 devices in a mesh: row: 8 (over x, core), col: 16 (over y, z).
Axes of the slice: x: 4, y: 4, z: 4, core: 2. Of those that a mesh axis runs over, the one named last changes fastest.
Arguments:
- right_side: float32 [131072, 128], P(('row', 'col')), may hold values from -6 to 6
- leaf_inverse: bfloat16 [131072, 1024], P(('row', 'col')), may hold values from -0.1875 to 0.1875
- compress: bfloat16 [131072, 2048], P(('row', 'col')), may hold values from -0.1875 to 0.1875
- middle: bfloat16 [262144, 2048], P(('row', 'col')), may hold values from -0.125 to 0.125
- expand: bfloat16 [131072, 2048], P(('row', 'col')), may hold values from -0.125 to 0.125
- row_project: bfloat16 [3, 131072, 256], P(None, ('row', 'col')), may hold values from -0.1875 to 0.1875
- row_expand: bfloat16 [3, 131072, 256], P(None, ('row', 'col')), may hold values from -0.25 to 0.25
- root_project: bfloat16 [131072, 256], P(('row', 'col')), may hold values from -0.015625 to 0.015625
- root_expand: bfloat16 [131072, 256], P(('row', 'col')), may hold values from -0.375 to 0.375
- owner_map: int32 [16], replicated, may hold values from 0 to 15, each once
Outputs:
- applied: float32 [131072, 128], P(('row', 'col'))
The draws below stay inside these ranges and needn't reach their ends.
Inputs may be any that keep to these rules, and one draw needn't show every extreme that they name: owner_map names each of the 16 column positions exactly once.
All inputs are finite; a program needn't handle non-finite values.
Results may differ from the reference program's by a relative error of at most 0.004.
Values may be sent and summed in bfloat16 or wider, within the bound.
A program may use at most 128 MiB of HBM per device.

```python
import jax
import jax.numpy as jnp
from jax import lax

LEAF = 1024
W = 128
S = 128
RANK = 256
LEVELS = 3
N = 131072
N_ROW = 8
N_COL = 16
DEVICES = 128


def block_scale(stream_key, dims, split, least, high):
    level = 1.0
    for dim, parts in split:
        heights = jax.random.uniform(jax.random.fold_in(jax.random.fold_in(stream_key, 6), dim), (parts,), jnp.float32, least / len(split), high / len(split))
        level = level * jnp.repeat(jnp.exp(heights), dims[dim] // parts).reshape((-1,) + (1,) * (len(dims) - 1 - dim))
    return level


def centred(rng, dims, scale, bound, cuts=(), held_as=jnp.bfloat16):
    drawn = jax.random.normal(rng, dims, jnp.float32) * scale
    if len(cuts) > 0:
        drawn = block_scale(rng, dims, cuts, -0.22, 0.18) * drawn
    return jnp.clip(drawn, min=-bound, max=bound).astype(held_as)


def setup_inputs(seed: int = 0) -> dict:
    streams_of = jax.random.split(jax.random.key(seed), 11)
    right_side = centred(streams_of[0], (N, W), 1.0, 6.0, ((0, 128),), jnp.float32)
    leaf_inverse = centred(streams_of[1], (N, LEAF), LEAF ** -0.5, 0.1875, ((0, 128),))
    compress = centred(streams_of[2], (N, N_COL * S), LEAF ** -0.5, 0.1875, ((0, 128),))
    middle = centred(streams_of[3], (N_ROW * N_COL * N_COL * S, N_COL * S), (N_COL * S) ** -0.5, 0.125, ((0, 128),))
    expand = centred(streams_of[4], (N, N_COL * S), (N_COL * S) ** -0.5, 0.125, ((0, 128),))
    row_project = centred(streams_of[5], (LEVELS, N, RANK), LEAF ** -0.5, 0.1875, ((1, 128),))
    row_expand = centred(streams_of[6], (LEVELS, N, RANK), (2 * RANK) ** -0.5, 0.25, ((1, 128),))
    root_project = centred(streams_of[7], (N, RANK), (LEAF * DEVICES) ** -0.5, 0.015625, ((0, 128),))
    root_expand = centred(streams_of[8], (N, RANK), RANK ** -0.5, 0.375, ((0, 128),))
    owner_map = jax.random.permutation(streams_of[9], N_COL).astype(jnp.int32)
    return dict(right_side=right_side, leaf_inverse=leaf_inverse, compress=compress, middle=middle, expand=expand, row_project=row_project, row_expand=row_expand, root_project=root_project, root_expand=root_expand, owner_map=owner_map)


def reference(right_side, leaf_inverse, compress, middle, expand, row_project, row_expand, root_project, root_expand, owner_map):
    leaves = N_ROW * N_COL
    block_rows = N_COL * S
    lowered = right_side.astype(jnp.bfloat16).reshape(leaves, LEAF, W)
    inverse_blocks = leaf_inverse.reshape(leaves, LEAF, LEAF)
    compress_blocks = compress.reshape(leaves, LEAF, block_rows)
    middle_blocks = middle.reshape(leaves, block_rows, block_rows)
    expand_blocks = expand.reshape(leaves, LEAF, block_rows)
    project_blocks = jnp.transpose(row_project.reshape(LEVELS, leaves, LEAF, RANK), (1, 0, 2, 3))
    expand_levels = jnp.transpose(row_expand.reshape(LEVELS, leaves, LEAF, RANK), (1, 0, 2, 3))
    root_in = root_project.reshape(leaves, LEAF, RANK)
    root_out = root_expand.reshape(leaves, LEAF, RANK)

    def leaf_work(operands):
        block, inverse_block, compress_block, project_block, root_block = operands
        dense_part = jnp.dot(inverse_block, block, preferred_element_type=jnp.float32)
        coeffs = jnp.dot(compress_block.T, block, preferred_element_type=jnp.float32).astype(jnp.bfloat16)
        level_coeffs = jnp.einsum("blr,lw->brw", project_block.astype(jnp.float32), block.astype(jnp.float32))
        root_term = jnp.dot(root_block.T, block, preferred_element_type=jnp.float32)
        return dense_part, coeffs, level_coeffs, root_term

    dense_part, coeffs, level_coeffs, root_term = lax.map(leaf_work, (lowered, inverse_blocks, compress_blocks, project_blocks, root_in))

    inverse = jnp.argsort(owner_map)
    by_source = coeffs.reshape(N_ROW, N_COL, N_COL, S, W)
    arrived = jnp.transpose(jnp.take(by_source, inverse, axis=2), (0, 2, 1, 3, 4)).reshape(leaves, block_rows, W)

    def mix_work(operands):
        return jnp.dot(operands[0], operands[1], preferred_element_type=jnp.float32).astype(jnp.bfloat16)

    mixed = lax.map(mix_work, (middle_blocks, arrived))
    by_owner = mixed.reshape(N_ROW, N_COL, N_COL, S, W)
    returned = jnp.transpose(jnp.take(by_owner, owner_map, axis=1), (0, 2, 1, 3, 4)).reshape(leaves, block_rows, W)

    def expand_work(operands):
        return jnp.dot(operands[0], operands[1], preferred_element_type=jnp.float32)

    cluster_part = lax.map(expand_work, (expand_blocks, returned))

    grid = level_coeffs.reshape(N_ROW, N_COL, LEVELS, RANK, W)
    sibling_list = []
    for level_bit in range(LEVELS):
        span = 2 ** level_bit
        pairs = N_ROW // (2 * span)
        grouped = grid[:, :, level_bit].reshape(pairs, 2, span, N_COL, RANK, W).sum(axis=2)
        swapped = grouped[:, ::-1]
        spread = jnp.broadcast_to(swapped[:, :, None], (pairs, 2, span, N_COL, RANK, W)).reshape(N_ROW, N_COL, RANK, W)
        sibling_list.append(spread)
    sibling = jnp.stack(sibling_list, axis=2).reshape(leaves, LEVELS, RANK, W).astype(jnp.bfloat16)
    root_coeffs = jnp.sum(root_term, axis=0).astype(jnp.bfloat16)

    def finish_work(operands):
        expand_block, sibling_block, root_block = operands
        coupled = jnp.einsum("blr,brw->lw", expand_block.astype(jnp.float32), sibling_block.astype(jnp.float32))
        root_part = jnp.dot(root_block, root_coeffs, preferred_element_type=jnp.float32)
        return coupled, root_part

    coupled, root_part = lax.map(finish_work, (expand_levels, sibling, root_out))
    applied = dense_part + cluster_part + coupled + root_part
    return applied.reshape(leaves * LEAF, W)
```

```python
import jax
import jax.numpy as jnp
from jax import lax
from jax.sharding import PartitionSpec as P

contract_first = (((0,), (0,)), ((), ()))


def swapped(x, axis, bit):
    return lax.ppermute(x, axis, [(i, i ^ 1 << bit) for i in range(lax.axis_size(axis))])


def per_device(
    right_side,
    leaf_inverse,
    compress,
    middle,
    expand,
    row_project,
    row_expand,
    root_project,
    root_expand,
    owner_map,
):
    lowered = right_side.astype(jnp.bfloat16)
    columns = lowered.shape[1]
    dense_part = jnp.dot(leaf_inverse, lowered, preferred_element_type=jnp.float32)
    coeffs = lax.dot_general(
        compress, lowered, contract_first, preferred_element_type=jnp.float32
    ).astype(jnp.bfloat16)
    col_count = lax.axis_size("col")
    pieces = coeffs.reshape(col_count, -1, columns)
    inverse = jnp.argsort(owner_map)
    outgoing = jnp.take(pieces, inverse, axis=0)
    arrived = lax.all_to_all(outgoing, "col", split_axis=0, concat_axis=0, tiled=True)
    shape_now = arrived.shape
    mixed_rows = jnp.dot(
        middle, arrived.reshape(-1, shape_now[2]), preferred_element_type=jnp.float32
    )
    mixed_rows = mixed_rows.astype(jnp.bfloat16).reshape(shape_now)
    returned = lax.all_to_all(mixed_rows, "col", split_axis=0, concat_axis=0, tiled=True)
    ordered = jnp.take(returned, owner_map, axis=0).reshape(-1, columns)
    cluster_part = jnp.dot(expand, ordered, preferred_element_type=jnp.float32)
    level_coeffs = jnp.einsum(
        "blr,lw->brw", row_project, lowered, preferred_element_type=jnp.float32
    )
    root_term = lax.dot_general(
        root_project, lowered, contract_first, preferred_element_type=jnp.float32
    )
    levels = lax.axis_size("row").bit_length() - 1
    running = level_coeffs
    siblings = []
    for level_bit in range(levels):
        partner = swapped(running[level_bit:], "row", level_bit)
        siblings.append(partner[0])
        running = jnp.concatenate(
            [running[: level_bit + 1], running[level_bit + 1 :] + partner[1:]], axis=0
        )
    sibling_sum = jnp.stack(siblings, axis=0)
    root_sum = jnp.sum(lax.all_gather(lax.psum(root_term, "row"), "col", axis=0), axis=0)
    coupled = jnp.einsum(
        "blr,brw->lw",
        row_expand,
        sibling_sum.astype(jnp.bfloat16),
        preferred_element_type=jnp.float32,
    )
    root_part = jnp.dot(
        root_expand, root_sum.astype(jnp.bfloat16), preferred_element_type=jnp.float32
    )
    return dense_part + cluster_part + coupled + root_part


def solution(mesh):
    in_specs = (
        P(("row", "col"), None),
        P(("row", "col"), None),
        P(("row", "col"), None),
        P(("row", "col"), None),
        P(("row", "col"), None),
        P(None, ("row", "col"), None),
        P(None, ("row", "col"), None),
        P(("row", "col"), None),
        P(("row", "col"), None),
        P(),
    )
    out_specs = P(("row", "col"), None)
    return jax.shard_map(
        per_device, mesh=mesh, in_specs=in_specs, out_specs=out_specs, check_vma=False
    )
```

```python
import functools

import jax
import jax.numpy as jnp
from jax import lax
from jax.experimental import pallas as pl
from jax.experimental.pallas import tpu as pltpu
from jax.sharding import PartitionSpec as P

contract_first = (((0,), (0,)), ((), ()))
MESH_ID = pl.DeviceIdType.MESH


def swapped(x, axis, bit):
    return lax.ppermute(x, axis, [(i, i ^ 1 << bit) for i in range(lax.axis_size(axis))])


def exchange_kernel(n, x_ref, o_ref, send_sem, recv_sem, local_sem):
    me = lax.axis_index("col")
    row = lax.axis_index("row")
    barrier = pltpu.get_barrier_semaphore()
    for s in range(1, n):
        peer = lax.rem(me + s, n)
        pl.semaphore_signal(barrier, inc=1, device_id=(row, peer), device_id_type=MESH_ID)
    pl.semaphore_wait(barrier, n - 1)

    local = pltpu.make_async_copy(x_ref.at[me], o_ref.at[me], local_sem)
    local.start()
    copies = []
    for s in range(1, n):
        peer = lax.rem(me + s, n)
        copy = pltpu.make_async_remote_copy(
            src_ref=x_ref.at[peer],
            dst_ref=o_ref.at[me],
            send_sem=send_sem.at[s],
            recv_sem=recv_sem.at[s],
            device_id=(row, peer),
            device_id_type=MESH_ID,
        )
        copy.start()
        copies.append(copy)
    for s in range(1, n):
        source = lax.rem(me + n - s, n)
        arriving = pltpu.make_async_remote_copy(
            src_ref=x_ref.at[source],
            dst_ref=o_ref.at[source],
            send_sem=send_sem.at[s],
            recv_sem=recv_sem.at[s],
            device_id=(row, source),
            device_id_type=MESH_ID,
        )
        copies[s - 1].wait_send()
        arriving.wait_recv()
    local.wait()


def exchange(x, cid):
    n = x.shape[0]
    return pl.pallas_call(
        functools.partial(exchange_kernel, n),
        out_shape=jax.ShapeDtypeStruct(x.shape, x.dtype),
        in_specs=[pl.BlockSpec(memory_space=pl.ANY)],
        out_specs=pl.BlockSpec(memory_space=pl.ANY),
        scratch_shapes=[
            pltpu.SemaphoreType.DMA((n,)),
            pltpu.SemaphoreType.DMA((n,)),
            pltpu.SemaphoreType.DMA,
        ],
        compiler_params=pltpu.CompilerParams(collective_id=cid, has_side_effects=True),
    )(x)


def per_device(
    right_side,
    leaf_inverse,
    compress,
    middle,
    expand,
    row_project,
    row_expand,
    root_project,
    root_expand,
    owner_map,
):
    lowered = right_side.astype(jnp.bfloat16)
    columns = lowered.shape[1]
    root_term = lax.dot_general(
        root_project, lowered, contract_first, preferred_element_type=jnp.float32
    )
    level_coeffs = jnp.einsum(
        "blr,lw->brw", row_project, lowered, preferred_element_type=jnp.float32
    )
    dense_part = jnp.dot(leaf_inverse, lowered, preferred_element_type=jnp.float32)
    coeffs = lax.dot_general(
        compress, lowered, contract_first, preferred_element_type=jnp.float32
    ).astype(jnp.bfloat16)
    col_count = lax.axis_size("col")
    pieces = coeffs.reshape(col_count, -1, columns)
    inverse = jnp.argsort(owner_map)
    outgoing = jnp.take(pieces, inverse, axis=0)
    arrived = exchange(outgoing, 0)
    shape_now = arrived.shape
    mixed_rows = jnp.dot(
        middle, arrived.reshape(-1, shape_now[2]), preferred_element_type=jnp.float32
    )
    mixed_rows = mixed_rows.astype(jnp.bfloat16).reshape(shape_now)
    returned = exchange(mixed_rows, 1)
    ordered = jnp.take(returned, owner_map, axis=0).reshape(-1, columns)
    cluster_part = jnp.dot(expand, ordered, preferred_element_type=jnp.float32)

    levels = lax.axis_size("row").bit_length() - 1
    running = jnp.concatenate([level_coeffs, root_term[None]], axis=0)
    siblings = []
    for level_bit in range(levels):
        partner = swapped(running[level_bit:], "row", level_bit)
        siblings.append(partner[0])
        running = jnp.concatenate(
            [running[: level_bit + 1], running[level_bit + 1 :] + partner[1:]], axis=0
        )
    sibling_sum = jnp.stack(siblings, axis=0)
    root_sum = running[levels]
    for bit in range(lax.axis_size("col").bit_length() - 1):
        root_sum = root_sum + swapped(root_sum, "col", bit)
    coupled = jnp.einsum(
        "blr,brw->lw",
        row_expand,
        sibling_sum.astype(jnp.bfloat16),
        preferred_element_type=jnp.float32,
    )
    root_part = jnp.dot(
        root_expand, root_sum.astype(jnp.bfloat16), preferred_element_type=jnp.float32
    )
    return dense_part + cluster_part + coupled + root_part


def solution(mesh):
    in_specs = (
        P(("row", "col"), None),
        P(("row", "col"), None),
        P(("row", "col"), None),
        P(("row", "col"), None),
        P(("row", "col"), None),
        P(None, ("row", "col"), None),
        P(None, ("row", "col"), None),
        P(("row", "col"), None),
        P(("row", "col"), None),
        P(),
    )
    out_specs = P(("row", "col"), None)
    return jax.shard_map(
        per_device, mesh=mesh, in_specs=in_specs, out_specs=out_specs, check_vma=False
    )
```

```python
import functools

import jax
import jax.numpy as jnp
from jax import lax
from jax.experimental import pallas as pl
from jax.experimental.pallas import tpu as pltpu
from jax.sharding import PartitionSpec as P

contract_first = (((0,), (0,)), ((), ()))
MESH_ID = pl.DeviceIdType.MESH


def swapped(x, axis, bit):
    return lax.ppermute(x, axis, [(i, i ^ 1 << bit) for i in range(lax.axis_size(axis))])


def col_peers(n):
    me = lax.axis_index("col")
    return [(s, lax.rem(me + s, n), lax.rem(me + n - s, n)) for s in range(1, n)]


def scatter_kernel(n, x_ref, r_ref, o_ref, share_ref, got, sems, local_sems):
    me = lax.axis_index("col")
    row = lax.axis_index("row")
    barrier = pltpu.get_barrier_semaphore()
    for s, peer, _ in col_peers(n):
        pl.semaphore_signal(barrier, inc=1, device_id=(row, peer), device_id_type=MESH_ID)
    pl.semaphore_wait(barrier, n - 1)

    local = pltpu.make_async_copy(x_ref.at[me], o_ref.at[me], local_sems.at[0])
    local.start()
    own = pltpu.make_async_copy(r_ref.at[me], got.at[me], local_sems.at[1])
    own.start()

    def piece(s, peer, slot):
        return pltpu.make_async_remote_copy(
            src_ref=x_ref.at[peer], dst_ref=o_ref.at[slot],
            send_sem=sems.at[0, s], recv_sem=sems.at[1, s],
            device_id=(row, peer), device_id_type=MESH_ID,
        )

    def share(s, peer, slot):
        return pltpu.make_async_remote_copy(
            src_ref=r_ref.at[peer], dst_ref=got.at[slot],
            send_sem=sems.at[2, s], recv_sem=sems.at[3, s],
            device_id=(row, peer), device_id_type=MESH_ID,
        )

    for s, peer, _ in col_peers(n):
        share(s, peer, me).start()
        piece(s, peer, me).start()
    for s, peer, source in col_peers(n):
        share(s, peer, me).wait_send()
        share(s, source, source).wait_recv()
    own.wait()
    share_ref[...] = jnp.sum(got[...], axis=0)
    for s, peer, source in col_peers(n):
        piece(s, peer, me).wait_send()
        piece(s, source, source).wait_recv()
    local.wait()


def scatter(x, r):
    n = x.shape[0]
    return pl.pallas_call(
        functools.partial(scatter_kernel, n),
        out_shape=(
            jax.ShapeDtypeStruct(x.shape, x.dtype),
            jax.ShapeDtypeStruct(r.shape[1:], r.dtype),
        ),
        in_specs=[pl.BlockSpec(memory_space=pl.ANY), pl.BlockSpec(memory_space=pltpu.VMEM)],
        out_specs=(pl.BlockSpec(memory_space=pl.ANY), pl.BlockSpec(memory_space=pltpu.VMEM)),
        scratch_shapes=[
            pltpu.VMEM(r.shape, r.dtype),
            pltpu.SemaphoreType.DMA((4, n)),
            pltpu.SemaphoreType.DMA((2,)),
        ],
        compiler_params=pltpu.CompilerParams(collective_id=0, has_side_effects=True),
    )(x, r)


def gather_kernel(n, m, x_ref, share_ref, o_ref, full_ref, rows_got, total, sems, row_sems, local_sems):
    me = lax.axis_index("col")
    row = lax.axis_index("row")
    row_peers = [(s, lax.rem(row + s, m), lax.rem(row + m - s, m)) for s in range(1, m)]
    barrier = pltpu.get_barrier_semaphore()
    for s, peer, _ in col_peers(n):
        pl.semaphore_signal(barrier, inc=1, device_id=(row, peer), device_id_type=MESH_ID)
    for s, peer, _ in row_peers:
        pl.semaphore_signal(barrier, inc=1, device_id=(peer, me), device_id_type=MESH_ID)
    pl.semaphore_wait(barrier, n - 1 + m - 1)

    local = pltpu.make_async_copy(x_ref.at[me], o_ref.at[me], local_sems.at[0])
    local.start()
    own = pltpu.make_async_copy(share_ref, rows_got.at[row], local_sems.at[1])
    own.start()

    def piece(s, peer, slot):
        return pltpu.make_async_remote_copy(
            src_ref=x_ref.at[peer], dst_ref=o_ref.at[slot],
            send_sem=sems.at[0, s], recv_sem=sems.at[1, s],
            device_id=(row, peer), device_id_type=MESH_ID,
        )

    def part(s, peer, slot):
        return pltpu.make_async_remote_copy(
            src_ref=share_ref, dst_ref=rows_got.at[slot],
            send_sem=row_sems.at[0, s], recv_sem=row_sems.at[1, s],
            device_id=(peer, me), device_id_type=MESH_ID,
        )

    def spread(s, peer, slot):
        return pltpu.make_async_remote_copy(
            src_ref=total, dst_ref=full_ref.at[slot],
            send_sem=sems.at[2, s], recv_sem=sems.at[3, s],
            device_id=(row, peer), device_id_type=MESH_ID,
        )

    for s, peer, _ in row_peers:
        part(s, peer, row).start()
    for s, peer, _ in col_peers(n):
        piece(s, peer, me).start()
    for s, peer, source in row_peers:
        part(s, peer, row).wait_send()
        part(s, source, source).wait_recv()
    own.wait()
    total[...] = jnp.sum(rows_got[...], axis=0)
    mine = pltpu.make_async_copy(total, full_ref.at[me], local_sems.at[2])
    mine.start()
    for s, peer, _ in col_peers(n):
        spread(s, peer, me).start()
    for s, peer, source in col_peers(n):
        spread(s, peer, me).wait_send()
        spread(s, source, source).wait_recv()
        piece(s, peer, me).wait_send()
        piece(s, source, source).wait_recv()
    mine.wait()
    local.wait()


def gather(x, share, m):
    n = x.shape[0]
    return pl.pallas_call(
        functools.partial(gather_kernel, n, m),
        out_shape=(
            jax.ShapeDtypeStruct(x.shape, x.dtype),
            jax.ShapeDtypeStruct((n,) + share.shape, share.dtype),
        ),
        in_specs=[pl.BlockSpec(memory_space=pl.ANY), pl.BlockSpec(memory_space=pltpu.VMEM)],
        out_specs=(pl.BlockSpec(memory_space=pl.ANY), pl.BlockSpec(memory_space=pltpu.VMEM)),
        scratch_shapes=[
            pltpu.VMEM((m,) + share.shape, share.dtype),
            pltpu.VMEM(share.shape, share.dtype),
            pltpu.SemaphoreType.DMA((4, n)),
            pltpu.SemaphoreType.DMA((2, m)),
            pltpu.SemaphoreType.DMA((3,)),
        ],
        compiler_params=pltpu.CompilerParams(collective_id=1, has_side_effects=True),
    )(x, share)


def per_device(
    right_side,
    leaf_inverse,
    compress,
    middle,
    expand,
    row_project,
    row_expand,
    root_project,
    root_expand,
    owner_map,
):
    lowered = right_side.astype(jnp.bfloat16)
    columns = lowered.shape[1]
    root_term = lax.dot_general(
        root_project, lowered, contract_first, preferred_element_type=jnp.float32
    )
    level_coeffs = jnp.einsum(
        "blr,lw->brw", row_project, lowered, preferred_element_type=jnp.float32
    )
    dense_part = jnp.dot(leaf_inverse, lowered, preferred_element_type=jnp.float32)
    coeffs = lax.dot_general(
        compress, lowered, contract_first, preferred_element_type=jnp.float32
    ).astype(jnp.bfloat16)
    col_count = lax.axis_size("col")
    pieces = coeffs.reshape(col_count, -1, columns)
    inverse = jnp.argsort(owner_map)
    outgoing = jnp.take(pieces, inverse, axis=0)
    root_shares = root_term.reshape(col_count, -1, columns)
    arrived, root_share = scatter(outgoing, root_shares)
    shape_now = arrived.shape
    mixed_rows = jnp.dot(
        middle, arrived.reshape(-1, shape_now[2]), preferred_element_type=jnp.float32
    )
    mixed_rows = mixed_rows.astype(jnp.bfloat16).reshape(shape_now)
    returned, root_full = gather(mixed_rows, root_share, lax.axis_size("row"))
    ordered = jnp.take(returned, owner_map, axis=0).reshape(-1, columns)
    cluster_part = jnp.dot(expand, ordered, preferred_element_type=jnp.float32)

    levels = lax.axis_size("row").bit_length() - 1
    running = level_coeffs
    siblings = []
    for level_bit in range(levels):
        partner = swapped(running[level_bit:], "row", level_bit)
        siblings.append(partner[0])
        running = jnp.concatenate(
            [running[: level_bit + 1], running[level_bit + 1 :] + partner[1:]], axis=0
        )
    sibling_sum = jnp.stack(siblings, axis=0)
    root_sum = root_full.reshape(-1, columns)
    coupled = jnp.einsum(
        "blr,brw->lw",
        row_expand,
        sibling_sum.astype(jnp.bfloat16),
        preferred_element_type=jnp.float32,
    )
    root_part = jnp.dot(
        root_expand, root_sum.astype(jnp.bfloat16), preferred_element_type=jnp.float32
    )
    return dense_part + cluster_part + coupled + root_part


def solution(mesh):
    in_specs = (
        P(("row", "col"), None),
        P(("row", "col"), None),
        P(("row", "col"), None),
        P(("row", "col"), None),
        P(("row", "col"), None),
        P(None, ("row", "col"), None),
        P(None, ("row", "col"), None),
        P(("row", "col"), None),
        P(("row", "col"), None),
        P(),
    )
    out_specs = P(("row", "col"), None)
    return jax.shard_map(
        per_device, mesh=mesh, in_specs=in_specs, out_specs=out_specs, check_vma=False
    )
```

```python
import functools

import jax
import jax.numpy as jnp
from jax import lax
from jax.experimental import pallas as pl
from jax.experimental.pallas import tpu as pltpu
from jax.sharding import PartitionSpec as P

contract_first = (((0,), (0,)), ((), ()))
MESH_ID = pl.DeviceIdType.MESH


def swapped(x, axis, bit):
    return lax.ppermute(x, axis, [(i, i ^ 1 << bit) for i in range(lax.axis_size(axis))])


def col_peers(n):
    me = lax.axis_index("col")
    return [(s, lax.rem(me + s, n), lax.rem(me + n - s, n)) for s in range(1, n)]


def scatter_kernel(n, x_ref, r_ref, o_ref, share_ref, got, sems, local_sems):
    me = lax.axis_index("col")
    row = lax.axis_index("row")
    barrier = pltpu.get_barrier_semaphore()
    for s, peer, _ in col_peers(n):
        pl.semaphore_signal(barrier, inc=1, device_id=(row, peer), device_id_type=MESH_ID)
    pl.semaphore_wait(barrier, n - 1)

    local = pltpu.make_async_copy(x_ref.at[me], o_ref.at[me], local_sems.at[0])
    local.start()
    own = pltpu.make_async_copy(r_ref.at[me], got.at[me], local_sems.at[1])
    own.start()

    def piece(s, peer, slot):
        return pltpu.make_async_remote_copy(
            src_ref=x_ref.at[peer], dst_ref=o_ref.at[slot],
            send_sem=sems.at[0, s], recv_sem=sems.at[1, s],
            device_id=(row, peer), device_id_type=MESH_ID,
        )

    def share(s, peer, slot):
        return pltpu.make_async_remote_copy(
            src_ref=r_ref.at[peer], dst_ref=got.at[slot],
            send_sem=sems.at[2, s], recv_sem=sems.at[3, s],
            device_id=(row, peer), device_id_type=MESH_ID,
        )

    for s, peer, _ in col_peers(n):
        share(s, peer, me).start()
        piece(s, peer, me).start()
    for s, peer, source in col_peers(n):
        share(s, peer, me).wait_send()
        share(s, source, source).wait_recv()
    own.wait()
    share_ref[...] = jnp.sum(got[...], axis=0)
    for s, peer, source in col_peers(n):
        piece(s, peer, me).wait_send()
        piece(s, source, source).wait_recv()
    local.wait()


def scatter(x, r):
    n = x.shape[0]
    return pl.pallas_call(
        functools.partial(scatter_kernel, n),
        out_shape=(
            jax.ShapeDtypeStruct(x.shape, x.dtype),
            jax.ShapeDtypeStruct(r.shape[1:], r.dtype),
        ),
        in_specs=[pl.BlockSpec(memory_space=pl.ANY), pl.BlockSpec(memory_space=pltpu.VMEM)],
        out_specs=(pl.BlockSpec(memory_space=pl.ANY), pl.BlockSpec(memory_space=pltpu.VMEM)),
        scratch_shapes=[
            pltpu.VMEM(r.shape, r.dtype),
            pltpu.SemaphoreType.DMA((4, n)),
            pltpu.SemaphoreType.DMA((2,)),
        ],
        compiler_params=pltpu.CompilerParams(collective_id=0, has_side_effects=True),
    )(x, r)


def gather_kernel(n, m, x_ref, share_ref, o_ref, full_ref, rows_got, total, sems, row_sems, local_sems):
    me = lax.axis_index("col")
    row = lax.axis_index("row")
    row_peers = [(s, lax.rem(row + s, m), lax.rem(row + m - s, m)) for s in range(1, m)]
    barrier = pltpu.get_barrier_semaphore()
    for s, peer, _ in col_peers(n):
        pl.semaphore_signal(barrier, inc=1, device_id=(row, peer), device_id_type=MESH_ID)
    for s, peer, _ in row_peers:
        pl.semaphore_signal(barrier, inc=1, device_id=(peer, me), device_id_type=MESH_ID)
    pl.semaphore_wait(barrier, n - 1 + m - 1)

    local = pltpu.make_async_copy(x_ref.at[me], o_ref.at[me], local_sems.at[0])
    local.start()
    own = pltpu.make_async_copy(share_ref, rows_got.at[row], local_sems.at[1])
    own.start()

    def piece(s, peer, slot):
        return pltpu.make_async_remote_copy(
            src_ref=x_ref.at[peer], dst_ref=o_ref.at[slot],
            send_sem=sems.at[0, s], recv_sem=sems.at[1, s],
            device_id=(row, peer), device_id_type=MESH_ID,
        )

    def part(s, peer, slot):
        return pltpu.make_async_remote_copy(
            src_ref=share_ref, dst_ref=rows_got.at[slot],
            send_sem=row_sems.at[0, s], recv_sem=row_sems.at[1, s],
            device_id=(peer, me), device_id_type=MESH_ID,
        )

    def spread(s, peer, slot):
        return pltpu.make_async_remote_copy(
            src_ref=total, dst_ref=full_ref.at[slot],
            send_sem=sems.at[2, s], recv_sem=sems.at[3, s],
            device_id=(row, peer), device_id_type=MESH_ID,
        )

    for s, peer, _ in row_peers:
        part(s, peer, row).start()
    for s, peer, _ in col_peers(n):
        piece(s, peer, me).start()
    for s, peer, source in row_peers:
        part(s, peer, row).wait_send()
        part(s, source, source).wait_recv()
    own.wait()
    total[...] = jnp.sum(rows_got[...], axis=0)
    mine = pltpu.make_async_copy(total, full_ref.at[me], local_sems.at[2])
    mine.start()
    for s, peer, _ in col_peers(n):
        spread(s, peer, me).start()
    for s, peer, source in col_peers(n):
        spread(s, peer, me).wait_send()
        spread(s, source, source).wait_recv()
        piece(s, peer, me).wait_send()
        piece(s, source, source).wait_recv()
    mine.wait()
    local.wait()


def gather(x, share, m):
    n = x.shape[0]
    return pl.pallas_call(
        functools.partial(gather_kernel, n, m),
        out_shape=(
            jax.ShapeDtypeStruct(x.shape, x.dtype),
            jax.ShapeDtypeStruct((n,) + share.shape, share.dtype),
        ),
        in_specs=[pl.BlockSpec(memory_space=pl.ANY), pl.BlockSpec(memory_space=pltpu.VMEM)],
        out_specs=(pl.BlockSpec(memory_space=pl.ANY), pl.BlockSpec(memory_space=pltpu.VMEM)),
        scratch_shapes=[
            pltpu.VMEM((m,) + share.shape, share.dtype),
            pltpu.VMEM(share.shape, share.dtype),
            pltpu.SemaphoreType.DMA((4, n)),
            pltpu.SemaphoreType.DMA((2, m)),
            pltpu.SemaphoreType.DMA((3,)),
        ],
        compiler_params=pltpu.CompilerParams(collective_id=1, has_side_effects=True),
    )(x, share)


def per_device(
    right_side,
    leaf_inverse,
    compress,
    middle,
    expand,
    row_project,
    row_expand,
    root_project,
    root_expand,
    owner_map,
):
    lowered = right_side.astype(jnp.bfloat16)
    columns = lowered.shape[1]
    root_term = lax.dot_general(
        root_project, lowered, contract_first, preferred_element_type=jnp.float32
    )
    level_coeffs = jnp.einsum(
        "blr,lw->brw", row_project, lowered, preferred_element_type=jnp.float32
    )
    dense_part = jnp.dot(leaf_inverse, lowered, preferred_element_type=jnp.float32)
    coeffs = lax.dot_general(
        compress, lowered, contract_first, preferred_element_type=jnp.float32
    ).astype(jnp.bfloat16)
    col_count = lax.axis_size("col")
    pieces = coeffs.reshape(col_count, -1, columns)
    chosen = (owner_map[:, None] == jnp.arange(col_count, dtype=owner_map.dtype)[None, :]).astype(
        jnp.bfloat16
    )
    outgoing = jnp.einsum(
        "kd,kxw->dxw", chosen, pieces, preferred_element_type=jnp.float32
    ).astype(jnp.bfloat16)
    root_shares = root_term.reshape(col_count, -1, columns)
    arrived, root_share = scatter(outgoing, root_shares)
    shape_now = arrived.shape
    mixed_rows = jnp.dot(
        middle, arrived.reshape(-1, shape_now[2]), preferred_element_type=jnp.float32
    )
    mixed_rows = mixed_rows.astype(jnp.bfloat16).reshape(shape_now)
    returned, root_full = gather(mixed_rows, root_share, lax.axis_size("row"))
    ordered = jnp.einsum(
        "jd,dxw->jxw", chosen, returned, preferred_element_type=jnp.float32
    ).astype(jnp.bfloat16).reshape(-1, columns)
    cluster_part = jnp.dot(expand, ordered, preferred_element_type=jnp.float32)

    levels = lax.axis_size("row").bit_length() - 1
    running = level_coeffs
    siblings = []
    for level_bit in range(levels):
        partner = swapped(running[level_bit:], "row", level_bit)
        siblings.append(partner[0])
        running = jnp.concatenate(
            [running[: level_bit + 1], running[level_bit + 1 :] + partner[1:]], axis=0
        )
    sibling_sum = jnp.stack(siblings, axis=0)
    root_sum = root_full.reshape(-1, columns)
    coupled = jnp.einsum(
        "blr,brw->lw",
        row_expand,
        sibling_sum.astype(jnp.bfloat16),
        preferred_element_type=jnp.float32,
    )
    root_part = jnp.dot(
        root_expand, root_sum.astype(jnp.bfloat16), preferred_element_type=jnp.float32
    )
    return dense_part + cluster_part + coupled + root_part


def solution(mesh):
    in_specs = (
        P(("row", "col"), None),
        P(("row", "col"), None),
        P(("row", "col"), None),
        P(("row", "col"), None),
        P(("row", "col"), None),
        P(None, ("row", "col"), None),
        P(None, ("row", "col"), None),
        P(("row", "col"), None),
        P(("row", "col"), None),
        P(),
    )
    out_specs = P(("row", "col"), None)
    return jax.shard_map(
        per_device, mesh=mesh, in_specs=in_specs, out_specs=out_specs, check_vma=False
    )
```

```python
import functools

import jax
import jax.numpy as jnp
from jax import lax
from jax.experimental import pallas as pl
from jax.experimental.pallas import tpu as pltpu
from jax.sharding import PartitionSpec as P

contract_first = (((0,), (0,)), ((), ()))
MESH_ID = pl.DeviceIdType.MESH


def swapped(x, axis, bit):
    return lax.ppermute(x, axis, [(i, i ^ 1 << bit) for i in range(lax.axis_size(axis))])


def flipped(index, bit):
    return index + bit - 2 * bit * lax.rem(index // bit, 2)


def col_peers(n):
    me = lax.axis_index("col")
    return [(s, lax.rem(me + s, n), lax.rem(me + n - s, n)) for s in range(1, n)]


def scatter_kernel(n, x_ref, r_ref, lv_ref, o_ref, share_ref, pair_ref, got, sems, local_sems, pair_sems):
    me = lax.axis_index("col")
    row = lax.axis_index("row")
    barrier = pltpu.get_barrier_semaphore()
    for s, peer, _ in col_peers(n):
        pl.semaphore_signal(barrier, inc=1, device_id=(row, peer), device_id_type=MESH_ID)
    partner = flipped(row, 1)
    pl.semaphore_signal(barrier, inc=1, device_id=(partner, me), device_id_type=MESH_ID)
    pl.semaphore_wait(barrier, n)

    levels = pltpu.make_async_remote_copy(
        src_ref=lv_ref, dst_ref=pair_ref,
        send_sem=pair_sems.at[0], recv_sem=pair_sems.at[1],
        device_id=(partner, me), device_id_type=MESH_ID,
    )
    levels.start()
    local = pltpu.make_async_copy(x_ref.at[me], o_ref.at[me], local_sems.at[0])
    local.start()
    own = pltpu.make_async_copy(r_ref.at[me], got.at[me], local_sems.at[1])
    own.start()

    def piece(s, peer, slot):
        return pltpu.make_async_remote_copy(
            src_ref=x_ref.at[peer], dst_ref=o_ref.at[slot],
            send_sem=sems.at[0, s], recv_sem=sems.at[1, s],
            device_id=(row, peer), device_id_type=MESH_ID,
        )

    def share(s, peer, slot):
        return pltpu.make_async_remote_copy(
            src_ref=r_ref.at[peer], dst_ref=got.at[slot],
            send_sem=sems.at[2, s], recv_sem=sems.at[3, s],
            device_id=(row, peer), device_id_type=MESH_ID,
        )

    for s, peer, _ in col_peers(n):
        share(s, peer, me).start()
        piece(s, peer, me).start()
    for s, peer, source in col_peers(n):
        share(s, peer, me).wait_send()
        share(s, source, source).wait_recv()
    own.wait()
    share_ref[...] = jnp.sum(got[...], axis=0)
    for s, peer, source in col_peers(n):
        piece(s, peer, me).wait_send()
        piece(s, source, source).wait_recv()
    local.wait()
    levels.wait()


def scatter(x, r, lv):
    n = x.shape[0]
    return pl.pallas_call(
        functools.partial(scatter_kernel, n),
        out_shape=(
            jax.ShapeDtypeStruct(x.shape, x.dtype),
            jax.ShapeDtypeStruct(r.shape[1:], r.dtype),
            jax.ShapeDtypeStruct(lv.shape, lv.dtype),
        ),
        in_specs=[
            pl.BlockSpec(memory_space=pl.ANY),
            pl.BlockSpec(memory_space=pltpu.VMEM),
            pl.BlockSpec(memory_space=pl.ANY),
        ],
        out_specs=(
            pl.BlockSpec(memory_space=pl.ANY),
            pl.BlockSpec(memory_space=pltpu.VMEM),
            pl.BlockSpec(memory_space=pl.ANY),
        ),
        scratch_shapes=[
            pltpu.VMEM(r.shape, r.dtype),
            pltpu.SemaphoreType.DMA((4, n)),
            pltpu.SemaphoreType.DMA((2,)),
            pltpu.SemaphoreType.DMA((2,)),
        ],
        compiler_params=pltpu.CompilerParams(collective_id=0, has_side_effects=True),
    )(x, r, lv)


def gather_kernel(
    n, m, x_ref, share_ref, c1_ref, c2_ref, o_ref, full_ref, got1, got2,
    rows_got, total, sems, row_sems, local_sems, sib_sems,
):
    me = lax.axis_index("col")
    row = lax.axis_index("row")
    row_peers = [(s, lax.rem(row + s, m), lax.rem(row + m - s, m)) for s in range(1, m)]
    barrier = pltpu.get_barrier_semaphore()
    for s, peer, _ in col_peers(n):
        pl.semaphore_signal(barrier, inc=1, device_id=(row, peer), device_id_type=MESH_ID)
    for s, peer, _ in row_peers:
        pl.semaphore_signal(barrier, inc=1, device_id=(peer, me), device_id_type=MESH_ID)
    pl.semaphore_wait(barrier, n - 1 + m - 1)

    local = pltpu.make_async_copy(x_ref.at[me], o_ref.at[me], local_sems.at[0])
    local.start()
    own = pltpu.make_async_copy(share_ref, rows_got.at[row], local_sems.at[1])
    own.start()

    def piece(s, peer, slot):
        return pltpu.make_async_remote_copy(
            src_ref=x_ref.at[peer], dst_ref=o_ref.at[slot],
            send_sem=sems.at[0, s], recv_sem=sems.at[1, s],
            device_id=(row, peer), device_id_type=MESH_ID,
        )

    def part(s, peer, slot):
        return pltpu.make_async_remote_copy(
            src_ref=share_ref, dst_ref=rows_got.at[slot],
            send_sem=row_sems.at[0, s], recv_sem=row_sems.at[1, s],
            device_id=(peer, me), device_id_type=MESH_ID,
        )

    def spread(s, peer, slot):
        return pltpu.make_async_remote_copy(
            src_ref=total, dst_ref=full_ref.at[slot],
            send_sem=sems.at[2, s], recv_sem=sems.at[3, s],
            device_id=(row, peer), device_id_type=MESH_ID,
        )

    sends = [
        (c1_ref, got1, flipped(row, 1 * 2)),
        (c2_ref, got2.at[0], flipped(row, 4)),
        (c2_ref, got2.at[1], flipped(flipped(row, 4), 2)),
    ]
    sibs = []
    for i, (src_ref, dst_ref, peer) in enumerate(sends):
        sib = pltpu.make_async_remote_copy(
            src_ref=src_ref, dst_ref=dst_ref,
            send_sem=sib_sems.at[0, i], recv_sem=sib_sems.at[1, i],
            device_id=(peer, me), device_id_type=MESH_ID,
        )
        sib.start()
        sibs.append(sib)
    for s, peer, _ in row_peers:
        part(s, peer, row).start()
    for s, peer, _ in col_peers(n):
        piece(s, peer, me).start()
    for s, peer, source in row_peers:
        part(s, peer, row).wait_send()
        part(s, source, source).wait_recv()
    own.wait()
    total[...] = jnp.sum(rows_got[...], axis=0)
    mine = pltpu.make_async_copy(total, full_ref.at[me], local_sems.at[2])
    mine.start()
    for s, peer, _ in col_peers(n):
        spread(s, peer, me).start()
    for s, peer, source in col_peers(n):
        spread(s, peer, me).wait_send()
        spread(s, source, source).wait_recv()
        piece(s, peer, me).wait_send()
        piece(s, source, source).wait_recv()
    mine.wait()
    local.wait()
    for sib in sibs:
        sib.wait()


def gather(x, share, c1, c2, m):
    n = x.shape[0]
    return pl.pallas_call(
        functools.partial(gather_kernel, n, m),
        out_shape=(
            jax.ShapeDtypeStruct(x.shape, x.dtype),
            jax.ShapeDtypeStruct((n,) + share.shape, share.dtype),
            jax.ShapeDtypeStruct(c1.shape, c1.dtype),
            jax.ShapeDtypeStruct((2,) + c2.shape, c2.dtype),
        ),
        in_specs=[
            pl.BlockSpec(memory_space=pl.ANY),
            pl.BlockSpec(memory_space=pltpu.VMEM),
            pl.BlockSpec(memory_space=pl.ANY),
            pl.BlockSpec(memory_space=pl.ANY),
        ],
        out_specs=(
            pl.BlockSpec(memory_space=pl.ANY),
            pl.BlockSpec(memory_space=pltpu.VMEM),
            pl.BlockSpec(memory_space=pl.ANY),
            pl.BlockSpec(memory_space=pl.ANY),
        ),
        scratch_shapes=[
            pltpu.VMEM((m,) + share.shape, share.dtype),
            pltpu.VMEM(share.shape, share.dtype),
            pltpu.SemaphoreType.DMA((4, n)),
            pltpu.SemaphoreType.DMA((2, m)),
            pltpu.SemaphoreType.DMA((3,)),
            pltpu.SemaphoreType.DMA((2, 3)),
        ],
        compiler_params=pltpu.CompilerParams(collective_id=1, has_side_effects=True),
    )(x, share, c1, c2)


def per_device(
    right_side,
    leaf_inverse,
    compress,
    middle,
    expand,
    row_project,
    row_expand,
    root_project,
    root_expand,
    owner_map,
):
    lowered = right_side.astype(jnp.bfloat16)
    columns = lowered.shape[1]
    root_term = lax.dot_general(
        root_project, lowered, contract_first, preferred_element_type=jnp.float32
    )
    level_coeffs = jnp.einsum(
        "blr,lw->brw", row_project, lowered, preferred_element_type=jnp.float32
    )
    dense_part = jnp.dot(leaf_inverse, lowered, preferred_element_type=jnp.float32)
    coeffs = lax.dot_general(
        compress, lowered, contract_first, preferred_element_type=jnp.float32
    ).astype(jnp.bfloat16)
    col_count = lax.axis_size("col")
    pieces = coeffs.reshape(col_count, -1, columns)
    chosen = (owner_map[:, None] == jnp.arange(col_count, dtype=owner_map.dtype)[None, :]).astype(
        jnp.bfloat16
    )
    outgoing = jnp.einsum(
        "kd,kxw->dxw", chosen, pieces, preferred_element_type=jnp.float32
    ).astype(jnp.bfloat16)
    root_shares = root_term.reshape(col_count, -1, columns)
    arrived, root_share, pair = scatter(outgoing, root_shares, level_coeffs)
    shape_now = arrived.shape
    mixed_rows = jnp.dot(
        middle, arrived.reshape(-1, shape_now[2]), preferred_element_type=jnp.float32
    )
    mixed_rows = mixed_rows.astype(jnp.bfloat16).reshape(shape_now)
    chip_sums = level_coeffs[1:] + pair[1:]
    returned, root_full, quad_one, quad_two = gather(
        mixed_rows, root_share, chip_sums[0], chip_sums[1], lax.axis_size("row")
    )
    ordered = jnp.einsum(
        "jd,dxw->jxw", chosen, returned, preferred_element_type=jnp.float32
    ).astype(jnp.bfloat16).reshape(-1, columns)
    cluster_part = jnp.dot(expand, ordered, preferred_element_type=jnp.float32)

    sibling_sum = jnp.stack([pair[0], quad_one, quad_two[0] + quad_two[1]], axis=0)
    root_sum = root_full.reshape(-1, columns)
    coupled = jnp.einsum(
        "blr,brw->lw",
        row_expand,
        sibling_sum.astype(jnp.bfloat16),
        preferred_element_type=jnp.float32,
    )
    root_part = jnp.dot(
        root_expand, root_sum.astype(jnp.bfloat16), preferred_element_type=jnp.float32
    )
    return dense_part + cluster_part + coupled + root_part


def solution(mesh):
    in_specs = (
        P(("row", "col"), None),
        P(("row", "col"), None),
        P(("row", "col"), None),
        P(("row", "col"), None),
        P(("row", "col"), None),
        P(None, ("row", "col"), None),
        P(None, ("row", "col"), None),
        P(("row", "col"), None),
        P(("row", "col"), None),
        P(),
    )
    out_specs = P(("row", "col"), None)
    return jax.shard_map(
        per_device, mesh=mesh, in_specs=in_specs, out_specs=out_specs, check_vma=False
    )
```

```python
import functools

import jax
import jax.numpy as jnp
from jax import lax
from jax.experimental import pallas as pl
from jax.experimental.pallas import tpu as pltpu
from jax.sharding import PartitionSpec as P

contract_first = (((0,), (0,)), ((), ()))
MESH_ID = pl.DeviceIdType.MESH


def swapped(x, axis, bit):
    return lax.ppermute(x, axis, [(i, i ^ 1 << bit) for i in range(lax.axis_size(axis))])


def flipped(index, bit):
    return index + bit - 2 * bit * lax.rem(index // bit, 2)


def col_peers(n):
    me = lax.axis_index("col")
    return [(s, lax.rem(me + s, n), lax.rem(me + n - s, n)) for s in range(1, n)]


def scatter_kernel(n, x_ref, r_ref, lv_ref, o_ref, share_ref, pair_ref, got, sems, local_sems, pair_sems):
    me = lax.axis_index("col")
    row = lax.axis_index("row")
    barrier = pltpu.get_barrier_semaphore()
    for s, peer, _ in col_peers(n):
        pl.semaphore_signal(barrier, inc=1, device_id=(row, peer), device_id_type=MESH_ID)
    partner = flipped(row, 1)
    pl.semaphore_signal(barrier, inc=1, device_id=(partner, me), device_id_type=MESH_ID)
    pl.semaphore_wait(barrier, n)

    levels = pltpu.make_async_remote_copy(
        src_ref=lv_ref, dst_ref=pair_ref,
        send_sem=pair_sems.at[0], recv_sem=pair_sems.at[1],
        device_id=(partner, me), device_id_type=MESH_ID,
    )
    levels.start()
    local = pltpu.make_async_copy(x_ref.at[me], o_ref.at[me], local_sems.at[0])
    local.start()
    own = pltpu.make_async_copy(r_ref.at[me], got.at[me], local_sems.at[1])
    own.start()

    def piece(s, peer, slot):
        return pltpu.make_async_remote_copy(
            src_ref=x_ref.at[peer], dst_ref=o_ref.at[slot],
            send_sem=sems.at[0, s], recv_sem=sems.at[1, s],
            device_id=(row, peer), device_id_type=MESH_ID,
        )

    def share(s, peer, slot):
        return pltpu.make_async_remote_copy(
            src_ref=r_ref.at[peer], dst_ref=got.at[slot],
            send_sem=sems.at[2, s], recv_sem=sems.at[3, s],
            device_id=(row, peer), device_id_type=MESH_ID,
        )

    for s, peer, _ in col_peers(n):
        share(s, peer, me).start()
        piece(s, peer, me).start()
    for s, peer, source in col_peers(n):
        share(s, peer, me).wait_send()
        share(s, source, source).wait_recv()
    own.wait()
    share_ref[...] = jnp.sum(got[...], axis=0)
    for s, peer, source in col_peers(n):
        piece(s, peer, me).wait_send()
        piece(s, source, source).wait_recv()
    local.wait()
    levels.wait()


def scatter(x, r, lv):
    n = x.shape[0]
    return pl.pallas_call(
        functools.partial(scatter_kernel, n),
        out_shape=(
            jax.ShapeDtypeStruct(x.shape, x.dtype),
            jax.ShapeDtypeStruct(r.shape[1:], r.dtype),
            jax.ShapeDtypeStruct(lv.shape, lv.dtype),
        ),
        in_specs=[
            pl.BlockSpec(memory_space=pl.ANY),
            pl.BlockSpec(memory_space=pltpu.VMEM),
            pl.BlockSpec(memory_space=pl.ANY),
        ],
        out_specs=(
            pl.BlockSpec(memory_space=pl.ANY),
            pl.BlockSpec(memory_space=pltpu.VMEM),
            pl.BlockSpec(memory_space=pl.ANY),
        ),
        scratch_shapes=[
            pltpu.VMEM(r.shape, r.dtype),
            pltpu.SemaphoreType.DMA((4, n)),
            pltpu.SemaphoreType.DMA((2,)),
            pltpu.SemaphoreType.DMA((2,)),
        ],
        compiler_params=pltpu.CompilerParams(collective_id=0, has_side_effects=True),
    )(x, r, lv)


def gather_kernel(
    n, m, a_ref, w_ref, share_ref, cs_ref, o_ref, full_ref, got1, got2,
    mixed, rows_got, total, sems, row_sems, local_sems, sib_sems,
):
    me = lax.axis_index("col")
    row = lax.axis_index("row")
    piece_rows = mixed.shape[1]
    row_peers = [(s, lax.rem(row + s, m), lax.rem(row + m - s, m)) for s in range(1, m)]
    barrier = pltpu.get_barrier_semaphore()
    for s, peer, _ in col_peers(n):
        pl.semaphore_signal(barrier, inc=1, device_id=(row, peer), device_id_type=MESH_ID)
    for s, peer, _ in row_peers:
        pl.semaphore_signal(barrier, inc=1, device_id=(peer, me), device_id_type=MESH_ID)
    pl.semaphore_wait(barrier, n - 1 + m - 1)

    own = pltpu.make_async_copy(share_ref, rows_got.at[row], local_sems.at[1])
    own.start()
    sends = [
        (cs_ref.at[0], got1, flipped(row, 2)),
        (cs_ref.at[1], got2.at[0], flipped(row, 4)),
        (cs_ref.at[1], got2.at[1], flipped(flipped(row, 4), 2)),
    ]
    sibs = []
    for i, (src_ref, dst_ref, peer) in enumerate(sends):
        sib = pltpu.make_async_remote_copy(
            src_ref=src_ref, dst_ref=dst_ref,
            send_sem=sib_sems.at[0, i], recv_sem=sib_sems.at[1, i],
            device_id=(peer, me), device_id_type=MESH_ID,
        )
        sib.start()
        sibs.append(sib)

    def part(s, peer, slot):
        return pltpu.make_async_remote_copy(
            src_ref=share_ref, dst_ref=rows_got.at[slot],
            send_sem=row_sems.at[0, s], recv_sem=row_sems.at[1, s],
            device_id=(peer, me), device_id_type=MESH_ID,
        )

    for s, peer, _ in row_peers:
        part(s, peer, row).start()

    def piece(s, peer, slot):
        return pltpu.make_async_remote_copy(
            src_ref=mixed.at[peer], dst_ref=o_ref.at[slot],
            send_sem=sems.at[0, s], recv_sem=sems.at[1, s],
            device_id=(row, peer), device_id_type=MESH_ID,
        )

    def compute(peer):
        first = pl.multiple_of(peer * piece_rows, piece_rows)
        mixed[peer] = jnp.dot(
            w_ref[pl.ds(first, piece_rows), :], a_ref[...], preferred_element_type=jnp.float32
        ).astype(mixed.dtype)

    def compute_and_send(s, carry):
        peer = lax.rem(me + s, n)
        compute(peer)
        piece(s, peer, me).start()
        return carry

    half = n // 2
    lax.fori_loop(1, half, compute_and_send, 0)

    def spread(s, peer, slot):
        return pltpu.make_async_remote_copy(
            src_ref=total, dst_ref=full_ref.at[slot],
            send_sem=sems.at[2, s], recv_sem=sems.at[3, s],
            device_id=(row, peer), device_id_type=MESH_ID,
        )

    for s, peer, source in row_peers:
        part(s, peer, row).wait_send()
        part(s, source, source).wait_recv()
    own.wait()
    total[...] = jnp.sum(rows_got[...], axis=0)
    mine = pltpu.make_async_copy(total, full_ref.at[me], local_sems.at[2])
    mine.start()
    for s, peer, _ in col_peers(n):
        spread(s, peer, me).start()

    lax.fori_loop(half, n, compute_and_send, 0)
    compute(me)
    local = pltpu.make_async_copy(mixed.at[me], o_ref.at[me], local_sems.at[0])
    local.start()

    for s, peer, source in col_peers(n):
        spread(s, peer, me).wait_send()
        spread(s, source, source).wait_recv()
        piece(s, peer, me).wait_send()
        piece(s, source, source).wait_recv()
    mine.wait()
    local.wait()
    for sib in sibs:
        sib.wait()


def gather(a, w, share, cs, n, m):
    piece_rows = w.shape[0] // n
    columns = a.shape[1]
    return pl.pallas_call(
        functools.partial(gather_kernel, n, m),
        out_shape=(
            jax.ShapeDtypeStruct((n, piece_rows, columns), a.dtype),
            jax.ShapeDtypeStruct((n,) + share.shape, share.dtype),
            jax.ShapeDtypeStruct(cs.shape[1:], cs.dtype),
            jax.ShapeDtypeStruct(cs.shape, cs.dtype),
        ),
        in_specs=[
            pl.BlockSpec(memory_space=pltpu.VMEM),
            pl.BlockSpec(memory_space=pltpu.VMEM),
            pl.BlockSpec(memory_space=pltpu.VMEM),
            pl.BlockSpec(memory_space=pl.ANY),
        ],
        out_specs=(
            pl.BlockSpec(memory_space=pl.ANY),
            pl.BlockSpec(memory_space=pltpu.VMEM),
            pl.BlockSpec(memory_space=pl.ANY),
            pl.BlockSpec(memory_space=pl.ANY),
        ),
        scratch_shapes=[
            pltpu.VMEM((n, piece_rows, columns), a.dtype),
            pltpu.VMEM((m,) + share.shape, share.dtype),
            pltpu.VMEM(share.shape, share.dtype),
            pltpu.SemaphoreType.DMA((4, n)),
            pltpu.SemaphoreType.DMA((2, m)),
            pltpu.SemaphoreType.DMA((3,)),
            pltpu.SemaphoreType.DMA((2, 3)),
        ],
        compiler_params=pltpu.CompilerParams(
            collective_id=1, has_side_effects=True, vmem_limit_bytes=48 * 1024 * 1024
        ),
    )(a, w, share, cs)


def per_device(
    right_side,
    leaf_inverse,
    compress,
    middle,
    expand,
    row_project,
    row_expand,
    root_project,
    root_expand,
    owner_map,
):
    lowered = right_side.astype(jnp.bfloat16)
    columns = lowered.shape[1]
    root_term = lax.dot_general(
        root_project, lowered, contract_first, preferred_element_type=jnp.float32
    )
    level_coeffs = jnp.einsum(
        "blr,lw->brw", row_project, lowered, preferred_element_type=jnp.float32
    )
    dense_part = jnp.dot(leaf_inverse, lowered, preferred_element_type=jnp.float32)
    coeffs = lax.dot_general(
        compress, lowered, contract_first, preferred_element_type=jnp.float32
    ).astype(jnp.bfloat16)
    col_count = lax.axis_size("col")
    pieces = coeffs.reshape(col_count, -1, columns)
    chosen = (owner_map[:, None] == jnp.arange(col_count, dtype=owner_map.dtype)[None, :]).astype(
        jnp.bfloat16
    )
    outgoing = jnp.einsum(
        "kd,kxw->dxw", chosen, pieces, preferred_element_type=jnp.float32
    ).astype(jnp.bfloat16)
    root_shares = root_term.reshape(col_count, -1, columns)
    arrived, root_share, pair = scatter(outgoing, root_shares, level_coeffs)
    chip_sums = level_coeffs[1:] + pair[1:]
    returned, root_full, quad_one, quad_two = gather(
        arrived.reshape(-1, columns), middle, root_share, chip_sums, col_count,
        lax.axis_size("row"),
    )
    ordered = jnp.einsum(
        "jd,dxw->jxw", chosen, returned, preferred_element_type=jnp.float32
    ).astype(jnp.bfloat16).reshape(-1, columns)
    cluster_part = jnp.dot(expand, ordered, preferred_element_type=jnp.float32)

    sibling_sum = jnp.stack([pair[0], quad_one, quad_two[0] + quad_two[1]], axis=0)
    root_sum = root_full.reshape(-1, columns)
    coupled = jnp.einsum(
        "blr,brw->lw",
        row_expand,
        sibling_sum.astype(jnp.bfloat16),
        preferred_element_type=jnp.float32,
    )
    root_part = jnp.dot(
        root_expand, root_sum.astype(jnp.bfloat16), preferred_element_type=jnp.float32
    )
    return dense_part + cluster_part + coupled + root_part


def solution(mesh):
    in_specs = (
        P(("row", "col"), None),
        P(("row", "col"), None),
        P(("row", "col"), None),
        P(("row", "col"), None),
        P(("row", "col"), None),
        P(None, ("row", "col"), None),
        P(None, ("row", "col"), None),
        P(("row", "col"), None),
        P(("row", "col"), None),
        P(),
    )
    out_specs = P(("row", "col"), None)
    return jax.shard_map(
        per_device, mesh=mesh, in_specs=in_specs, out_specs=out_specs, check_vma=False
    )
```

```python
import functools

import jax
import jax.numpy as jnp
from jax import lax
from jax.experimental import pallas as pl
from jax.experimental.pallas import tpu as pltpu
from jax.sharding import PartitionSpec as P

contract_first = (((0,), (0,)), ((), ()))
MESH_ID = pl.DeviceIdType.MESH


def swapped(x, axis, bit):
    return lax.ppermute(x, axis, [(i, i ^ 1 << bit) for i in range(lax.axis_size(axis))])


def flipped(index, bit):
    return index + bit - 2 * bit * lax.rem(index // bit, 2)


def col_peers(n):
    me = lax.axis_index("col")
    return [(s, lax.rem(me + s, n), lax.rem(me + n - s, n)) for s in range(1, n)]


def scatter_kernel(n, x_ref, r_ref, lv_ref, o_ref, share_ref, pair_ref, got, sems, local_sems, pair_sems):
    me = lax.axis_index("col")
    row = lax.axis_index("row")
    barrier = pltpu.get_barrier_semaphore()
    for s, peer, _ in col_peers(n):
        pl.semaphore_signal(barrier, inc=1, device_id=(row, peer), device_id_type=MESH_ID)
    partner = flipped(row, 1)
    pl.semaphore_signal(barrier, inc=1, device_id=(partner, me), device_id_type=MESH_ID)
    pl.semaphore_wait(barrier, n)

    levels = pltpu.make_async_remote_copy(
        src_ref=lv_ref, dst_ref=pair_ref,
        send_sem=pair_sems.at[0], recv_sem=pair_sems.at[1],
        device_id=(partner, me), device_id_type=MESH_ID,
    )
    levels.start()
    local = pltpu.make_async_copy(x_ref.at[me], o_ref.at[me], local_sems.at[0])
    local.start()
    own = pltpu.make_async_copy(r_ref.at[me], got.at[me], local_sems.at[1])
    own.start()

    def piece(s, peer, slot):
        return pltpu.make_async_remote_copy(
            src_ref=x_ref.at[peer], dst_ref=o_ref.at[slot],
            send_sem=sems.at[0, s], recv_sem=sems.at[1, s],
            device_id=(row, peer), device_id_type=MESH_ID,
        )

    def share(s, peer, slot):
        return pltpu.make_async_remote_copy(
            src_ref=r_ref.at[peer], dst_ref=got.at[slot],
            send_sem=sems.at[2, s], recv_sem=sems.at[3, s],
            device_id=(row, peer), device_id_type=MESH_ID,
        )

    for s, peer, _ in col_peers(n):
        share(s, peer, me).start()
        piece(s, peer, me).start()
    for s, peer, source in col_peers(n):
        share(s, peer, me).wait_send()
        share(s, source, source).wait_recv()
    own.wait()
    share_ref[...] = jnp.sum(got[...], axis=0)
    for s, peer, source in col_peers(n):
        piece(s, peer, me).wait_send()
        piece(s, source, source).wait_recv()
    local.wait()
    levels.wait()


def scatter(x, r, lv):
    n = x.shape[0]
    return pl.pallas_call(
        functools.partial(scatter_kernel, n),
        out_shape=(
            jax.ShapeDtypeStruct(x.shape, x.dtype),
            jax.ShapeDtypeStruct(r.shape[1:], r.dtype),
            jax.ShapeDtypeStruct(lv.shape, lv.dtype),
        ),
        in_specs=[
            pl.BlockSpec(memory_space=pl.ANY),
            pl.BlockSpec(memory_space=pltpu.VMEM),
            pl.BlockSpec(memory_space=pl.ANY),
        ],
        out_specs=(
            pl.BlockSpec(memory_space=pl.ANY),
            pl.BlockSpec(memory_space=pltpu.VMEM),
            pl.BlockSpec(memory_space=pl.ANY),
        ),
        scratch_shapes=[
            pltpu.VMEM(r.shape, r.dtype),
            pltpu.SemaphoreType.DMA((4, n)),
            pltpu.SemaphoreType.DMA((2,)),
            pltpu.SemaphoreType.DMA((2,)),
        ],
        compiler_params=pltpu.CompilerParams(collective_id=0, has_side_effects=True),
    )(x, r, lv)


def gather_kernel(
    n, m, a_ref, w_ref, share_ref, cs_ref, o_ref, full_ref, got1, got2,
    mixed, rows_got, total, sems, row_sems, local_sems, sib_sems,
):
    me = lax.axis_index("col")
    row = lax.axis_index("row")
    piece_rows = mixed.shape[1]
    row_peers = [(s, lax.rem(row + s, m), lax.rem(row + m - s, m)) for s in range(1, m)]
    barrier = pltpu.get_barrier_semaphore()
    for s, peer, _ in col_peers(n):
        pl.semaphore_signal(barrier, inc=1, device_id=(row, peer), device_id_type=MESH_ID)
    for s, peer, _ in row_peers:
        pl.semaphore_signal(barrier, inc=1, device_id=(peer, me), device_id_type=MESH_ID)
    pl.semaphore_wait(barrier, n - 1 + m - 1)

    own = pltpu.make_async_copy(share_ref, rows_got.at[row], local_sems.at[1])
    own.start()
    sends = [
        (cs_ref.at[0], got1, flipped(row, 2)),
        (cs_ref.at[1], got2.at[0], flipped(row, 4)),
        (cs_ref.at[1], got2.at[1], flipped(flipped(row, 4), 2)),
    ]
    sibs = []
    for i, (src_ref, dst_ref, peer) in enumerate(sends):
        sib = pltpu.make_async_remote_copy(
            src_ref=src_ref, dst_ref=dst_ref,
            send_sem=sib_sems.at[0, i], recv_sem=sib_sems.at[1, i],
            device_id=(peer, me), device_id_type=MESH_ID,
        )
        sib.start()
        sibs.append(sib)

    def part(s, peer, slot):
        return pltpu.make_async_remote_copy(
            src_ref=share_ref, dst_ref=rows_got.at[slot],
            send_sem=row_sems.at[0, s], recv_sem=row_sems.at[1, s],
            device_id=(peer, me), device_id_type=MESH_ID,
        )

    for s, peer, _ in row_peers:
        part(s, peer, row).start()

    def piece(s, peer, slot):
        return pltpu.make_async_remote_copy(
            src_ref=mixed.at[peer], dst_ref=o_ref.at[slot],
            send_sem=sems.at[0, s], recv_sem=sems.at[1, s],
            device_id=(row, peer), device_id_type=MESH_ID,
        )

    def compute(peer):
        first = pl.multiple_of(peer * piece_rows, piece_rows)
        mixed[peer] = jnp.dot(
            w_ref[pl.ds(first, piece_rows), :], a_ref[...], preferred_element_type=jnp.float32
        ).astype(mixed.dtype)

    def compute_and_send(s, carry):
        peer = lax.rem(me + s, n)
        compute(peer)
        piece(s, peer, me).start()
        return carry

    half = n // 2
    lax.fori_loop(1, half, compute_and_send, 0)

    def spread(s, peer, slot):
        return pltpu.make_async_remote_copy(
            src_ref=total, dst_ref=full_ref.at[slot],
            send_sem=sems.at[2, s], recv_sem=sems.at[3, s],
            device_id=(row, peer), device_id_type=MESH_ID,
        )

    for s, peer, source in row_peers:
        part(s, peer, row).wait_send()
        part(s, source, source).wait_recv()
    own.wait()
    total[...] = jnp.sum(rows_got[...], axis=0)
    mine = pltpu.make_async_copy(total, full_ref.at[me], local_sems.at[2])
    mine.start()
    for s, peer, _ in col_peers(n):
        spread(s, peer, me).start()

    lax.fori_loop(half, n, compute_and_send, 0)
    compute(me)
    local = pltpu.make_async_copy(mixed.at[me], o_ref.at[me], local_sems.at[0])
    local.start()

    for s, peer, source in col_peers(n):
        spread(s, peer, me).wait_send()
        spread(s, source, source).wait_recv()
        piece(s, peer, me).wait_send()
        piece(s, source, source).wait_recv()
    mine.wait()
    local.wait()
    for sib in sibs:
        sib.wait()


def gather(a, w, share, cs, n, m):
    piece_rows = w.shape[0] // n
    columns = a.shape[1]
    return pl.pallas_call(
        functools.partial(gather_kernel, n, m),
        out_shape=(
            jax.ShapeDtypeStruct((n, piece_rows, columns), a.dtype),
            jax.ShapeDtypeStruct((n,) + share.shape, share.dtype),
            jax.ShapeDtypeStruct(cs.shape[1:], cs.dtype),
            jax.ShapeDtypeStruct(cs.shape, cs.dtype),
        ),
        in_specs=[
            pl.BlockSpec(memory_space=pltpu.VMEM),
            pl.BlockSpec(memory_space=pltpu.VMEM),
            pl.BlockSpec(memory_space=pltpu.VMEM),
            pl.BlockSpec(memory_space=pl.ANY),
        ],
        out_specs=(
            pl.BlockSpec(memory_space=pl.ANY),
            pl.BlockSpec(memory_space=pltpu.VMEM),
            pl.BlockSpec(memory_space=pl.ANY),
            pl.BlockSpec(memory_space=pl.ANY),
        ),
        scratch_shapes=[
            pltpu.VMEM((n, piece_rows, columns), a.dtype),
            pltpu.VMEM((m,) + share.shape, share.dtype),
            pltpu.VMEM(share.shape, share.dtype),
            pltpu.SemaphoreType.DMA((4, n)),
            pltpu.SemaphoreType.DMA((2, m)),
            pltpu.SemaphoreType.DMA((3,)),
            pltpu.SemaphoreType.DMA((2, 3)),
        ],
        compiler_params=pltpu.CompilerParams(
            collective_id=1, has_side_effects=True, vmem_limit_bytes=48 * 1024 * 1024
        ),
    )(a, w, share, cs)


def per_device(
    right_side,
    leaf_inverse,
    compress,
    middle,
    expand,
    row_project,
    row_expand,
    root_project,
    root_expand,
    owner_map,
):
    lowered = right_side.astype(jnp.bfloat16)
    columns = lowered.shape[1]
    root_term = lax.dot_general(
        root_project, lowered, contract_first, preferred_element_type=jnp.float32
    )
    level_coeffs = jnp.einsum(
        "blr,lw->brw", row_project, lowered, preferred_element_type=jnp.float32
    )
    dense_part = jnp.dot(leaf_inverse, lowered, preferred_element_type=jnp.float32)
    coeffs = lax.dot_general(
        compress, lowered, contract_first, preferred_element_type=jnp.float32
    ).astype(jnp.bfloat16)
    col_count = lax.axis_size("col")
    pieces = coeffs.reshape(col_count, -1, columns)
    chosen = (owner_map[:, None] == jnp.arange(col_count, dtype=owner_map.dtype)[None, :]).astype(
        jnp.bfloat16
    )
    outgoing = jnp.einsum(
        "kd,kxw->dxw", chosen, pieces, preferred_element_type=jnp.float32
    ).astype(jnp.bfloat16)
    root_shares = root_term.reshape(col_count, -1, columns)
    arrived, root_share, pair = scatter(outgoing, root_shares, level_coeffs)
    chip_sums = (level_coeffs[1:] + pair[1:]).astype(jnp.bfloat16)
    returned, root_full, quad_one, quad_two = gather(
        arrived.reshape(-1, columns), middle, root_share, chip_sums, col_count,
        lax.axis_size("row"),
    )
    ordered = jnp.einsum(
        "jd,dxw->jxw", chosen, returned, preferred_element_type=jnp.float32
    ).astype(jnp.bfloat16).reshape(-1, columns)
    cluster_part = jnp.dot(expand, ordered, preferred_element_type=jnp.float32)

    sibling_sum = jnp.stack(
        [
            pair[0],
            quad_one.astype(jnp.float32),
            quad_two[0].astype(jnp.float32) + quad_two[1].astype(jnp.float32),
        ],
        axis=0,
    )
    root_sum = root_full.reshape(-1, columns)
    coupled = jnp.einsum(
        "blr,brw->lw",
        row_expand,
        sibling_sum.astype(jnp.bfloat16),
        preferred_element_type=jnp.float32,
    )
    root_part = jnp.dot(
        root_expand, root_sum.astype(jnp.bfloat16), preferred_element_type=jnp.float32
    )
    return dense_part + cluster_part + coupled + root_part


def solution(mesh):
    in_specs = (
        P(("row", "col"), None),
        P(("row", "col"), None),
        P(("row", "col"), None),
        P(("row", "col"), None),
        P(("row", "col"), None),
        P(None, ("row", "col"), None),
        P(None, ("row", "col"), None),
        P(("row", "col"), None),
        P(("row", "col"), None),
        P(),
    )
    out_specs = P(("row", "col"), None)
    return jax.shard_map(
        per_device, mesh=mesh, in_specs=in_specs, out_specs=out_specs, check_vma=False
    )
```

```python
import functools

import jax
import jax.numpy as jnp
from jax import lax
from jax.experimental import pallas as pl
from jax.experimental.pallas import tpu as pltpu
from jax.sharding import PartitionSpec as P

contract_first = (((0,), (0,)), ((), ()))
MESH_ID = pl.DeviceIdType.MESH


def swapped(x, axis, bit):
    return lax.ppermute(x, axis, [(i, i ^ 1 << bit) for i in range(lax.axis_size(axis))])


def flipped(index, bit):
    return index + bit - 2 * bit * lax.rem(index // bit, 2)


def col_peers(n):
    me = lax.axis_index("col")
    return [(s, lax.rem(me + s, n), lax.rem(me + n - s, n)) for s in range(1, n)]


def scatter_kernel(
    n, x_ref, r_ref, lv_ref, o_ref, share_ref, pair_ref, far_ref, got, sems, local_sems, pair_sems,
):
    me = lax.axis_index("col")
    row = lax.axis_index("row")
    barrier = pltpu.get_barrier_semaphore()
    for s, peer, _ in col_peers(n):
        pl.semaphore_signal(barrier, inc=1, device_id=(row, peer), device_id_type=MESH_ID)
    partner = flipped(row, 1)
    far = [flipped(row, 4), flipped(flipped(row, 4), 2)]
    for peer in [partner] + far:
        pl.semaphore_signal(barrier, inc=1, device_id=(peer, me), device_id_type=MESH_ID)
    pl.semaphore_wait(barrier, n + 2)

    low = pair_ref.shape[0]
    level_copies = [
        pltpu.make_async_remote_copy(
            src_ref=lv_ref.at[pl.ds(0, low)], dst_ref=pair_ref,
            send_sem=pair_sems.at[0, 0], recv_sem=pair_sems.at[1, 0],
            device_id=(partner, me), device_id_type=MESH_ID,
        )
    ]
    for i, peer in enumerate(far):
        level_copies.append(
            pltpu.make_async_remote_copy(
                src_ref=lv_ref.at[low], dst_ref=far_ref.at[i],
                send_sem=pair_sems.at[0, i + 1], recv_sem=pair_sems.at[1, i + 1],
                device_id=(peer, me), device_id_type=MESH_ID,
            )
        )
    for copy in level_copies:
        copy.start()
    local = pltpu.make_async_copy(x_ref.at[me], o_ref.at[me], local_sems.at[0])
    local.start()
    own = pltpu.make_async_copy(r_ref.at[me], got.at[me], local_sems.at[1])
    own.start()

    def piece(s, peer, slot):
        return pltpu.make_async_remote_copy(
            src_ref=x_ref.at[peer], dst_ref=o_ref.at[slot],
            send_sem=sems.at[0, s], recv_sem=sems.at[1, s],
            device_id=(row, peer), device_id_type=MESH_ID,
        )

    def share(s, peer, slot):
        return pltpu.make_async_remote_copy(
            src_ref=r_ref.at[peer], dst_ref=got.at[slot],
            send_sem=sems.at[2, s], recv_sem=sems.at[3, s],
            device_id=(row, peer), device_id_type=MESH_ID,
        )

    for s, peer, _ in col_peers(n):
        share(s, peer, me).start()
        piece(s, peer, me).start()
    for s, peer, source in col_peers(n):
        share(s, peer, me).wait_send()
        share(s, source, source).wait_recv()
    own.wait()
    share_ref[...] = jnp.sum(got[...], axis=0)
    for s, peer, source in col_peers(n):
        piece(s, peer, me).wait_send()
        piece(s, source, source).wait_recv()
    local.wait()
    for copy in level_copies:
        copy.wait()


def scatter(x, r, lv):
    n = x.shape[0]
    return pl.pallas_call(
        functools.partial(scatter_kernel, n),
        out_shape=(
            jax.ShapeDtypeStruct(x.shape, x.dtype),
            jax.ShapeDtypeStruct(r.shape[1:], r.dtype),
            jax.ShapeDtypeStruct((lv.shape[0] - 1,) + lv.shape[1:], lv.dtype),
            jax.ShapeDtypeStruct((2,) + lv.shape[1:], lv.dtype),
        ),
        in_specs=[
            pl.BlockSpec(memory_space=pl.ANY),
            pl.BlockSpec(memory_space=pltpu.VMEM),
            pl.BlockSpec(memory_space=pl.ANY),
        ],
        out_specs=(
            pl.BlockSpec(memory_space=pl.ANY),
            pl.BlockSpec(memory_space=pltpu.VMEM),
            pl.BlockSpec(memory_space=pl.ANY),
            pl.BlockSpec(memory_space=pl.ANY),
        ),
        scratch_shapes=[
            pltpu.VMEM(r.shape, r.dtype),
            pltpu.SemaphoreType.DMA((4, n)),
            pltpu.SemaphoreType.DMA((2,)),
            pltpu.SemaphoreType.DMA((2, 3)),
        ],
        compiler_params=pltpu.CompilerParams(collective_id=0, has_side_effects=True),
    )(x, r, lv)


def gather_kernel(
    n, m, a_ref, w_ref, share_ref, c1_ref, p_ref, o_ref, full_ref, got1, got2,
    mixed, rows_got, total, sems, row_sems, local_sems, sib_sems,
):
    me = lax.axis_index("col")
    row = lax.axis_index("row")
    piece_rows = mixed.shape[1]
    row_peers = [(s, lax.rem(row + s, m), lax.rem(row + m - s, m)) for s in range(1, m)]
    barrier = pltpu.get_barrier_semaphore()
    for s, peer, _ in col_peers(n):
        pl.semaphore_signal(barrier, inc=1, device_id=(row, peer), device_id_type=MESH_ID)
    for s, peer, _ in row_peers:
        pl.semaphore_signal(barrier, inc=1, device_id=(peer, me), device_id_type=MESH_ID)
    pl.semaphore_wait(barrier, n - 1 + m - 1)

    own = pltpu.make_async_copy(share_ref, rows_got.at[row], local_sems.at[1])
    own.start()
    sends = [(c1_ref, got1, flipped(row, 2)), (p_ref, got2, flipped(row, 1))]
    sibs = []
    for i, (src_ref, dst_ref, peer) in enumerate(sends):
        sib = pltpu.make_async_remote_copy(
            src_ref=src_ref, dst_ref=dst_ref,
            send_sem=sib_sems.at[0, i], recv_sem=sib_sems.at[1, i],
            device_id=(peer, me), device_id_type=MESH_ID,
        )
        sib.start()
        sibs.append(sib)

    def part(s, peer, slot):
        return pltpu.make_async_remote_copy(
            src_ref=share_ref, dst_ref=rows_got.at[slot],
            send_sem=row_sems.at[0, s], recv_sem=row_sems.at[1, s],
            device_id=(peer, me), device_id_type=MESH_ID,
        )

    for s, peer, _ in row_peers:
        part(s, peer, row).start()

    def piece(s, peer, slot):
        return pltpu.make_async_remote_copy(
            src_ref=mixed.at[peer], dst_ref=o_ref.at[slot],
            send_sem=sems.at[0, s], recv_sem=sems.at[1, s],
            device_id=(row, peer), device_id_type=MESH_ID,
        )

    def compute(peer):
        first = pl.multiple_of(peer * piece_rows, piece_rows)
        mixed[peer] = jnp.dot(
            w_ref[pl.ds(first, piece_rows), :], a_ref[...], preferred_element_type=jnp.float32
        ).astype(mixed.dtype)

    def compute_and_send(s, carry):
        peer = lax.rem(me + s, n)
        compute(peer)
        piece(s, peer, me).start()
        return carry

    half = n // 2
    lax.fori_loop(1, half, compute_and_send, 0)

    def spread(s, peer, slot):
        return pltpu.make_async_remote_copy(
            src_ref=total, dst_ref=full_ref.at[slot],
            send_sem=sems.at[2, s], recv_sem=sems.at[3, s],
            device_id=(row, peer), device_id_type=MESH_ID,
        )

    for s, peer, source in row_peers:
        part(s, peer, row).wait_send()
        part(s, source, source).wait_recv()
    own.wait()
    total[...] = jnp.sum(rows_got[...], axis=0)
    mine = pltpu.make_async_copy(total, full_ref.at[me], local_sems.at[2])
    mine.start()
    for s, peer, _ in col_peers(n):
        spread(s, peer, me).start()

    lax.fori_loop(half, n, compute_and_send, 0)
    compute(me)
    local = pltpu.make_async_copy(mixed.at[me], o_ref.at[me], local_sems.at[0])
    local.start()

    for s, peer, source in col_peers(n):
        spread(s, peer, me).wait_send()
        spread(s, source, source).wait_recv()
        piece(s, peer, me).wait_send()
        piece(s, source, source).wait_recv()
    mine.wait()
    local.wait()
    for sib in sibs:
        sib.wait()


def gather(a, w, share, c1, p, n, m):
    piece_rows = w.shape[0] // n
    columns = a.shape[1]
    return pl.pallas_call(
        functools.partial(gather_kernel, n, m),
        out_shape=(
            jax.ShapeDtypeStruct((n, piece_rows, columns), a.dtype),
            jax.ShapeDtypeStruct((n,) + share.shape, share.dtype),
            jax.ShapeDtypeStruct(c1.shape, c1.dtype),
            jax.ShapeDtypeStruct(p.shape, p.dtype),
        ),
        in_specs=[
            pl.BlockSpec(memory_space=pltpu.VMEM),
            pl.BlockSpec(memory_space=pltpu.VMEM),
            pl.BlockSpec(memory_space=pltpu.VMEM),
            pl.BlockSpec(memory_space=pl.ANY),
            pl.BlockSpec(memory_space=pl.ANY),
        ],
        out_specs=(
            pl.BlockSpec(memory_space=pl.ANY),
            pl.BlockSpec(memory_space=pltpu.VMEM),
            pl.BlockSpec(memory_space=pl.ANY),
            pl.BlockSpec(memory_space=pl.ANY),
        ),
        scratch_shapes=[
            pltpu.VMEM((n, piece_rows, columns), a.dtype),
            pltpu.VMEM((m,) + share.shape, share.dtype),
            pltpu.VMEM(share.shape, share.dtype),
            pltpu.SemaphoreType.DMA((4, n)),
            pltpu.SemaphoreType.DMA((2, m)),
            pltpu.SemaphoreType.DMA((3,)),
            pltpu.SemaphoreType.DMA((2, 2)),
        ],
        compiler_params=pltpu.CompilerParams(
            collective_id=1, has_side_effects=True, vmem_limit_bytes=48 * 1024 * 1024
        ),
    )(a, w, share, c1, p)


def per_device(
    right_side,
    leaf_inverse,
    compress,
    middle,
    expand,
    row_project,
    row_expand,
    root_project,
    root_expand,
    owner_map,
):
    lowered = right_side.astype(jnp.bfloat16)
    columns = lowered.shape[1]
    root_term = lax.dot_general(
        root_project, lowered, contract_first, preferred_element_type=jnp.float32
    )
    level_coeffs = jnp.einsum(
        "blr,lw->brw", row_project, lowered, preferred_element_type=jnp.float32
    )
    dense_part = jnp.dot(leaf_inverse, lowered, preferred_element_type=jnp.float32)
    coeffs = lax.dot_general(
        compress, lowered, contract_first, preferred_element_type=jnp.float32
    ).astype(jnp.bfloat16)
    col_count = lax.axis_size("col")
    pieces = coeffs.reshape(col_count, -1, columns)
    chosen = (owner_map[:, None] == jnp.arange(col_count, dtype=owner_map.dtype)[None, :]).astype(
        jnp.bfloat16
    )
    outgoing = jnp.einsum(
        "kd,kxw->dxw", chosen, pieces, preferred_element_type=jnp.float32
    ).astype(jnp.bfloat16)
    root_shares = root_term.reshape(col_count, -1, columns)
    arrived, root_share, pair, far = scatter(outgoing, root_shares, level_coeffs)
    pair_sum = (level_coeffs[1] + pair[1]).astype(jnp.bfloat16)
    far_sum = far[0] + far[1]
    returned, root_full, quad_one, quad_two = gather(
        arrived.reshape(-1, columns), middle, root_share, pair_sum, far_sum, col_count,
        lax.axis_size("row"),
    )
    ordered = jnp.einsum(
        "jd,dxw->jxw", chosen, returned, preferred_element_type=jnp.float32
    ).astype(jnp.bfloat16).reshape(-1, columns)
    cluster_part = jnp.dot(expand, ordered, preferred_element_type=jnp.float32)

    sibling_sum = jnp.stack(
        [pair[0], quad_one.astype(jnp.float32), far_sum + quad_two], axis=0
    )
    root_sum = root_full.reshape(-1, columns)
    coupled = jnp.einsum(
        "blr,brw->lw",
        row_expand,
        sibling_sum.astype(jnp.bfloat16),
        preferred_element_type=jnp.float32,
    )
    root_part = jnp.dot(
        root_expand, root_sum.astype(jnp.bfloat16), preferred_element_type=jnp.float32
    )
    return dense_part + cluster_part + coupled + root_part


def solution(mesh):
    in_specs = (
        P(("row", "col"), None),
        P(("row", "col"), None),
        P(("row", "col"), None),
        P(("row", "col"), None),
        P(("row", "col"), None),
        P(None, ("row", "col"), None),
        P(None, ("row", "col"), None),
        P(("row", "col"), None),
        P(("row", "col"), None),
        P(),
    )
    out_specs = P(("row", "col"), None)
    return jax.shard_map(
        per_device, mesh=mesh, in_specs=in_specs, out_specs=out_specs, check_vma=False
    )
```

```python
import functools

import jax
import jax.numpy as jnp
from jax import lax
from jax.experimental import pallas as pl
from jax.experimental.pallas import tpu as pltpu
from jax.sharding import PartitionSpec as P

contract_first = (((0,), (0,)), ((), ()))
MESH_ID = pl.DeviceIdType.MESH


def swapped(x, axis, bit):
    return lax.ppermute(x, axis, [(i, i ^ 1 << bit) for i in range(lax.axis_size(axis))])


def flipped(index, bit):
    return index + bit - 2 * bit * lax.rem(index // bit, 2)


def col_peers(n):
    me = lax.axis_index("col")
    return [(s, lax.rem(me + s, n), lax.rem(me + n - s, n)) for s in range(1, n)]


def scatter_kernel(
    n, x_ref, r_ref, lv_ref, o_ref, share_ref, pair_ref, far_ref, got, sems, local_sems, pair_sems,
):
    me = lax.axis_index("col")
    row = lax.axis_index("row")
    barrier = pltpu.get_barrier_semaphore()
    for s, peer, _ in col_peers(n):
        pl.semaphore_signal(barrier, inc=1, device_id=(row, peer), device_id_type=MESH_ID)
    partner = flipped(row, 1)
    far = [flipped(row, 4), flipped(flipped(row, 4), 2)]
    for peer in [partner] + far:
        pl.semaphore_signal(barrier, inc=1, device_id=(peer, me), device_id_type=MESH_ID)
    pl.semaphore_wait(barrier, n + 2)

    low = pair_ref.shape[0]
    level_copies = [
        pltpu.make_async_remote_copy(
            src_ref=lv_ref.at[pl.ds(0, low)], dst_ref=pair_ref,
            send_sem=pair_sems.at[0, 0], recv_sem=pair_sems.at[1, 0],
            device_id=(partner, me), device_id_type=MESH_ID,
        )
    ]
    for i, peer in enumerate(far):
        level_copies.append(
            pltpu.make_async_remote_copy(
                src_ref=lv_ref.at[low], dst_ref=far_ref.at[i],
                send_sem=pair_sems.at[0, i + 1], recv_sem=pair_sems.at[1, i + 1],
                device_id=(peer, me), device_id_type=MESH_ID,
            )
        )
    for copy in level_copies:
        copy.start()
    local = pltpu.make_async_copy(x_ref.at[me], o_ref.at[me], local_sems.at[0])
    local.start()
    own = pltpu.make_async_copy(r_ref.at[me], got.at[me], local_sems.at[1])
    own.start()

    def piece(s, peer, slot):
        return pltpu.make_async_remote_copy(
            src_ref=x_ref.at[peer], dst_ref=o_ref.at[slot],
            send_sem=sems.at[0, s], recv_sem=sems.at[1, s],
            device_id=(row, peer), device_id_type=MESH_ID,
        )

    def share(s, peer, slot):
        return pltpu.make_async_remote_copy(
            src_ref=r_ref.at[peer], dst_ref=got.at[slot],
            send_sem=sems.at[2, s], recv_sem=sems.at[3, s],
            device_id=(row, peer), device_id_type=MESH_ID,
        )

    for s, peer, _ in col_peers(n):
        share(s, peer, me).start()
        piece(s, peer, me).start()
    for s, peer, source in col_peers(n):
        share(s, peer, me).wait_send()
        share(s, source, source).wait_recv()
    own.wait()
    share_ref[...] = jnp.sum(got[...], axis=0)
    for s, peer, source in col_peers(n):
        piece(s, peer, me).wait_send()
        piece(s, source, source).wait_recv()
    local.wait()
    for copy in level_copies:
        copy.wait()


def scatter(x, r, lv):
    n = x.shape[0]
    return pl.pallas_call(
        functools.partial(scatter_kernel, n),
        out_shape=(
            jax.ShapeDtypeStruct(x.shape, x.dtype),
            jax.ShapeDtypeStruct(r.shape[1:], r.dtype),
            jax.ShapeDtypeStruct((lv.shape[0] - 1,) + lv.shape[1:], lv.dtype),
            jax.ShapeDtypeStruct((2,) + lv.shape[1:], lv.dtype),
        ),
        in_specs=[
            pl.BlockSpec(memory_space=pl.ANY),
            pl.BlockSpec(memory_space=pltpu.VMEM),
            pl.BlockSpec(memory_space=pl.ANY),
        ],
        out_specs=(
            pl.BlockSpec(memory_space=pl.ANY),
            pl.BlockSpec(memory_space=pltpu.VMEM),
            pl.BlockSpec(memory_space=pl.ANY),
            pl.BlockSpec(memory_space=pl.ANY),
        ),
        scratch_shapes=[
            pltpu.VMEM(r.shape, r.dtype),
            pltpu.SemaphoreType.DMA((4, n)),
            pltpu.SemaphoreType.DMA((2,)),
            pltpu.SemaphoreType.DMA((2, 3)),
        ],
        compiler_params=pltpu.CompilerParams(
            collective_id=0, has_side_effects=True, vmem_limit_bytes=4 * 1024 * 1024
        ),
    )(x, r, lv)


def gather_kernel(
    n, m, a_ref, w_ref, share_ref, c1_ref, p_ref, o_ref, full_ref, got1, got2,
    mixed, rows_got, total, sems, row_sems, local_sems, sib_sems,
):
    me = lax.axis_index("col")
    row = lax.axis_index("row")
    piece_rows = mixed.shape[1]
    row_peers = [(s, lax.rem(row + s, m), lax.rem(row + m - s, m)) for s in range(1, m)]
    barrier = pltpu.get_barrier_semaphore()
    for s, peer, _ in col_peers(n):
        pl.semaphore_signal(barrier, inc=1, device_id=(row, peer), device_id_type=MESH_ID)
    for s, peer, _ in row_peers:
        pl.semaphore_signal(barrier, inc=1, device_id=(peer, me), device_id_type=MESH_ID)
    pl.semaphore_wait(barrier, n - 1 + m - 1)

    own = pltpu.make_async_copy(share_ref, rows_got.at[row], local_sems.at[1])
    own.start()
    sends = [(c1_ref, got1, flipped(row, 2)), (p_ref, got2, flipped(row, 1))]
    sibs = []
    for i, (src_ref, dst_ref, peer) in enumerate(sends):
        sib = pltpu.make_async_remote_copy(
            src_ref=src_ref, dst_ref=dst_ref,
            send_sem=sib_sems.at[0, i], recv_sem=sib_sems.at[1, i],
            device_id=(peer, me), device_id_type=MESH_ID,
        )
        sib.start()
        sibs.append(sib)

    def part(s, peer, slot):
        return pltpu.make_async_remote_copy(
            src_ref=share_ref, dst_ref=rows_got.at[slot],
            send_sem=row_sems.at[0, s], recv_sem=row_sems.at[1, s],
            device_id=(peer, me), device_id_type=MESH_ID,
        )

    for s, peer, _ in row_peers:
        part(s, peer, row).start()

    def piece(s, peer, slot):
        return pltpu.make_async_remote_copy(
            src_ref=mixed.at[peer], dst_ref=o_ref.at[slot],
            send_sem=sems.at[0, s], recv_sem=sems.at[1, s],
            device_id=(row, peer), device_id_type=MESH_ID,
        )

    def compute(peer):
        first = pl.multiple_of(peer * piece_rows, piece_rows)
        mixed[peer] = jnp.dot(
            w_ref[pl.ds(first, piece_rows), :], a_ref[...], preferred_element_type=jnp.float32
        ).astype(mixed.dtype)

    def compute_and_send(s, carry):
        peer = lax.rem(me + s, n)
        compute(peer)
        piece(s, peer, me).start()
        return carry

    half = n // 2
    lax.fori_loop(1, half, compute_and_send, 0)

    def spread(s, peer, slot):
        return pltpu.make_async_remote_copy(
            src_ref=total, dst_ref=full_ref.at[slot],
            send_sem=sems.at[2, s], recv_sem=sems.at[3, s],
            device_id=(row, peer), device_id_type=MESH_ID,
        )

    for s, peer, source in row_peers:
        part(s, peer, row).wait_send()
        part(s, source, source).wait_recv()
    own.wait()
    total[...] = jnp.sum(rows_got[...], axis=0)
    mine = pltpu.make_async_copy(total, full_ref.at[me], local_sems.at[2])
    mine.start()
    for s, peer, _ in col_peers(n):
        spread(s, peer, me).start()

    lax.fori_loop(half, n, compute_and_send, 0)
    compute(me)
    local = pltpu.make_async_copy(mixed.at[me], o_ref.at[me], local_sems.at[0])
    local.start()

    for s, peer, source in col_peers(n):
        spread(s, peer, me).wait_send()
        spread(s, source, source).wait_recv()
        piece(s, peer, me).wait_send()
        piece(s, source, source).wait_recv()
    mine.wait()
    local.wait()
    for sib in sibs:
        sib.wait()


def gather(a, w, share, c1, p, n, m):
    piece_rows = w.shape[0] // n
    columns = a.shape[1]
    return pl.pallas_call(
        functools.partial(gather_kernel, n, m),
        out_shape=(
            jax.ShapeDtypeStruct((n, piece_rows, columns), a.dtype),
            jax.ShapeDtypeStruct((n,) + share.shape, share.dtype),
            jax.ShapeDtypeStruct(c1.shape, c1.dtype),
            jax.ShapeDtypeStruct(p.shape, p.dtype),
        ),
        in_specs=[
            pl.BlockSpec(memory_space=pltpu.VMEM),
            pl.BlockSpec(memory_space=pltpu.VMEM),
            pl.BlockSpec(memory_space=pltpu.VMEM),
            pl.BlockSpec(memory_space=pl.ANY),
            pl.BlockSpec(memory_space=pl.ANY),
        ],
        out_specs=(
            pl.BlockSpec(memory_space=pl.ANY),
            pl.BlockSpec(memory_space=pltpu.VMEM),
            pl.BlockSpec(memory_space=pl.ANY),
            pl.BlockSpec(memory_space=pl.ANY),
        ),
        scratch_shapes=[
            pltpu.VMEM((n, piece_rows, columns), a.dtype),
            pltpu.VMEM((m,) + share.shape, share.dtype),
            pltpu.VMEM(share.shape, share.dtype),
            pltpu.SemaphoreType.DMA((4, n)),
            pltpu.SemaphoreType.DMA((2, m)),
            pltpu.SemaphoreType.DMA((3,)),
            pltpu.SemaphoreType.DMA((2, 2)),
        ],
        compiler_params=pltpu.CompilerParams(
            collective_id=1, has_side_effects=True, vmem_limit_bytes=48 * 1024 * 1024
        ),
    )(a, w, share, c1, p)


def per_device(
    right_side,
    leaf_inverse,
    compress,
    middle,
    expand,
    row_project,
    row_expand,
    root_project,
    root_expand,
    owner_map,
):
    lowered = right_side.astype(jnp.bfloat16)
    columns = lowered.shape[1]
    root_term = lax.dot_general(
        root_project, lowered, contract_first, preferred_element_type=jnp.float32
    )
    level_coeffs = jnp.einsum(
        "blr,lw->brw", row_project, lowered, preferred_element_type=jnp.float32
    )
    dense_part = jnp.dot(leaf_inverse, lowered, preferred_element_type=jnp.float32)
    coeffs = lax.dot_general(
        compress, lowered, contract_first, preferred_element_type=jnp.float32
    ).astype(jnp.bfloat16)
    col_count = lax.axis_size("col")
    pieces = coeffs.reshape(col_count, -1, columns)
    chosen = (owner_map[:, None] == jnp.arange(col_count, dtype=owner_map.dtype)[None, :]).astype(
        jnp.bfloat16
    )
    outgoing = jnp.einsum(
        "kd,kxw->dxw", chosen, pieces, preferred_element_type=jnp.float32
    ).astype(jnp.bfloat16)
    root_shares = root_term.reshape(col_count, -1, columns)
    arrived, root_share, pair, far = scatter(outgoing, root_shares, level_coeffs)
    pair_sum = (level_coeffs[1] + pair[1]).astype(jnp.bfloat16)
    far_sum = far[0] + far[1]
    returned, root_full, quad_one, quad_two = gather(
        arrived.reshape(-1, columns), middle, root_share, pair_sum, far_sum, col_count,
        lax.axis_size("row"),
    )
    ordered = jnp.einsum(
        "jd,dxw->jxw", chosen, returned, preferred_element_type=jnp.float32
    ).astype(jnp.bfloat16).reshape(-1, columns)
    cluster_part = jnp.dot(expand, ordered, preferred_element_type=jnp.float32)

    sibling_sum = jnp.stack(
        [pair[0], quad_one.astype(jnp.float32), far_sum + quad_two], axis=0
    )
    root_sum = root_full.reshape(-1, columns)
    coupled = jnp.einsum(
        "blr,brw->lw",
        row_expand,
        sibling_sum.astype(jnp.bfloat16),
        preferred_element_type=jnp.float32,
    )
    root_part = jnp.dot(
        root_expand, root_sum.astype(jnp.bfloat16), preferred_element_type=jnp.float32
    )
    return dense_part + cluster_part + coupled + root_part


def solution(mesh):
    in_specs = (
        P(("row", "col"), None),
        P(("row", "col"), None),
        P(("row", "col"), None),
        P(("row", "col"), None),
        P(("row", "col"), None),
        P(None, ("row", "col"), None),
        P(None, ("row", "col"), None),
        P(("row", "col"), None),
        P(("row", "col"), None),
        P(),
    )
    out_specs = P(("row", "col"), None)
    return jax.shard_map(
        per_device, mesh=mesh, in_specs=in_specs, out_specs=out_specs, check_vma=False
    )
```

```python
import functools

import jax
import jax.numpy as jnp
from jax import lax
from jax.experimental import pallas as pl
from jax.experimental.pallas import tpu as pltpu
from jax.sharding import PartitionSpec as P

contract_first = (((0,), (0,)), ((), ()))
MESH_ID = pl.DeviceIdType.MESH


def swapped(x, axis, bit):
    return lax.ppermute(x, axis, [(i, i ^ 1 << bit) for i in range(lax.axis_size(axis))])


def flipped(index, bit):
    return index + bit - 2 * bit * lax.rem(index // bit, 2)


def col_peers(n):
    me = lax.axis_index("col")
    return [(s, lax.rem(me + s, n), lax.rem(me + n - s, n)) for s in range(1, n)]


def scatter_kernel(
    n, x_ref, r_ref, lv_ref, o_ref, share_ref, pair_ref, far_ref, got, sems, local_sems, pair_sems,
):
    me = lax.axis_index("col")
    row = lax.axis_index("row")
    barrier = pltpu.get_barrier_semaphore()
    for s, peer, _ in col_peers(n):
        pl.semaphore_signal(barrier, inc=1, device_id=(row, peer), device_id_type=MESH_ID)
    partner = flipped(row, 1)
    far = [flipped(row, 4), flipped(flipped(row, 4), 2)]
    for peer in [partner] + far:
        pl.semaphore_signal(barrier, inc=1, device_id=(peer, me), device_id_type=MESH_ID)
    pl.semaphore_wait(barrier, n + 2)

    low = pair_ref.shape[0]
    level_copies = [
        pltpu.make_async_remote_copy(
            src_ref=lv_ref.at[pl.ds(0, low)], dst_ref=pair_ref,
            send_sem=pair_sems.at[0, 0], recv_sem=pair_sems.at[1, 0],
            device_id=(partner, me), device_id_type=MESH_ID,
        )
    ]
    for i, peer in enumerate(far):
        level_copies.append(
            pltpu.make_async_remote_copy(
                src_ref=lv_ref.at[low], dst_ref=far_ref.at[i],
                send_sem=pair_sems.at[0, i + 1], recv_sem=pair_sems.at[1, i + 1],
                device_id=(peer, me), device_id_type=MESH_ID,
            )
        )
    for copy in level_copies:
        copy.start()
    local = pltpu.make_async_copy(x_ref.at[me], o_ref.at[me], local_sems.at[0])
    local.start()
    own = pltpu.make_async_copy(r_ref.at[me], got.at[me], local_sems.at[1])
    own.start()

    def piece(s, peer, slot):
        return pltpu.make_async_remote_copy(
            src_ref=x_ref.at[peer], dst_ref=o_ref.at[slot],
            send_sem=sems.at[0, s], recv_sem=sems.at[1, s],
            device_id=(row, peer), device_id_type=MESH_ID,
        )

    def share(s, peer, slot):
        return pltpu.make_async_remote_copy(
            src_ref=r_ref.at[peer], dst_ref=got.at[slot],
            send_sem=sems.at[2, s], recv_sem=sems.at[3, s],
            device_id=(row, peer), device_id_type=MESH_ID,
        )

    for s, peer, _ in col_peers(n):
        share(s, peer, me).start()
        piece(s, peer, me).start()
    for s, peer, source in col_peers(n):
        share(s, peer, me).wait_send()
        share(s, source, source).wait_recv()
    own.wait()
    share_ref[...] = jnp.sum(got[...], axis=0)
    for s, peer, source in col_peers(n):
        piece(s, peer, me).wait_send()
        piece(s, source, source).wait_recv()
    local.wait()
    for copy in level_copies:
        copy.wait()


def scatter(x, r, lv):
    n = x.shape[0]
    return pl.pallas_call(
        functools.partial(scatter_kernel, n),
        out_shape=(
            jax.ShapeDtypeStruct(x.shape, x.dtype),
            jax.ShapeDtypeStruct(r.shape[1:], r.dtype),
            jax.ShapeDtypeStruct((lv.shape[0] - 1,) + lv.shape[1:], lv.dtype),
            jax.ShapeDtypeStruct((2,) + lv.shape[1:], lv.dtype),
        ),
        in_specs=[
            pl.BlockSpec(memory_space=pl.ANY),
            pl.BlockSpec(memory_space=pltpu.VMEM),
            pl.BlockSpec(memory_space=pl.ANY),
        ],
        out_specs=(
            pl.BlockSpec(memory_space=pl.ANY),
            pl.BlockSpec(memory_space=pltpu.VMEM),
            pl.BlockSpec(memory_space=pl.ANY),
            pl.BlockSpec(memory_space=pl.ANY),
        ),
        scratch_shapes=[
            pltpu.VMEM(r.shape, r.dtype),
            pltpu.SemaphoreType.DMA((4, n)),
            pltpu.SemaphoreType.DMA((2,)),
            pltpu.SemaphoreType.DMA((2, 3)),
        ],
        compiler_params=pltpu.CompilerParams(
            collective_id=0, has_side_effects=True, vmem_limit_bytes=4 * 1024 * 1024
        ),
    )(x, r, lv)


def gather_kernel(
    n, m, a_ref, w_ref, share_ref, c1_ref, p_ref, o_ref, full_ref, got1, got2,
    mixed, rows_got, total, sems, row_sems, local_sems, sib_sems,
):
    me = lax.axis_index("col")
    row = lax.axis_index("row")
    piece_rows = mixed.shape[1]
    row_peers = [(s, lax.rem(row + s, m), lax.rem(row + m - s, m)) for s in range(1, m)]

    def compute(peer):
        first = pl.multiple_of(peer * piece_rows, piece_rows)
        mixed[peer] = jnp.dot(
            w_ref[pl.ds(first, piece_rows), :], a_ref[...], preferred_element_type=jnp.float32
        ).astype(mixed.dtype)

    def compute_one(peer, carry):
        compute(peer)
        return carry

    lax.fori_loop(0, n, compute_one, 0)

    barrier = pltpu.get_barrier_semaphore()
    for s, peer, _ in col_peers(n):
        pl.semaphore_signal(barrier, inc=1, device_id=(row, peer), device_id_type=MESH_ID)
    for s, peer, _ in row_peers:
        pl.semaphore_signal(barrier, inc=1, device_id=(peer, me), device_id_type=MESH_ID)
    pl.semaphore_wait(barrier, n - 1 + m - 1)

    own = pltpu.make_async_copy(share_ref, rows_got.at[row], local_sems.at[1])
    own.start()
    sends = [(c1_ref, got1, flipped(row, 2)), (p_ref, got2, flipped(row, 1))]
    sibs = []
    for i, (src_ref, dst_ref, peer) in enumerate(sends):
        sib = pltpu.make_async_remote_copy(
            src_ref=src_ref, dst_ref=dst_ref,
            send_sem=sib_sems.at[0, i], recv_sem=sib_sems.at[1, i],
            device_id=(peer, me), device_id_type=MESH_ID,
        )
        sib.start()
        sibs.append(sib)

    def part(s, peer, slot):
        return pltpu.make_async_remote_copy(
            src_ref=share_ref, dst_ref=rows_got.at[slot],
            send_sem=row_sems.at[0, s], recv_sem=row_sems.at[1, s],
            device_id=(peer, me), device_id_type=MESH_ID,
        )

    for s, peer, _ in row_peers:
        part(s, peer, row).start()

    def piece(s, peer, slot):
        return pltpu.make_async_remote_copy(
            src_ref=mixed.at[peer], dst_ref=o_ref.at[slot],
            send_sem=sems.at[0, s], recv_sem=sems.at[1, s],
            device_id=(row, peer), device_id_type=MESH_ID,
        )

    for s, peer, _ in col_peers(n):
        piece(s, peer, me).start()
    local = pltpu.make_async_copy(mixed.at[me], o_ref.at[me], local_sems.at[0])
    local.start()

    def spread(s, peer, slot):
        return pltpu.make_async_remote_copy(
            src_ref=total, dst_ref=full_ref.at[slot],
            send_sem=sems.at[2, s], recv_sem=sems.at[3, s],
            device_id=(row, peer), device_id_type=MESH_ID,
        )

    for s, peer, source in row_peers:
        part(s, peer, row).wait_send()
        part(s, source, source).wait_recv()
    own.wait()
    total[...] = jnp.sum(rows_got[...], axis=0)
    mine = pltpu.make_async_copy(total, full_ref.at[me], local_sems.at[2])
    mine.start()
    for s, peer, _ in col_peers(n):
        spread(s, peer, me).start()


    for s, peer, source in col_peers(n):
        spread(s, peer, me).wait_send()
        spread(s, source, source).wait_recv()
        piece(s, peer, me).wait_send()
        piece(s, source, source).wait_recv()
    mine.wait()
    local.wait()
    for sib in sibs:
        sib.wait()


def gather(a, w, share, c1, p, n, m):
    piece_rows = w.shape[0] // n
    columns = a.shape[1]
    return pl.pallas_call(
        functools.partial(gather_kernel, n, m),
        out_shape=(
            jax.ShapeDtypeStruct((n, piece_rows, columns), a.dtype),
            jax.ShapeDtypeStruct((n,) + share.shape, share.dtype),
            jax.ShapeDtypeStruct(c1.shape, c1.dtype),
            jax.ShapeDtypeStruct(p.shape, p.dtype),
        ),
        in_specs=[
            pl.BlockSpec(memory_space=pltpu.VMEM),
            pl.BlockSpec(memory_space=pltpu.VMEM),
            pl.BlockSpec(memory_space=pltpu.VMEM),
            pl.BlockSpec(memory_space=pl.ANY),
            pl.BlockSpec(memory_space=pl.ANY),
        ],
        out_specs=(
            pl.BlockSpec(memory_space=pl.ANY),
            pl.BlockSpec(memory_space=pltpu.VMEM),
            pl.BlockSpec(memory_space=pl.ANY),
            pl.BlockSpec(memory_space=pl.ANY),
        ),
        scratch_shapes=[
            pltpu.VMEM((n, piece_rows, columns), a.dtype),
            pltpu.VMEM((m,) + share.shape, share.dtype),
            pltpu.VMEM(share.shape, share.dtype),
            pltpu.SemaphoreType.DMA((4, n)),
            pltpu.SemaphoreType.DMA((2, m)),
            pltpu.SemaphoreType.DMA((3,)),
            pltpu.SemaphoreType.DMA((2, 2)),
        ],
        compiler_params=pltpu.CompilerParams(
            collective_id=1, has_side_effects=True, vmem_limit_bytes=48 * 1024 * 1024
        ),
    )(a, w, share, c1, p)


def per_device(
    right_side,
    leaf_inverse,
    compress,
    middle,
    expand,
    row_project,
    row_expand,
    root_project,
    root_expand,
    owner_map,
):
    lowered = right_side.astype(jnp.bfloat16)
    columns = lowered.shape[1]
    root_term = lax.dot_general(
        root_project, lowered, contract_first, preferred_element_type=jnp.float32
    )
    level_coeffs = jnp.einsum(
        "blr,lw->brw", row_project, lowered, preferred_element_type=jnp.float32
    )
    dense_part = jnp.dot(leaf_inverse, lowered, preferred_element_type=jnp.float32)
    coeffs = lax.dot_general(
        compress, lowered, contract_first, preferred_element_type=jnp.float32
    ).astype(jnp.bfloat16)
    col_count = lax.axis_size("col")
    pieces = coeffs.reshape(col_count, -1, columns)
    chosen = (owner_map[:, None] == jnp.arange(col_count, dtype=owner_map.dtype)[None, :]).astype(
        jnp.bfloat16
    )
    outgoing = jnp.einsum(
        "kd,kxw->dxw", chosen, pieces, preferred_element_type=jnp.float32
    ).astype(jnp.bfloat16)
    root_shares = root_term.reshape(col_count, -1, columns)
    arrived, root_share, pair, far = scatter(outgoing, root_shares, level_coeffs)
    pair_sum = (level_coeffs[1] + pair[1]).astype(jnp.bfloat16)
    far_sum = far[0] + far[1]
    returned, root_full, quad_one, quad_two = gather(
        arrived.reshape(-1, columns), middle, root_share, pair_sum, far_sum, col_count,
        lax.axis_size("row"),
    )
    ordered = jnp.einsum(
        "jd,dxw->jxw", chosen, returned, preferred_element_type=jnp.float32
    ).astype(jnp.bfloat16).reshape(-1, columns)
    cluster_part = jnp.dot(expand, ordered, preferred_element_type=jnp.float32)

    sibling_sum = jnp.stack(
        [pair[0], quad_one.astype(jnp.float32), far_sum + quad_two], axis=0
    )
    root_sum = root_full.reshape(-1, columns)
    coupled = jnp.einsum(
        "blr,brw->lw",
        row_expand,
        sibling_sum.astype(jnp.bfloat16),
        preferred_element_type=jnp.float32,
    )
    root_part = jnp.dot(
        root_expand, root_sum.astype(jnp.bfloat16), preferred_element_type=jnp.float32
    )
    return dense_part + cluster_part + coupled + root_part


def solution(mesh):
    in_specs = (
        P(("row", "col"), None),
        P(("row", "col"), None),
        P(("row", "col"), None),
        P(("row", "col"), None),
        P(("row", "col"), None),
        P(None, ("row", "col"), None),
        P(None, ("row", "col"), None),
        P(("row", "col"), None),
        P(("row", "col"), None),
        P(),
    )
    out_specs = P(("row", "col"), None)
    return jax.shard_map(
        per_device, mesh=mesh, in_specs=in_specs, out_specs=out_specs, check_vma=False
    )
```

```python
import functools

import jax
import jax.numpy as jnp
from jax import lax
from jax.experimental import pallas as pl
from jax.experimental.pallas import tpu as pltpu
from jax.sharding import PartitionSpec as P

contract_first = (((0,), (0,)), ((), ()))
MESH_ID = pl.DeviceIdType.MESH


def swapped(x, axis, bit):
    return lax.ppermute(x, axis, [(i, i ^ 1 << bit) for i in range(lax.axis_size(axis))])


def flipped(index, bit):
    return index + bit - 2 * bit * lax.rem(index // bit, 2)


def col_peers(n):
    me = lax.axis_index("col")
    return [(s, lax.rem(me + s, n), lax.rem(me + n - s, n)) for s in range(1, n)]


def scatter_kernel(
    n, x_ref, r_ref, lv_ref, o_ref, share_ref, pair_ref, far_ref, got, sems, local_sems, pair_sems,
):
    me = lax.axis_index("col")
    row = lax.axis_index("row")
    width = x_ref.shape[1] // n
    barrier = pltpu.get_barrier_semaphore()
    for s, peer, _ in col_peers(n):
        pl.semaphore_signal(barrier, inc=1, device_id=(row, peer), device_id_type=MESH_ID)
    partner = flipped(row, 1)
    far = [flipped(row, 4), flipped(flipped(row, 4), 2)]
    for peer in [partner] + far:
        pl.semaphore_signal(barrier, inc=1, device_id=(peer, me), device_id_type=MESH_ID)
    pl.semaphore_wait(barrier, n + 2)

    low = pair_ref.shape[0]
    level_copies = [
        pltpu.make_async_remote_copy(
            src_ref=lv_ref.at[pl.ds(0, low)], dst_ref=pair_ref,
            send_sem=pair_sems.at[0, 0], recv_sem=pair_sems.at[1, 0],
            device_id=(partner, me), device_id_type=MESH_ID,
        )
    ]
    for i, peer in enumerate(far):
        level_copies.append(
            pltpu.make_async_remote_copy(
                src_ref=lv_ref.at[low], dst_ref=far_ref.at[i],
                send_sem=pair_sems.at[0, i + 1], recv_sem=pair_sems.at[1, i + 1],
                device_id=(peer, me), device_id_type=MESH_ID,
            )
        )
    for copy in level_copies:
        copy.start()
    local = pltpu.make_async_copy(
        x_ref.at[:, pl.ds(me * width, width)], o_ref.at[:, pl.ds(me * width, width)],
        local_sems.at[0],
    )
    local.start()
    own = pltpu.make_async_copy(r_ref.at[me], got.at[me], local_sems.at[1])
    own.start()

    def piece(s, peer, slot):
        return pltpu.make_async_remote_copy(
            src_ref=x_ref.at[:, pl.ds(peer * width, width)],
            dst_ref=o_ref.at[:, pl.ds(slot * width, width)],
            send_sem=sems.at[0, s], recv_sem=sems.at[1, s],
            device_id=(row, peer), device_id_type=MESH_ID,
        )

    def share(s, peer, slot):
        return pltpu.make_async_remote_copy(
            src_ref=r_ref.at[peer], dst_ref=got.at[slot],
            send_sem=sems.at[2, s], recv_sem=sems.at[3, s],
            device_id=(row, peer), device_id_type=MESH_ID,
        )

    for s, peer, _ in col_peers(n):
        share(s, peer, me).start()
        piece(s, peer, me).start()
    for s, peer, source in col_peers(n):
        share(s, peer, me).wait_send()
        share(s, source, source).wait_recv()
    own.wait()
    share_ref[...] = jnp.sum(got[...], axis=0)
    for s, peer, source in col_peers(n):
        piece(s, peer, me).wait_send()
        piece(s, source, source).wait_recv()
    local.wait()
    for copy in level_copies:
        copy.wait()


def scatter(x, r, lv):
    n = r.shape[0]
    return pl.pallas_call(
        functools.partial(scatter_kernel, n),
        out_shape=(
            jax.ShapeDtypeStruct(x.shape, x.dtype),
            jax.ShapeDtypeStruct(r.shape[1:], r.dtype),
            jax.ShapeDtypeStruct((lv.shape[0] - 1,) + lv.shape[1:], lv.dtype),
            jax.ShapeDtypeStruct((2,) + lv.shape[1:], lv.dtype),
        ),
        in_specs=[
            pl.BlockSpec(memory_space=pl.ANY),
            pl.BlockSpec(memory_space=pltpu.VMEM),
            pl.BlockSpec(memory_space=pl.ANY),
        ],
        out_specs=(
            pl.BlockSpec(memory_space=pl.ANY),
            pl.BlockSpec(memory_space=pltpu.VMEM),
            pl.BlockSpec(memory_space=pl.ANY),
            pl.BlockSpec(memory_space=pl.ANY),
        ),
        scratch_shapes=[
            pltpu.VMEM(r.shape, r.dtype),
            pltpu.SemaphoreType.DMA((4, n)),
            pltpu.SemaphoreType.DMA((2,)),
            pltpu.SemaphoreType.DMA((2, 3)),
        ],
        compiler_params=pltpu.CompilerParams(
            collective_id=0, has_side_effects=True, vmem_limit_bytes=4 * 1024 * 1024
        ),
    )(x, r, lv)


def gather_kernel(
    n, m, a_ref, w_ref, share_ref, c1_ref, p_ref, o_ref, full_ref, got1, got2,
    mixed, rows_got, total, rounded, sems, row_sems, local_sems, sib_sems,
):
    me = lax.axis_index("col")
    row = lax.axis_index("row")
    piece_rows = mixed.shape[1]
    row_peers = [(s, lax.rem(row + s, m), lax.rem(row + m - s, m)) for s in range(1, m)]
    barrier = pltpu.get_barrier_semaphore()
    for s, peer, _ in col_peers(n):
        pl.semaphore_signal(barrier, inc=1, device_id=(row, peer), device_id_type=MESH_ID)
    for s, peer, _ in row_peers:
        pl.semaphore_signal(barrier, inc=1, device_id=(peer, me), device_id_type=MESH_ID)
    pl.semaphore_wait(barrier, n - 1 + m - 1)

    own = pltpu.make_async_copy(share_ref, rows_got.at[row], local_sems.at[1])
    own.start()
    sends = [(c1_ref, got1, flipped(row, 2)), (p_ref, got2, flipped(row, 1))]
    sibs = []
    for i, (src_ref, dst_ref, peer) in enumerate(sends):
        sib = pltpu.make_async_remote_copy(
            src_ref=src_ref, dst_ref=dst_ref,
            send_sem=sib_sems.at[0, i], recv_sem=sib_sems.at[1, i],
            device_id=(peer, me), device_id_type=MESH_ID,
        )
        sib.start()
        sibs.append(sib)

    def part(s, peer, slot):
        return pltpu.make_async_remote_copy(
            src_ref=share_ref, dst_ref=rows_got.at[slot],
            send_sem=row_sems.at[0, s], recv_sem=row_sems.at[1, s],
            device_id=(peer, me), device_id_type=MESH_ID,
        )

    for s, peer, _ in row_peers:
        part(s, peer, row).start()

    def piece(s, peer, slot):
        return pltpu.make_async_remote_copy(
            src_ref=mixed.at[peer], dst_ref=o_ref.at[slot],
            send_sem=sems.at[0, s], recv_sem=sems.at[1, s],
            device_id=(row, peer), device_id_type=MESH_ID,
        )

    def compute(peer):
        first = pl.multiple_of(peer * piece_rows, piece_rows)
        mixed[peer] = lax.dot_general(
            w_ref[pl.ds(first, piece_rows), :], a_ref[...], (((1,), (1,)), ((), ())),
            preferred_element_type=jnp.float32,
        ).astype(mixed.dtype)

    def compute_and_send(s, carry):
        peer = lax.rem(me + s, n)
        compute(peer)
        piece(s, peer, me).start()
        return carry

    half = n // 2
    lax.fori_loop(1, half, compute_and_send, 0)

    def spread(s, peer, slot):
        return pltpu.make_async_remote_copy(
            src_ref=rounded, dst_ref=full_ref.at[slot],
            send_sem=sems.at[2, s], recv_sem=sems.at[3, s],
            device_id=(row, peer), device_id_type=MESH_ID,
        )

    for s, peer, source in row_peers:
        part(s, peer, row).wait_send()
        part(s, source, source).wait_recv()
    own.wait()
    total[...] = jnp.sum(rows_got[...], axis=0)
    rounded[...] = total[...].astype(rounded.dtype)
    mine = pltpu.make_async_copy(rounded, full_ref.at[me], local_sems.at[2])
    mine.start()
    for s, peer, _ in col_peers(n):
        spread(s, peer, me).start()

    lax.fori_loop(half, n, compute_and_send, 0)
    compute(me)
    local = pltpu.make_async_copy(mixed.at[me], o_ref.at[me], local_sems.at[0])
    local.start()

    for s, peer, source in col_peers(n):
        spread(s, peer, me).wait_send()
        spread(s, source, source).wait_recv()
        piece(s, peer, me).wait_send()
        piece(s, source, source).wait_recv()
    mine.wait()
    local.wait()
    for sib in sibs:
        sib.wait()


def gather(a, w, share, c1, p, n, m):
    piece_rows = w.shape[0] // n
    columns = a.shape[0]
    return pl.pallas_call(
        functools.partial(gather_kernel, n, m),
        out_shape=(
            jax.ShapeDtypeStruct((n, piece_rows, columns), a.dtype),
            jax.ShapeDtypeStruct((n,) + share.shape, jnp.bfloat16),
            jax.ShapeDtypeStruct(c1.shape, c1.dtype),
            jax.ShapeDtypeStruct(p.shape, p.dtype),
        ),
        in_specs=[
            pl.BlockSpec(memory_space=pltpu.VMEM),
            pl.BlockSpec(memory_space=pltpu.VMEM),
            pl.BlockSpec(memory_space=pltpu.VMEM),
            pl.BlockSpec(memory_space=pl.ANY),
            pl.BlockSpec(memory_space=pl.ANY),
        ],
        out_specs=(
            pl.BlockSpec(memory_space=pl.ANY),
            pl.BlockSpec(memory_space=pltpu.VMEM),
            pl.BlockSpec(memory_space=pl.ANY),
            pl.BlockSpec(memory_space=pl.ANY),
        ),
        scratch_shapes=[
            pltpu.VMEM((n, piece_rows, columns), a.dtype),
            pltpu.VMEM((m,) + share.shape, share.dtype),
            pltpu.VMEM(share.shape, share.dtype),
            pltpu.VMEM(share.shape, jnp.bfloat16),
            pltpu.SemaphoreType.DMA((4, n)),
            pltpu.SemaphoreType.DMA((2, m)),
            pltpu.SemaphoreType.DMA((3,)),
            pltpu.SemaphoreType.DMA((2, 2)),
        ],
        compiler_params=pltpu.CompilerParams(
            collective_id=1, has_side_effects=True, vmem_limit_bytes=48 * 1024 * 1024
        ),
    )(a, w, share, c1, p)


def per_device(
    right_side,
    leaf_inverse,
    compress,
    middle,
    expand,
    row_project,
    row_expand,
    root_project,
    root_expand,
    owner_map,
):
    lowered = right_side.astype(jnp.bfloat16)
    columns = lowered.shape[1]
    root_term = lax.dot_general(
        lowered, root_project, contract_first, preferred_element_type=jnp.float32
    )
    level_coeffs = jnp.einsum(
        "lw,blr->bwr", lowered, row_project, preferred_element_type=jnp.float32
    )
    dense_part = jnp.dot(leaf_inverse, lowered, preferred_element_type=jnp.float32)
    coeffs = lax.dot_general(
        lowered, compress, contract_first, preferred_element_type=jnp.float32
    ).astype(jnp.bfloat16)
    col_count = lax.axis_size("col")
    pieces = coeffs.reshape(columns, col_count, -1)
    chosen = (owner_map[:, None] == jnp.arange(col_count, dtype=owner_map.dtype)[None, :]).astype(
        jnp.bfloat16
    )
    outgoing = jnp.einsum(
        "kd,wkx->wdx", chosen, pieces, preferred_element_type=jnp.float32
    ).astype(jnp.bfloat16)
    root_shares = root_term.reshape(col_count, -1, root_term.shape[1])
    arrived, root_share, pair, far = scatter(
        outgoing.reshape(columns, -1), root_shares, level_coeffs
    )
    pair_sum = (level_coeffs[1] + pair[1]).astype(jnp.bfloat16)
    far_sum = far[0] + far[1]
    returned, root_full, quad_one, quad_two = gather(
        arrived, middle, root_share, pair_sum, far_sum, col_count,
        lax.axis_size("row"),
    )
    ordered = jnp.einsum(
        "jd,dxw->jxw", chosen, returned, preferred_element_type=jnp.float32
    ).astype(jnp.bfloat16).reshape(-1, columns)
    cluster_part = jnp.dot(expand, ordered, preferred_element_type=jnp.float32)

    sibling_sum = jnp.stack(
        [pair[0], quad_one.astype(jnp.float32), far_sum + quad_two], axis=0
    )
    root_coeffs = root_full.reshape(columns, -1)
    coupled = jnp.einsum(
        "blr,bwr->lw",
        row_expand,
        sibling_sum.astype(jnp.bfloat16),
        preferred_element_type=jnp.float32,
    )
    root_part = lax.dot_general(
        root_expand, root_coeffs, (((1,), (1,)), ((), ())), preferred_element_type=jnp.float32
    )
    return dense_part + cluster_part + coupled + root_part


def solution(mesh):
    in_specs = (
        P(("row", "col"), None),
        P(("row", "col"), None),
        P(("row", "col"), None),
        P(("row", "col"), None),
        P(("row", "col"), None),
        P(None, ("row", "col"), None),
        P(None, ("row", "col"), None),
        P(("row", "col"), None),
        P(("row", "col"), None),
        P(),
    )
    out_specs = P(("row", "col"), None)
    return jax.shard_map(
        per_device, mesh=mesh, in_specs=in_specs, out_specs=out_specs, check_vma=False
    )
```

```python
import functools

import jax
import jax.numpy as jnp
from jax import lax
from jax.experimental import pallas as pl
from jax.experimental.pallas import tpu as pltpu
from jax.sharding import PartitionSpec as P

contract_first = (((0,), (0,)), ((), ()))
MESH_ID = pl.DeviceIdType.MESH


def swapped(x, axis, bit):
    return lax.ppermute(x, axis, [(i, i ^ 1 << bit) for i in range(lax.axis_size(axis))])


def flipped(index, bit):
    return index + bit - 2 * bit * lax.rem(index // bit, 2)


def col_peers(n):
    me = lax.axis_index("col")
    return [(s, lax.rem(me + s, n), lax.rem(me + n - s, n)) for s in range(1, n)]


def scatter_kernel(
    n, x_ref, r_ref, lv_ref, e0_ref, o_ref, share_ref, pair_ref, far_ref, got, sems, local_sems, pair_sems,
):
    me = lax.axis_index("col")
    row = lax.axis_index("row")
    width = x_ref.shape[1] // n
    barrier = pltpu.get_barrier_semaphore()
    for s, peer, _ in col_peers(n):
        pl.semaphore_signal(barrier, inc=1, device_id=(row, peer), device_id_type=MESH_ID)
    partner = flipped(row, 1)
    far = [flipped(row, 4), flipped(flipped(row, 4), 2)]
    for peer in [partner] + far:
        pl.semaphore_signal(barrier, inc=1, device_id=(peer, me), device_id_type=MESH_ID)
    pl.semaphore_wait(barrier, n + 2)

    low = pair_ref.shape[0]
    level_copies = [
        pltpu.make_async_remote_copy(
            src_ref=lv_ref.at[pl.ds(0, low)], dst_ref=pair_ref,
            send_sem=pair_sems.at[0, 0], recv_sem=pair_sems.at[1, 0],
            device_id=(partner, me), device_id_type=MESH_ID,
        )
    ]
    for i, peer in enumerate(far):
        level_copies.append(
            pltpu.make_async_remote_copy(
                src_ref=lv_ref.at[low], dst_ref=far_ref.at[i],
                send_sem=pair_sems.at[0, i + 1], recv_sem=pair_sems.at[1, i + 1],
                device_id=(peer, me), device_id_type=MESH_ID,
            )
        )
    for copy in level_copies:
        copy.start()
    local = pltpu.make_async_copy(
        x_ref.at[:, pl.ds(me * width, width)], o_ref.at[:, pl.ds(me * width, width)],
        local_sems.at[0],
    )
    local.start()
    own = pltpu.make_async_copy(r_ref.at[me], got.at[me], local_sems.at[1])
    own.start()

    def piece(s, peer, slot):
        return pltpu.make_async_remote_copy(
            src_ref=x_ref.at[:, pl.ds(peer * width, width)],
            dst_ref=o_ref.at[:, pl.ds(slot * width, width)],
            send_sem=sems.at[0, s], recv_sem=sems.at[1, s],
            device_id=(row, peer), device_id_type=MESH_ID,
        )

    def share(s, peer, slot):
        return pltpu.make_async_remote_copy(
            src_ref=r_ref.at[peer], dst_ref=got.at[slot],
            send_sem=sems.at[2, s], recv_sem=sems.at[3, s],
            device_id=(row, peer), device_id_type=MESH_ID,
        )

    for s, peer, _ in col_peers(n):
        share(s, peer, me).start()
        piece(s, peer, me).start()
    for s, peer, source in col_peers(n):
        share(s, peer, me).wait_send()
        share(s, source, source).wait_recv()
    own.wait()
    share_ref[...] = jnp.sum(got[...], axis=0)
    for s, peer, source in col_peers(n):
        piece(s, peer, me).wait_send()
        piece(s, source, source).wait_recv()
    local.wait()
    for copy in level_copies:
        copy.wait()


def scatter(x, r, lv, staged):
    n = r.shape[0]
    return pl.pallas_call(
        functools.partial(scatter_kernel, n),
        out_shape=(
            jax.ShapeDtypeStruct(x.shape, x.dtype),
            jax.ShapeDtypeStruct(r.shape[1:], r.dtype),
            jax.ShapeDtypeStruct((lv.shape[0] - 1,) + lv.shape[1:], lv.dtype),
            jax.ShapeDtypeStruct((2,) + lv.shape[1:], lv.dtype),
        ),
        in_specs=[
            pl.BlockSpec(memory_space=pl.ANY),
            pl.BlockSpec(memory_space=pltpu.VMEM),
            pl.BlockSpec(memory_space=pl.ANY),
            pl.BlockSpec(memory_space=pltpu.VMEM),
        ],
        out_specs=(
            pl.BlockSpec(memory_space=pl.ANY),
            pl.BlockSpec(memory_space=pltpu.VMEM),
            pl.BlockSpec(memory_space=pl.ANY),
            pl.BlockSpec(memory_space=pl.ANY),
        ),
        scratch_shapes=[
            pltpu.VMEM(r.shape, r.dtype),
            pltpu.SemaphoreType.DMA((4, n)),
            pltpu.SemaphoreType.DMA((2,)),
            pltpu.SemaphoreType.DMA((2, 3)),
        ],
        compiler_params=pltpu.CompilerParams(
            collective_id=0, has_side_effects=True, vmem_limit_bytes=4 * 1024 * 1024
        ),
    )(x, r, lv, staged)


def gather_kernel(
    n, m, a_ref, w_ref, share_ref, c1_ref, p_ref, e2_ref, e3_ref, o_ref, full_ref, got1, got2,
    mixed, rows_got, total, rounded, sems, row_sems, local_sems, sib_sems,
):
    me = lax.axis_index("col")
    row = lax.axis_index("row")
    piece_rows = mixed.shape[1]
    row_peers = [(s, lax.rem(row + s, m), lax.rem(row + m - s, m)) for s in range(1, m)]
    barrier = pltpu.get_barrier_semaphore()
    for s, peer, _ in col_peers(n):
        pl.semaphore_signal(barrier, inc=1, device_id=(row, peer), device_id_type=MESH_ID)
    for s, peer, _ in row_peers:
        pl.semaphore_signal(barrier, inc=1, device_id=(peer, me), device_id_type=MESH_ID)
    pl.semaphore_wait(barrier, n - 1 + m - 1)

    own = pltpu.make_async_copy(share_ref, rows_got.at[row], local_sems.at[1])
    own.start()
    sends = [(c1_ref, got1, flipped(row, 2)), (p_ref, got2, flipped(row, 1))]
    sibs = []
    for i, (src_ref, dst_ref, peer) in enumerate(sends):
        sib = pltpu.make_async_remote_copy(
            src_ref=src_ref, dst_ref=dst_ref,
            send_sem=sib_sems.at[0, i], recv_sem=sib_sems.at[1, i],
            device_id=(peer, me), device_id_type=MESH_ID,
        )
        sib.start()
        sibs.append(sib)

    def part(s, peer, slot):
        return pltpu.make_async_remote_copy(
            src_ref=share_ref, dst_ref=rows_got.at[slot],
            send_sem=row_sems.at[0, s], recv_sem=row_sems.at[1, s],
            device_id=(peer, me), device_id_type=MESH_ID,
        )

    for s, peer, _ in row_peers:
        part(s, peer, row).start()

    def piece(s, peer, slot):
        return pltpu.make_async_remote_copy(
            src_ref=mixed.at[peer], dst_ref=o_ref.at[slot],
            send_sem=sems.at[0, s], recv_sem=sems.at[1, s],
            device_id=(row, peer), device_id_type=MESH_ID,
        )

    def compute(peer):
        first = pl.multiple_of(peer * piece_rows, piece_rows)
        mixed[peer] = lax.dot_general(
            w_ref[pl.ds(first, piece_rows), :], a_ref[...], (((1,), (1,)), ((), ())),
            preferred_element_type=jnp.float32,
        ).astype(mixed.dtype)

    def compute_and_send(s, carry):
        peer = lax.rem(me + s, n)
        compute(peer)
        piece(s, peer, me).start()
        return carry

    half = n // 2
    lax.fori_loop(1, half, compute_and_send, 0)

    def spread(s, peer, slot):
        return pltpu.make_async_remote_copy(
            src_ref=rounded, dst_ref=full_ref.at[slot],
            send_sem=sems.at[2, s], recv_sem=sems.at[3, s],
            device_id=(row, peer), device_id_type=MESH_ID,
        )

    for s, peer, source in row_peers:
        part(s, peer, row).wait_send()
        part(s, source, source).wait_recv()
    own.wait()
    total[...] = jnp.sum(rows_got[...], axis=0)
    rounded[...] = total[...].astype(rounded.dtype)
    mine = pltpu.make_async_copy(rounded, full_ref.at[me], local_sems.at[2])
    mine.start()
    for s, peer, _ in col_peers(n):
        spread(s, peer, me).start()

    lax.fori_loop(half, n, compute_and_send, 0)
    compute(me)
    local = pltpu.make_async_copy(mixed.at[me], o_ref.at[me], local_sems.at[0])
    local.start()

    for s, peer, source in col_peers(n):
        spread(s, peer, me).wait_send()
        spread(s, source, source).wait_recv()
        piece(s, peer, me).wait_send()
        piece(s, source, source).wait_recv()
    mine.wait()
    local.wait()
    for sib in sibs:
        sib.wait()


def gather(a, w, share, c1, p, staged, n, m):
    piece_rows = w.shape[0] // n
    columns = a.shape[0]
    return pl.pallas_call(
        functools.partial(gather_kernel, n, m),
        out_shape=(
            jax.ShapeDtypeStruct((n, piece_rows, columns), a.dtype),
            jax.ShapeDtypeStruct((n,) + share.shape, jnp.bfloat16),
            jax.ShapeDtypeStruct(c1.shape, c1.dtype),
            jax.ShapeDtypeStruct(p.shape, p.dtype),
        ),
        in_specs=[
            pl.BlockSpec(memory_space=pltpu.VMEM),
            pl.BlockSpec(memory_space=pltpu.VMEM),
            pl.BlockSpec(memory_space=pltpu.VMEM),
            pl.BlockSpec(memory_space=pl.ANY),
            pl.BlockSpec(memory_space=pl.ANY),
        ]
        + [pl.BlockSpec(memory_space=pltpu.VMEM)] * len(staged),
        out_specs=(
            pl.BlockSpec(memory_space=pl.ANY),
            pl.BlockSpec(memory_space=pltpu.VMEM),
            pl.BlockSpec(memory_space=pl.ANY),
            pl.BlockSpec(memory_space=pl.ANY),
        ),
        scratch_shapes=[
            pltpu.VMEM((n, piece_rows, columns), a.dtype),
            pltpu.VMEM((m,) + share.shape, share.dtype),
            pltpu.VMEM(share.shape, share.dtype),
            pltpu.VMEM(share.shape, jnp.bfloat16),
            pltpu.SemaphoreType.DMA((4, n)),
            pltpu.SemaphoreType.DMA((2, m)),
            pltpu.SemaphoreType.DMA((3,)),
            pltpu.SemaphoreType.DMA((2, 2)),
        ],
        compiler_params=pltpu.CompilerParams(
            collective_id=1, has_side_effects=True, vmem_limit_bytes=48 * 1024 * 1024
        ),
    )(a, w, share, c1, p, *staged)


def per_device(
    right_side,
    leaf_inverse,
    compress,
    middle,
    expand,
    row_project,
    row_expand,
    root_project,
    root_expand,
    owner_map,
):
    lowered = right_side.astype(jnp.bfloat16)
    columns = lowered.shape[1]
    root_term = lax.dot_general(
        lowered, root_project, contract_first, preferred_element_type=jnp.float32
    )
    level_coeffs = jnp.einsum(
        "lw,blr->bwr", lowered, row_project, preferred_element_type=jnp.float32
    )
    dense_part = jnp.dot(leaf_inverse, lowered, preferred_element_type=jnp.float32)
    coeffs = lax.dot_general(
        lowered, compress, contract_first, preferred_element_type=jnp.float32
    ).astype(jnp.bfloat16)
    col_count = lax.axis_size("col")
    pieces = coeffs.reshape(columns, col_count, -1)
    chosen = (owner_map[:, None] == jnp.arange(col_count, dtype=owner_map.dtype)[None, :]).astype(
        jnp.bfloat16
    )
    outgoing = jnp.einsum(
        "kd,wkx->wdx", chosen, pieces, preferred_element_type=jnp.float32
    ).astype(jnp.bfloat16)
    root_shares = root_term.reshape(col_count, -1, root_term.shape[1])
    arrived, root_share, pair, far = scatter(
        outgoing.reshape(columns, -1), root_shares, level_coeffs, expand
    )
    pair_sum = (level_coeffs[1] + pair[1]).astype(jnp.bfloat16)
    far_sum = far[0] + far[1]
    returned, root_full, quad_one, quad_two = gather(
        arrived, middle, root_share, pair_sum, far_sum, (row_expand, root_expand), col_count,
        lax.axis_size("row"),
    )
    ordered = jnp.einsum(
        "jd,dxw->jxw", chosen, returned, preferred_element_type=jnp.float32
    ).astype(jnp.bfloat16).reshape(-1, columns)
    cluster_part = jnp.dot(expand, ordered, preferred_element_type=jnp.float32)

    sibling_sum = jnp.stack(
        [pair[0], quad_one.astype(jnp.float32), far_sum + quad_two], axis=0
    )
    root_coeffs = root_full.reshape(columns, -1)
    coupled = jnp.einsum(
        "blr,bwr->lw",
        row_expand,
        sibling_sum.astype(jnp.bfloat16),
        preferred_element_type=jnp.float32,
    )
    root_part = lax.dot_general(
        root_expand, root_coeffs, (((1,), (1,)), ((), ())), preferred_element_type=jnp.float32
    )
    return dense_part + cluster_part + coupled + root_part


def solution(mesh):
    in_specs = (
        P(("row", "col"), None),
        P(("row", "col"), None),
        P(("row", "col"), None),
        P(("row", "col"), None),
        P(("row", "col"), None),
        P(None, ("row", "col"), None),
        P(None, ("row", "col"), None),
        P(("row", "col"), None),
        P(("row", "col"), None),
        P(),
    )
    out_specs = P(("row", "col"), None)
    return jax.shard_map(
        per_device, mesh=mesh, in_specs=in_specs, out_specs=out_specs, check_vma=False
    )
```

```python
import functools

import jax
import jax.numpy as jnp
from jax import lax
from jax.experimental import pallas as pl
from jax.experimental.pallas import tpu as pltpu
from jax.sharding import PartitionSpec as P

contract_first = (((0,), (0,)), ((), ()))
MESH_ID = pl.DeviceIdType.MESH


def swapped(x, axis, bit):
    return lax.ppermute(x, axis, [(i, i ^ 1 << bit) for i in range(lax.axis_size(axis))])


def flipped(index, bit):
    return index + bit - 2 * bit * lax.rem(index // bit, 2)


def col_peers(n):
    me = lax.axis_index("col")
    return [(s, lax.rem(me + s, n), lax.rem(me + n - s, n)) for s in range(1, n)]


def scatter_kernel(
    n, x_ref, r_ref, lv_ref, e0_ref, li_ref, y_ref, o_ref, share_ref, pair_ref, far_ref, d_ref,
    got, sems, local_sems, pair_sems,
):
    me = lax.axis_index("col")
    row = lax.axis_index("row")
    width = x_ref.shape[1] // n
    barrier = pltpu.get_barrier_semaphore()
    for s, peer, _ in col_peers(n):
        pl.semaphore_signal(barrier, inc=1, device_id=(row, peer), device_id_type=MESH_ID)
    partner = flipped(row, 1)
    far = [flipped(row, 4), flipped(flipped(row, 4), 2)]
    for peer in [partner] + far:
        pl.semaphore_signal(barrier, inc=1, device_id=(peer, me), device_id_type=MESH_ID)
    pl.semaphore_wait(barrier, n + 2)

    low = pair_ref.shape[0]
    level_copies = [
        pltpu.make_async_remote_copy(
            src_ref=lv_ref.at[pl.ds(0, low)], dst_ref=pair_ref,
            send_sem=pair_sems.at[0, 0], recv_sem=pair_sems.at[1, 0],
            device_id=(partner, me), device_id_type=MESH_ID,
        )
    ]
    for i, peer in enumerate(far):
        level_copies.append(
            pltpu.make_async_remote_copy(
                src_ref=lv_ref.at[low], dst_ref=far_ref.at[i],
                send_sem=pair_sems.at[0, i + 1], recv_sem=pair_sems.at[1, i + 1],
                device_id=(peer, me), device_id_type=MESH_ID,
            )
        )
    for copy in level_copies:
        copy.start()
    local = pltpu.make_async_copy(
        x_ref.at[:, pl.ds(me * width, width)], o_ref.at[:, pl.ds(me * width, width)],
        local_sems.at[0],
    )
    local.start()
    own = pltpu.make_async_copy(r_ref.at[me], got.at[me], local_sems.at[1])
    own.start()

    def piece(s, peer, slot):
        return pltpu.make_async_remote_copy(
            src_ref=x_ref.at[:, pl.ds(peer * width, width)],
            dst_ref=o_ref.at[:, pl.ds(slot * width, width)],
            send_sem=sems.at[0, s], recv_sem=sems.at[1, s],
            device_id=(row, peer), device_id_type=MESH_ID,
        )

    def share(s, peer, slot):
        return pltpu.make_async_remote_copy(
            src_ref=r_ref.at[peer], dst_ref=got.at[slot],
            send_sem=sems.at[2, s], recv_sem=sems.at[3, s],
            device_id=(row, peer), device_id_type=MESH_ID,
        )

    for s, peer, _ in col_peers(n):
        share(s, peer, me).start()
        piece(s, peer, me).start()
    d_ref[...] = jnp.dot(li_ref[...], y_ref[...], preferred_element_type=jnp.float32)
    for s, peer, source in col_peers(n):
        share(s, peer, me).wait_send()
        share(s, source, source).wait_recv()
    own.wait()
    share_ref[...] = jnp.sum(got[...], axis=0)
    for s, peer, source in col_peers(n):
        piece(s, peer, me).wait_send()
        piece(s, source, source).wait_recv()
    local.wait()
    for copy in level_copies:
        copy.wait()


def scatter(x, r, lv, staged, li, y):
    n = r.shape[0]
    return pl.pallas_call(
        functools.partial(scatter_kernel, n),
        out_shape=(
            jax.ShapeDtypeStruct(x.shape, x.dtype),
            jax.ShapeDtypeStruct(r.shape[1:], r.dtype),
            jax.ShapeDtypeStruct((lv.shape[0] - 1,) + lv.shape[1:], lv.dtype),
            jax.ShapeDtypeStruct((2,) + lv.shape[1:], lv.dtype),
            jax.ShapeDtypeStruct((li.shape[0], y.shape[1]), jnp.float32),
        ),
        in_specs=[
            pl.BlockSpec(memory_space=pl.ANY),
            pl.BlockSpec(memory_space=pltpu.VMEM),
            pl.BlockSpec(memory_space=pl.ANY),
            pl.BlockSpec(memory_space=pltpu.VMEM),
            pl.BlockSpec(memory_space=pltpu.VMEM),
            pl.BlockSpec(memory_space=pltpu.VMEM),
        ],
        out_specs=(
            pl.BlockSpec(memory_space=pl.ANY),
            pl.BlockSpec(memory_space=pltpu.VMEM),
            pl.BlockSpec(memory_space=pl.ANY),
            pl.BlockSpec(memory_space=pl.ANY),
            pl.BlockSpec(memory_space=pltpu.VMEM),
        ),
        scratch_shapes=[
            pltpu.VMEM(r.shape, r.dtype),
            pltpu.SemaphoreType.DMA((4, n)),
            pltpu.SemaphoreType.DMA((2,)),
            pltpu.SemaphoreType.DMA((2, 3)),
        ],
        compiler_params=pltpu.CompilerParams(
            collective_id=0, has_side_effects=True, vmem_limit_bytes=4 * 1024 * 1024
        ),
    )(x, r, lv, staged, li, y)


def gather_kernel(
    n, m, a_ref, w_ref, share_ref, c1_ref, p_ref, e2_ref, e3_ref, o_ref, full_ref, got1, got2,
    mixed, rows_got, total, rounded, sems, row_sems, local_sems, sib_sems,
):
    me = lax.axis_index("col")
    row = lax.axis_index("row")
    piece_rows = mixed.shape[1]
    row_peers = [(s, lax.rem(row + s, m), lax.rem(row + m - s, m)) for s in range(1, m)]
    barrier = pltpu.get_barrier_semaphore()
    for s, peer, _ in col_peers(n):
        pl.semaphore_signal(barrier, inc=1, device_id=(row, peer), device_id_type=MESH_ID)
    for s, peer, _ in row_peers:
        pl.semaphore_signal(barrier, inc=1, device_id=(peer, me), device_id_type=MESH_ID)
    pl.semaphore_wait(barrier, n - 1 + m - 1)

    own = pltpu.make_async_copy(share_ref, rows_got.at[row], local_sems.at[1])
    own.start()
    sends = [(c1_ref, got1, flipped(row, 2)), (p_ref, got2, flipped(row, 1))]
    sibs = []
    for i, (src_ref, dst_ref, peer) in enumerate(sends):
        sib = pltpu.make_async_remote_copy(
            src_ref=src_ref, dst_ref=dst_ref,
            send_sem=sib_sems.at[0, i], recv_sem=sib_sems.at[1, i],
            device_id=(peer, me), device_id_type=MESH_ID,
        )
        sib.start()
        sibs.append(sib)

    def part(s, peer, slot):
        return pltpu.make_async_remote_copy(
            src_ref=share_ref, dst_ref=rows_got.at[slot],
            send_sem=row_sems.at[0, s], recv_sem=row_sems.at[1, s],
            device_id=(peer, me), device_id_type=MESH_ID,
        )

    for s, peer, _ in row_peers:
        part(s, peer, row).start()

    def piece(s, peer, slot):
        return pltpu.make_async_remote_copy(
            src_ref=mixed.at[peer], dst_ref=o_ref.at[slot],
            send_sem=sems.at[0, s], recv_sem=sems.at[1, s],
            device_id=(row, peer), device_id_type=MESH_ID,
        )

    def compute(peer):
        first = pl.multiple_of(peer * piece_rows, piece_rows)
        mixed[peer] = lax.dot_general(
            w_ref[pl.ds(first, piece_rows), :], a_ref[...], (((1,), (1,)), ((), ())),
            preferred_element_type=jnp.float32,
        ).astype(mixed.dtype)

    def compute_and_send(s, carry):
        peer = lax.rem(me + s, n)
        compute(peer)
        piece(s, peer, me).start()
        return carry

    half = n // 2
    lax.fori_loop(1, half, compute_and_send, 0)

    def spread(s, peer, slot):
        return pltpu.make_async_remote_copy(
            src_ref=rounded, dst_ref=full_ref.at[slot],
            send_sem=sems.at[2, s], recv_sem=sems.at[3, s],
            device_id=(row, peer), device_id_type=MESH_ID,
        )

    for s, peer, source in row_peers:
        part(s, peer, row).wait_send()
        part(s, source, source).wait_recv()
    own.wait()
    total[...] = jnp.sum(rows_got[...], axis=0)
    rounded[...] = total[...].astype(rounded.dtype)
    mine = pltpu.make_async_copy(rounded, full_ref.at[me], local_sems.at[2])
    mine.start()
    for s, peer, _ in col_peers(n):
        spread(s, peer, me).start()

    lax.fori_loop(half, n, compute_and_send, 0)
    compute(me)
    local = pltpu.make_async_copy(mixed.at[me], o_ref.at[me], local_sems.at[0])
    local.start()

    for s, peer, source in col_peers(n):
        spread(s, peer, me).wait_send()
        spread(s, source, source).wait_recv()
        piece(s, peer, me).wait_send()
        piece(s, source, source).wait_recv()
    mine.wait()
    local.wait()
    for sib in sibs:
        sib.wait()


def gather(a, w, share, c1, p, staged, n, m):
    piece_rows = w.shape[0] // n
    columns = a.shape[0]
    return pl.pallas_call(
        functools.partial(gather_kernel, n, m),
        out_shape=(
            jax.ShapeDtypeStruct((n, piece_rows, columns), a.dtype),
            jax.ShapeDtypeStruct((n,) + share.shape, jnp.bfloat16),
            jax.ShapeDtypeStruct(c1.shape, c1.dtype),
            jax.ShapeDtypeStruct(p.shape, p.dtype),
        ),
        in_specs=[
            pl.BlockSpec(memory_space=pltpu.VMEM),
            pl.BlockSpec(memory_space=pltpu.VMEM),
            pl.BlockSpec(memory_space=pltpu.VMEM),
            pl.BlockSpec(memory_space=pl.ANY),
            pl.BlockSpec(memory_space=pl.ANY),
        ]
        + [pl.BlockSpec(memory_space=pltpu.VMEM)] * len(staged),
        out_specs=(
            pl.BlockSpec(memory_space=pl.ANY),
            pl.BlockSpec(memory_space=pltpu.VMEM),
            pl.BlockSpec(memory_space=pl.ANY),
            pl.BlockSpec(memory_space=pl.ANY),
        ),
        scratch_shapes=[
            pltpu.VMEM((n, piece_rows, columns), a.dtype),
            pltpu.VMEM((m,) + share.shape, share.dtype),
            pltpu.VMEM(share.shape, share.dtype),
            pltpu.VMEM(share.shape, jnp.bfloat16),
            pltpu.SemaphoreType.DMA((4, n)),
            pltpu.SemaphoreType.DMA((2, m)),
            pltpu.SemaphoreType.DMA((3,)),
            pltpu.SemaphoreType.DMA((2, 2)),
        ],
        compiler_params=pltpu.CompilerParams(
            collective_id=1, has_side_effects=True, vmem_limit_bytes=48 * 1024 * 1024
        ),
    )(a, w, share, c1, p, *staged)


def per_device(
    right_side,
    leaf_inverse,
    compress,
    middle,
    expand,
    row_project,
    row_expand,
    root_project,
    root_expand,
    owner_map,
):
    lowered = right_side.astype(jnp.bfloat16)
    columns = lowered.shape[1]
    root_term = lax.dot_general(
        lowered, root_project, contract_first, preferred_element_type=jnp.float32
    )
    level_coeffs = jnp.einsum(
        "lw,blr->bwr", lowered, row_project, preferred_element_type=jnp.float32
    )
    coeffs = lax.dot_general(
        lowered, compress, contract_first, preferred_element_type=jnp.float32
    ).astype(jnp.bfloat16)
    col_count = lax.axis_size("col")
    pieces = coeffs.reshape(columns, col_count, -1)
    chosen = (owner_map[:, None] == jnp.arange(col_count, dtype=owner_map.dtype)[None, :]).astype(
        jnp.bfloat16
    )
    outgoing = jnp.einsum(
        "kd,wkx->wdx", chosen, pieces, preferred_element_type=jnp.float32
    ).astype(jnp.bfloat16)
    root_shares = root_term.reshape(col_count, -1, root_term.shape[1])
    arrived, root_share, pair, far, dense_part = scatter(
        outgoing.reshape(columns, -1), root_shares, level_coeffs, expand, leaf_inverse, lowered
    )
    pair_sum = (level_coeffs[1] + pair[1]).astype(jnp.bfloat16)
    far_sum = far[0] + far[1]
    returned, root_full, quad_one, quad_two = gather(
        arrived, middle, root_share, pair_sum, far_sum, (row_expand, root_expand), col_count,
        lax.axis_size("row"),
    )
    ordered = jnp.einsum(
        "jd,dxw->jxw", chosen, returned, preferred_element_type=jnp.float32
    ).astype(jnp.bfloat16).reshape(-1, columns)
    cluster_part = jnp.dot(expand, ordered, preferred_element_type=jnp.float32)

    sibling_sum = jnp.stack(
        [pair[0], quad_one.astype(jnp.float32), far_sum + quad_two], axis=0
    )
    root_coeffs = root_full.reshape(columns, -1)
    coupled = jnp.einsum(
        "blr,bwr->lw",
        row_expand,
        sibling_sum.astype(jnp.bfloat16),
        preferred_element_type=jnp.float32,
    )
    root_part = lax.dot_general(
        root_expand, root_coeffs, (((1,), (1,)), ((), ())), preferred_element_type=jnp.float32
    )
    return dense_part + cluster_part + coupled + root_part


def solution(mesh):
    in_specs = (
        P(("row", "col"), None),
        P(("row", "col"), None),
        P(("row", "col"), None),
        P(("row", "col"), None),
        P(("row", "col"), None),
        P(None, ("row", "col"), None),
        P(None, ("row", "col"), None),
        P(("row", "col"), None),
        P(("row", "col"), None),
        P(),
    )
    out_specs = P(("row", "col"), None)
    return jax.shard_map(
        per_device, mesh=mesh, in_specs=in_specs, out_specs=out_specs, check_vma=False
    )
```

```python
import functools

import jax
import jax.numpy as jnp
from jax import lax
from jax.experimental import pallas as pl
from jax.experimental.pallas import tpu as pltpu
from jax.sharding import PartitionSpec as P

contract_first = (((0,), (0,)), ((), ()))
MESH_ID = pl.DeviceIdType.MESH


def swapped(x, axis, bit):
    return lax.ppermute(x, axis, [(i, i ^ 1 << bit) for i in range(lax.axis_size(axis))])


def flipped(index, bit):
    return index + bit - 2 * bit * lax.rem(index // bit, 2)


def col_peers(n):
    me = lax.axis_index("col")
    return [(s, lax.rem(me + s, n), lax.rem(me + n - s, n)) for s in range(1, n)]


def scatter_kernel(
    n, x_ref, r_ref, lv_ref, e0_ref, li_ref, y_ref, o_ref, share_ref, pair_ref, far_ref, d_ref,
    got, sems, local_sems, pair_sems,
):
    me = lax.axis_index("col")
    row = lax.axis_index("row")
    width = x_ref.shape[1] // n
    barrier = pltpu.get_barrier_semaphore()
    for s, peer, _ in col_peers(n):
        pl.semaphore_signal(barrier, inc=1, device_id=(row, peer), device_id_type=MESH_ID)
    partner = flipped(row, 1)
    far = [flipped(row, 4), flipped(flipped(row, 4), 2)]
    for peer in [partner] + far:
        pl.semaphore_signal(barrier, inc=1, device_id=(peer, me), device_id_type=MESH_ID)
    pl.semaphore_wait(barrier, n + 2)

    low = pair_ref.shape[0]
    level_copies = [
        pltpu.make_async_remote_copy(
            src_ref=lv_ref.at[pl.ds(0, low)], dst_ref=pair_ref,
            send_sem=pair_sems.at[0, 0], recv_sem=pair_sems.at[1, 0],
            device_id=(partner, me), device_id_type=MESH_ID,
        )
    ]
    for i, peer in enumerate(far):
        level_copies.append(
            pltpu.make_async_remote_copy(
                src_ref=lv_ref.at[low], dst_ref=far_ref.at[i],
                send_sem=pair_sems.at[0, i + 1], recv_sem=pair_sems.at[1, i + 1],
                device_id=(peer, me), device_id_type=MESH_ID,
            )
        )
    for copy in level_copies:
        copy.start()
    local = pltpu.make_async_copy(
        x_ref.at[:, pl.ds(me * width, width)], o_ref.at[:, pl.ds(me * width, width)],
        local_sems.at[0],
    )
    local.start()
    own = pltpu.make_async_copy(r_ref.at[me], got.at[me], local_sems.at[1])
    own.start()

    def piece(s, peer, slot):
        return pltpu.make_async_remote_copy(
            src_ref=x_ref.at[:, pl.ds(peer * width, width)],
            dst_ref=o_ref.at[:, pl.ds(slot * width, width)],
            send_sem=sems.at[0, s], recv_sem=sems.at[1, s],
            device_id=(row, peer), device_id_type=MESH_ID,
        )

    def share(s, peer, slot):
        return pltpu.make_async_remote_copy(
            src_ref=r_ref.at[peer], dst_ref=got.at[slot],
            send_sem=sems.at[2, s], recv_sem=sems.at[3, s],
            device_id=(row, peer), device_id_type=MESH_ID,
        )

    for s, peer, _ in col_peers(n):
        share(s, peer, me).start()
        piece(s, peer, me).start()
    d_ref[...] = jnp.dot(li_ref[...], y_ref[...], preferred_element_type=jnp.float32)
    for s, peer, source in col_peers(n):
        share(s, peer, me).wait_send()
        share(s, source, source).wait_recv()
    own.wait()
    share_ref[...] = jnp.sum(got[...], axis=0)
    for s, peer, source in col_peers(n):
        piece(s, peer, me).wait_send()
        piece(s, source, source).wait_recv()
    local.wait()
    for copy in level_copies:
        copy.wait()


def scatter(x, r, lv, staged, li, y):
    n = r.shape[0]
    return pl.pallas_call(
        functools.partial(scatter_kernel, n),
        out_shape=(
            jax.ShapeDtypeStruct(x.shape, x.dtype),
            jax.ShapeDtypeStruct(r.shape[1:], r.dtype),
            jax.ShapeDtypeStruct((lv.shape[0] - 1,) + lv.shape[1:], lv.dtype),
            jax.ShapeDtypeStruct((2,) + lv.shape[1:], lv.dtype),
            jax.ShapeDtypeStruct((li.shape[0], y.shape[1]), jnp.float32),
        ),
        in_specs=[
            pl.BlockSpec(memory_space=pl.ANY),
            pl.BlockSpec(memory_space=pltpu.VMEM),
            pl.BlockSpec(memory_space=pl.ANY),
            pl.BlockSpec(memory_space=pltpu.VMEM),
            pl.BlockSpec(memory_space=pltpu.VMEM),
            pl.BlockSpec(memory_space=pltpu.VMEM),
        ],
        out_specs=(
            pl.BlockSpec(memory_space=pl.ANY),
            pl.BlockSpec(memory_space=pltpu.VMEM),
            pl.BlockSpec(memory_space=pl.ANY),
            pl.BlockSpec(memory_space=pl.ANY),
            pl.BlockSpec(memory_space=pltpu.VMEM),
        ),
        scratch_shapes=[
            pltpu.VMEM(r.shape, r.dtype),
            pltpu.SemaphoreType.DMA((4, n)),
            pltpu.SemaphoreType.DMA((2,)),
            pltpu.SemaphoreType.DMA((2, 3)),
        ],
        compiler_params=pltpu.CompilerParams(
            collective_id=0, has_side_effects=True, vmem_limit_bytes=4 * 1024 * 1024
        ),
    )(x, r, lv, staged, li, y)


def gather_kernel(
    n, m, a_ref, w_ref, share_ref, c1_ref, p_ref, s0_ref, e2_ref, e3_ref, o_ref, full_ref, got1, got2,
    cpl_ref,
    mixed, rows_got, total, rounded, sems, row_sems, local_sems, sib_sems,
):
    me = lax.axis_index("col")
    row = lax.axis_index("row")
    piece_rows = mixed.shape[1]
    row_peers = [(s, lax.rem(row + s, m), lax.rem(row + m - s, m)) for s in range(1, m)]
    barrier = pltpu.get_barrier_semaphore()
    for s, peer, _ in col_peers(n):
        pl.semaphore_signal(barrier, inc=1, device_id=(row, peer), device_id_type=MESH_ID)
    for s, peer, _ in row_peers:
        pl.semaphore_signal(barrier, inc=1, device_id=(peer, me), device_id_type=MESH_ID)
    pl.semaphore_wait(barrier, n - 1 + m - 1)

    own = pltpu.make_async_copy(share_ref, rows_got.at[row], local_sems.at[1])
    own.start()
    sends = [(c1_ref, got1, flipped(row, 2)), (p_ref, got2, flipped(row, 1))]
    sibs = []
    for i, (src_ref, dst_ref, peer) in enumerate(sends):
        sib = pltpu.make_async_remote_copy(
            src_ref=src_ref, dst_ref=dst_ref,
            send_sem=sib_sems.at[0, i], recv_sem=sib_sems.at[1, i],
            device_id=(peer, me), device_id_type=MESH_ID,
        )
        sib.start()
        sibs.append(sib)

    def part(s, peer, slot):
        return pltpu.make_async_remote_copy(
            src_ref=share_ref, dst_ref=rows_got.at[slot],
            send_sem=row_sems.at[0, s], recv_sem=row_sems.at[1, s],
            device_id=(peer, me), device_id_type=MESH_ID,
        )

    for s, peer, _ in row_peers:
        part(s, peer, row).start()

    def piece(s, peer, slot):
        return pltpu.make_async_remote_copy(
            src_ref=mixed.at[peer], dst_ref=o_ref.at[slot],
            send_sem=sems.at[0, s], recv_sem=sems.at[1, s],
            device_id=(row, peer), device_id_type=MESH_ID,
        )

    def compute(peer):
        first = pl.multiple_of(peer * piece_rows, piece_rows)
        mixed[peer] = lax.dot_general(
            w_ref[pl.ds(first, piece_rows), :], a_ref[...], (((1,), (1,)), ((), ())),
            preferred_element_type=jnp.float32,
        ).astype(mixed.dtype)

    def compute_and_send(s, carry):
        peer = lax.rem(me + s, n)
        compute(peer)
        piece(s, peer, me).start()
        return carry

    half = n // 2
    lax.fori_loop(1, half, compute_and_send, 0)

    def spread(s, peer, slot):
        return pltpu.make_async_remote_copy(
            src_ref=rounded, dst_ref=full_ref.at[slot],
            send_sem=sems.at[2, s], recv_sem=sems.at[3, s],
            device_id=(row, peer), device_id_type=MESH_ID,
        )

    for s, peer, source in row_peers:
        part(s, peer, row).wait_send()
        part(s, source, source).wait_recv()
    own.wait()
    total[...] = jnp.sum(rows_got[...], axis=0)
    rounded[...] = total[...].astype(rounded.dtype)
    mine = pltpu.make_async_copy(rounded, full_ref.at[me], local_sems.at[2])
    mine.start()
    for s, peer, _ in col_peers(n):
        spread(s, peer, me).start()

    lax.fori_loop(half, n, compute_and_send, 0)
    compute(me)
    local = pltpu.make_async_copy(mixed.at[me], o_ref.at[me], local_sems.at[0])
    local.start()

    sibs[0].wait()
    cpl_ref[...] = lax.dot_general(
        e2_ref[0], s0_ref[...], (((1,), (1,)), ((), ())), preferred_element_type=jnp.float32
    ) + lax.dot_general(
        e2_ref[1], got1[...], (((1,), (1,)), ((), ())), preferred_element_type=jnp.float32
    )
    for s, peer, source in col_peers(n):
        spread(s, peer, me).wait_send()
        spread(s, source, source).wait_recv()
        piece(s, peer, me).wait_send()
        piece(s, source, source).wait_recv()
    mine.wait()
    local.wait()
    sibs[1].wait()


def gather(a, w, share, c1, p, s0, staged, n, m):
    piece_rows = w.shape[0] // n
    columns = a.shape[0]
    return pl.pallas_call(
        functools.partial(gather_kernel, n, m),
        out_shape=(
            jax.ShapeDtypeStruct((n, piece_rows, columns), a.dtype),
            jax.ShapeDtypeStruct((n,) + share.shape, jnp.bfloat16),
            jax.ShapeDtypeStruct(c1.shape, c1.dtype),
            jax.ShapeDtypeStruct(p.shape, p.dtype),
            jax.ShapeDtypeStruct((staged[0].shape[1], a.shape[0]), jnp.float32),
        ),
        in_specs=[
            pl.BlockSpec(memory_space=pltpu.VMEM),
            pl.BlockSpec(memory_space=pltpu.VMEM),
            pl.BlockSpec(memory_space=pltpu.VMEM),
            pl.BlockSpec(memory_space=pltpu.VMEM),
            pl.BlockSpec(memory_space=pl.ANY),
            pl.BlockSpec(memory_space=pltpu.VMEM),
        ]
        + [pl.BlockSpec(memory_space=pltpu.VMEM)] * len(staged),
        out_specs=(
            pl.BlockSpec(memory_space=pl.ANY),
            pl.BlockSpec(memory_space=pltpu.VMEM),
            pl.BlockSpec(memory_space=pltpu.VMEM),
            pl.BlockSpec(memory_space=pl.ANY),
            pl.BlockSpec(memory_space=pltpu.VMEM),
        ),
        scratch_shapes=[
            pltpu.VMEM((n, piece_rows, columns), a.dtype),
            pltpu.VMEM((m,) + share.shape, share.dtype),
            pltpu.VMEM(share.shape, share.dtype),
            pltpu.VMEM(share.shape, jnp.bfloat16),
            pltpu.SemaphoreType.DMA((4, n)),
            pltpu.SemaphoreType.DMA((2, m)),
            pltpu.SemaphoreType.DMA((3,)),
            pltpu.SemaphoreType.DMA((2, 2)),
        ],
        compiler_params=pltpu.CompilerParams(
            collective_id=1, has_side_effects=True, vmem_limit_bytes=48 * 1024 * 1024
        ),
    )(a, w, share, c1, p, s0, *staged)


def per_device(
    right_side,
    leaf_inverse,
    compress,
    middle,
    expand,
    row_project,
    row_expand,
    root_project,
    root_expand,
    owner_map,
):
    lowered = right_side.astype(jnp.bfloat16)
    columns = lowered.shape[1]
    root_term = lax.dot_general(
        lowered, root_project, contract_first, preferred_element_type=jnp.float32
    )
    level_coeffs = jnp.einsum(
        "lw,blr->bwr", lowered, row_project, preferred_element_type=jnp.float32
    )
    coeffs = lax.dot_general(
        lowered, compress, contract_first, preferred_element_type=jnp.float32
    ).astype(jnp.bfloat16)
    col_count = lax.axis_size("col")
    pieces = coeffs.reshape(columns, col_count, -1)
    chosen = (owner_map[:, None] == jnp.arange(col_count, dtype=owner_map.dtype)[None, :]).astype(
        jnp.bfloat16
    )
    outgoing = jnp.einsum(
        "kd,wkx->wdx", chosen, pieces, preferred_element_type=jnp.float32
    ).astype(jnp.bfloat16)
    root_shares = root_term.reshape(col_count, -1, root_term.shape[1])
    arrived, root_share, pair, far, dense_part = scatter(
        outgoing.reshape(columns, -1), root_shares, level_coeffs, expand, leaf_inverse, lowered
    )
    pair_sum = (level_coeffs[1] + pair[1]).astype(jnp.bfloat16)
    far_sum = far[0] + far[1]
    returned, root_full, quad_one, quad_two, near_coupled = gather(
        arrived, middle, root_share, pair_sum, far_sum, pair[0].astype(jnp.bfloat16),
        (row_expand, root_expand), col_count,
        lax.axis_size("row"),
    )
    ordered = jnp.einsum(
        "jd,dxw->jxw", chosen, returned, preferred_element_type=jnp.float32
    ).astype(jnp.bfloat16).reshape(-1, columns)
    cluster_part = jnp.dot(expand, ordered, preferred_element_type=jnp.float32)

    root_coeffs = root_full.reshape(columns, -1)
    coupled = near_coupled + lax.dot_general(
        row_expand[2],
        (far_sum + quad_two).astype(jnp.bfloat16),
        (((1,), (1,)), ((), ())),
        preferred_element_type=jnp.float32,
    )
    root_part = lax.dot_general(
        root_expand, root_coeffs, (((1,), (1,)), ((), ())), preferred_element_type=jnp.float32
    )
    return dense_part + cluster_part + coupled + root_part


def solution(mesh):
    in_specs = (
        P(("row", "col"), None),
        P(("row", "col"), None),
        P(("row", "col"), None),
        P(("row", "col"), None),
        P(("row", "col"), None),
        P(None, ("row", "col"), None),
        P(None, ("row", "col"), None),
        P(("row", "col"), None),
        P(("row", "col"), None),
        P(),
    )
    out_specs = P(("row", "col"), None)
    return jax.shard_map(
        per_device, mesh=mesh, in_specs=in_specs, out_specs=out_specs, check_vma=False
    )
```

```python
import functools

import jax
import jax.numpy as jnp
from jax import lax
from jax.experimental import pallas as pl
from jax.experimental.pallas import tpu as pltpu
from jax.sharding import PartitionSpec as P

contract_first = (((0,), (0,)), ((), ()))
MESH_ID = pl.DeviceIdType.MESH


def swapped(x, axis, bit):
    return lax.ppermute(x, axis, [(i, i ^ 1 << bit) for i in range(lax.axis_size(axis))])


def flipped(index, bit):
    return index + bit - 2 * bit * lax.rem(index // bit, 2)


def col_peers(n):
    me = lax.axis_index("col")
    return [(s, lax.rem(me + s, n), lax.rem(me + n - s, n)) for s in range(1, n)]


def scatter_kernel(
    n, x_ref, r_ref, lv_ref, e0_ref, li_ref, y_ref, o_ref, share_ref, pair_ref, far_ref, d_ref,
    got, sems, local_sems, pair_sems,
):
    me = lax.axis_index("col")
    row = lax.axis_index("row")
    width = x_ref.shape[1] // n
    barrier = pltpu.get_barrier_semaphore()
    for s, peer, _ in col_peers(n):
        pl.semaphore_signal(barrier, inc=1, device_id=(row, peer), device_id_type=MESH_ID)
    partner = flipped(row, 1)
    far = [flipped(row, 4), flipped(flipped(row, 4), 2)]
    for peer in [partner] + far:
        pl.semaphore_signal(barrier, inc=1, device_id=(peer, me), device_id_type=MESH_ID)
    pl.semaphore_wait(barrier, n + 2)

    low = pair_ref.shape[0]
    level_copies = [
        pltpu.make_async_remote_copy(
            src_ref=lv_ref.at[pl.ds(0, low)], dst_ref=pair_ref,
            send_sem=pair_sems.at[0, 0], recv_sem=pair_sems.at[1, 0],
            device_id=(partner, me), device_id_type=MESH_ID,
        )
    ]
    for i, peer in enumerate(far):
        level_copies.append(
            pltpu.make_async_remote_copy(
                src_ref=lv_ref.at[low], dst_ref=far_ref.at[i],
                send_sem=pair_sems.at[0, i + 1], recv_sem=pair_sems.at[1, i + 1],
                device_id=(peer, me), device_id_type=MESH_ID,
            )
        )
    for copy in level_copies:
        copy.start()
    local = pltpu.make_async_copy(
        x_ref.at[:, pl.ds(me * width, width)], o_ref.at[:, pl.ds(me * width, width)],
        local_sems.at[0],
    )
    local.start()
    own = pltpu.make_async_copy(r_ref.at[me], got.at[me], local_sems.at[1])
    own.start()

    def piece(s, peer, slot):
        return pltpu.make_async_remote_copy(
            src_ref=x_ref.at[:, pl.ds(peer * width, width)],
            dst_ref=o_ref.at[:, pl.ds(slot * width, width)],
            send_sem=sems.at[0, s], recv_sem=sems.at[1, s],
            device_id=(row, peer), device_id_type=MESH_ID,
        )

    def share(s, peer, slot):
        return pltpu.make_async_remote_copy(
            src_ref=r_ref.at[peer], dst_ref=got.at[slot],
            send_sem=sems.at[2, s], recv_sem=sems.at[3, s],
            device_id=(row, peer), device_id_type=MESH_ID,
        )

    for s, peer, _ in col_peers(n):
        share(s, peer, me).start()
        piece(s, peer, me).start()
    d_ref[...] = jnp.dot(li_ref[...], y_ref[...], preferred_element_type=jnp.float32)
    for s, peer, source in col_peers(n):
        share(s, peer, me).wait_send()
        share(s, source, source).wait_recv()
    own.wait()
    share_ref[...] = jnp.sum(got[...], axis=0)
    for s, peer, source in col_peers(n):
        piece(s, peer, me).wait_send()
        piece(s, source, source).wait_recv()
    local.wait()
    for copy in level_copies:
        copy.wait()


def scatter(x, r, lv, staged, li, y):
    n = r.shape[0]
    return pl.pallas_call(
        functools.partial(scatter_kernel, n),
        out_shape=(
            jax.ShapeDtypeStruct(x.shape, x.dtype),
            jax.ShapeDtypeStruct(r.shape[1:], r.dtype),
            jax.ShapeDtypeStruct((lv.shape[0] - 1,) + lv.shape[1:], lv.dtype),
            jax.ShapeDtypeStruct((2,) + lv.shape[1:], lv.dtype),
            jax.ShapeDtypeStruct((li.shape[0], y.shape[1]), jnp.float32),
        ),
        in_specs=[
            pl.BlockSpec(memory_space=pl.ANY),
            pl.BlockSpec(memory_space=pltpu.VMEM),
            pl.BlockSpec(memory_space=pl.ANY),
            pl.BlockSpec(memory_space=pltpu.VMEM),
            pl.BlockSpec(memory_space=pltpu.VMEM),
            pl.BlockSpec(memory_space=pltpu.VMEM),
        ],
        out_specs=(
            pl.BlockSpec(memory_space=pl.ANY),
            pl.BlockSpec(memory_space=pltpu.VMEM),
            pl.BlockSpec(memory_space=pl.ANY),
            pl.BlockSpec(memory_space=pl.ANY),
            pl.BlockSpec(memory_space=pltpu.VMEM),
        ),
        scratch_shapes=[
            pltpu.VMEM(r.shape, r.dtype),
            pltpu.SemaphoreType.DMA((4, n)),
            pltpu.SemaphoreType.DMA((2,)),
            pltpu.SemaphoreType.DMA((2, 3)),
        ],
        compiler_params=pltpu.CompilerParams(
            collective_id=0, has_side_effects=True, vmem_limit_bytes=4 * 1024 * 1024
        ),
    )(x, r, lv, staged, li, y)


def gather_kernel(
    n, m, a_ref, w_ref, share_ref, c1_ref, p_ref, e2_ref, e3_ref, o_ref, full_ref, got1, got2,
    mixed, rows_got, total, rounded, sems, row_sems, local_sems, sib_sems,
):
    me = lax.axis_index("col")
    row = lax.axis_index("row")
    piece_rows = mixed.shape[1]
    row_peers = [(s, lax.rem(row + s, m), lax.rem(row + m - s, m)) for s in range(1, m)]
    barrier = pltpu.get_barrier_semaphore()
    for s, peer, _ in col_peers(n):
        pl.semaphore_signal(barrier, inc=1, device_id=(row, peer), device_id_type=MESH_ID)
    for s, peer, _ in row_peers:
        pl.semaphore_signal(barrier, inc=1, device_id=(peer, me), device_id_type=MESH_ID)
    pl.semaphore_wait(barrier, n - 1 + m - 1)

    own = pltpu.make_async_copy(share_ref, rows_got.at[row], local_sems.at[1])
    own.start()
    sends = [(c1_ref, got1, flipped(row, 2)), (p_ref, got2, flipped(row, 1))]
    sibs = []
    for i, (src_ref, dst_ref, peer) in enumerate(sends):
        sib = pltpu.make_async_remote_copy(
            src_ref=src_ref, dst_ref=dst_ref,
            send_sem=sib_sems.at[0, i], recv_sem=sib_sems.at[1, i],
            device_id=(peer, me), device_id_type=MESH_ID,
        )
        sib.start()
        sibs.append(sib)

    def part(s, peer, slot):
        return pltpu.make_async_remote_copy(
            src_ref=share_ref, dst_ref=rows_got.at[slot],
            send_sem=row_sems.at[0, s], recv_sem=row_sems.at[1, s],
            device_id=(peer, me), device_id_type=MESH_ID,
        )

    for s, peer, _ in row_peers:
        part(s, peer, row).start()

    def piece(s, peer, slot):
        return pltpu.make_async_remote_copy(
            src_ref=mixed.at[peer], dst_ref=o_ref.at[slot],
            send_sem=sems.at[0, s], recv_sem=sems.at[1, s],
            device_id=(row, peer), device_id_type=MESH_ID,
        )

    def compute(peer):
        first = pl.multiple_of(peer * piece_rows, piece_rows)
        mixed[peer] = lax.dot_general(
            w_ref[pl.ds(first, piece_rows), :], a_ref[...], (((1,), (1,)), ((), ())),
            preferred_element_type=jnp.float32,
        ).astype(mixed.dtype)

    def compute_and_send(s, carry):
        peer = lax.rem(me + s, n)
        compute(peer)
        piece(s, peer, me).start()
        return carry

    half = n // 4
    lax.fori_loop(1, half, compute_and_send, 0)

    def spread(s, peer, slot):
        return pltpu.make_async_remote_copy(
            src_ref=rounded, dst_ref=full_ref.at[slot],
            send_sem=sems.at[2, s], recv_sem=sems.at[3, s],
            device_id=(row, peer), device_id_type=MESH_ID,
        )

    for s, peer, source in row_peers:
        part(s, peer, row).wait_send()
        part(s, source, source).wait_recv()
    own.wait()
    total[...] = jnp.sum(rows_got[...], axis=0)
    rounded[...] = total[...].astype(rounded.dtype)
    mine = pltpu.make_async_copy(rounded, full_ref.at[me], local_sems.at[2])
    mine.start()
    for s, peer, _ in col_peers(n):
        spread(s, peer, me).start()

    lax.fori_loop(half, n, compute_and_send, 0)
    compute(me)
    local = pltpu.make_async_copy(mixed.at[me], o_ref.at[me], local_sems.at[0])
    local.start()

    for s, peer, source in col_peers(n):
        spread(s, peer, me).wait_send()
        spread(s, source, source).wait_recv()
        piece(s, peer, me).wait_send()
        piece(s, source, source).wait_recv()
    mine.wait()
    local.wait()
    for sib in sibs:
        sib.wait()


def gather(a, w, share, c1, p, staged, n, m):
    piece_rows = w.shape[0] // n
    columns = a.shape[0]
    return pl.pallas_call(
        functools.partial(gather_kernel, n, m),
        out_shape=(
            jax.ShapeDtypeStruct((n, piece_rows, columns), a.dtype),
            jax.ShapeDtypeStruct((n,) + share.shape, jnp.bfloat16),
            jax.ShapeDtypeStruct(c1.shape, c1.dtype),
            jax.ShapeDtypeStruct(p.shape, p.dtype),
        ),
        in_specs=[
            pl.BlockSpec(memory_space=pltpu.VMEM),
            pl.BlockSpec(memory_space=pltpu.VMEM),
            pl.BlockSpec(memory_space=pltpu.VMEM),
            pl.BlockSpec(memory_space=pl.ANY),
            pl.BlockSpec(memory_space=pl.ANY),
        ]
        + [pl.BlockSpec(memory_space=pltpu.VMEM)] * len(staged),
        out_specs=(
            pl.BlockSpec(memory_space=pl.ANY),
            pl.BlockSpec(memory_space=pltpu.VMEM),
            pl.BlockSpec(memory_space=pl.ANY),
            pl.BlockSpec(memory_space=pl.ANY),
        ),
        scratch_shapes=[
            pltpu.VMEM((n, piece_rows, columns), a.dtype),
            pltpu.VMEM((m,) + share.shape, share.dtype),
            pltpu.VMEM(share.shape, share.dtype),
            pltpu.VMEM(share.shape, jnp.bfloat16),
            pltpu.SemaphoreType.DMA((4, n)),
            pltpu.SemaphoreType.DMA((2, m)),
            pltpu.SemaphoreType.DMA((3,)),
            pltpu.SemaphoreType.DMA((2, 2)),
        ],
        compiler_params=pltpu.CompilerParams(
            collective_id=1, has_side_effects=True, vmem_limit_bytes=48 * 1024 * 1024
        ),
    )(a, w, share, c1, p, *staged)


def per_device(
    right_side,
    leaf_inverse,
    compress,
    middle,
    expand,
    row_project,
    row_expand,
    root_project,
    root_expand,
    owner_map,
):
    lowered = right_side.astype(jnp.bfloat16)
    columns = lowered.shape[1]
    root_term = lax.dot_general(
        lowered, root_project, contract_first, preferred_element_type=jnp.float32
    )
    level_coeffs = jnp.einsum(
        "lw,blr->bwr", lowered, row_project, preferred_element_type=jnp.float32
    )
    coeffs = lax.dot_general(
        lowered, compress, contract_first, preferred_element_type=jnp.float32
    ).astype(jnp.bfloat16)
    col_count = lax.axis_size("col")
    pieces = coeffs.reshape(columns, col_count, -1)
    chosen = (owner_map[:, None] == jnp.arange(col_count, dtype=owner_map.dtype)[None, :]).astype(
        jnp.bfloat16
    )
    outgoing = jnp.einsum(
        "kd,wkx->wdx", chosen, pieces, preferred_element_type=jnp.float32
    ).astype(jnp.bfloat16)
    root_shares = root_term.reshape(col_count, -1, root_term.shape[1])
    arrived, root_share, pair, far, dense_part = scatter(
        outgoing.reshape(columns, -1), root_shares, level_coeffs, expand, leaf_inverse, lowered
    )
    pair_sum = (level_coeffs[1] + pair[1]).astype(jnp.bfloat16)
    far_sum = far[0] + far[1]
    returned, root_full, quad_one, quad_two = gather(
        arrived, middle, root_share, pair_sum, far_sum, (row_expand, root_expand), col_count,
        lax.axis_size("row"),
    )
    ordered = jnp.einsum(
        "jd,dxw->jxw", chosen, returned, preferred_element_type=jnp.float32
    ).astype(jnp.bfloat16).reshape(-1, columns)
    cluster_part = jnp.dot(expand, ordered, preferred_element_type=jnp.float32)

    sibling_sum = jnp.stack(
        [pair[0], quad_one.astype(jnp.float32), far_sum + quad_two], axis=0
    )
    root_coeffs = root_full.reshape(columns, -1)
    coupled = jnp.einsum(
        "blr,bwr->lw",
        row_expand,
        sibling_sum.astype(jnp.bfloat16),
        preferred_element_type=jnp.float32,
    )
    root_part = lax.dot_general(
        root_expand, root_coeffs, (((1,), (1,)), ((), ())), preferred_element_type=jnp.float32
    )
    return dense_part + cluster_part + coupled + root_part


def solution(mesh):
    in_specs = (
        P(("row", "col"), None),
        P(("row", "col"), None),
        P(("row", "col"), None),
        P(("row", "col"), None),
        P(("row", "col"), None),
        P(None, ("row", "col"), None),
        P(None, ("row", "col"), None),
        P(("row", "col"), None),
        P(("row", "col"), None),
        P(),
    )
    out_specs = P(("row", "col"), None)
    return jax.shard_map(
        per_device, mesh=mesh, in_specs=in_specs, out_specs=out_specs, check_vma=False
    )
```

```python
import functools

import jax
import jax.numpy as jnp
from jax import lax
from jax.experimental import pallas as pl
from jax.experimental.pallas import tpu as pltpu
from jax.sharding import PartitionSpec as P

contract_first = (((0,), (0,)), ((), ()))
MESH_ID = pl.DeviceIdType.MESH


def swapped(x, axis, bit):
    return lax.ppermute(x, axis, [(i, i ^ 1 << bit) for i in range(lax.axis_size(axis))])


def flipped(index, bit):
    return index + bit - 2 * bit * lax.rem(index // bit, 2)


def col_peers(n):
    me = lax.axis_index("col")
    return [(s, lax.rem(me + s, n), lax.rem(me + n - s, n)) for s in range(1, n)]


def scatter_kernel(
    n, x_ref, r_ref, lv_ref, e0_ref, li_ref, y_ref, o_ref, share_ref, pair_ref, far_ref, d_ref,
    got, sems, local_sems, pair_sems,
):
    me = lax.axis_index("col")
    row = lax.axis_index("row")
    width = x_ref.shape[1] // n
    barrier = pltpu.get_barrier_semaphore()
    for s, peer, _ in col_peers(n):
        pl.semaphore_signal(barrier, inc=1, device_id=(row, peer), device_id_type=MESH_ID)
    partner = flipped(row, 1)
    far = [flipped(row, 4), flipped(flipped(row, 4), 2)]
    for peer in [partner] + far:
        pl.semaphore_signal(barrier, inc=1, device_id=(peer, me), device_id_type=MESH_ID)
    pl.semaphore_wait(barrier, n + 2)

    low = pair_ref.shape[0]
    level_copies = [
        pltpu.make_async_remote_copy(
            src_ref=lv_ref.at[pl.ds(0, low)], dst_ref=pair_ref,
            send_sem=pair_sems.at[0, 0], recv_sem=pair_sems.at[1, 0],
            device_id=(partner, me), device_id_type=MESH_ID,
        )
    ]
    for i, peer in enumerate(far):
        level_copies.append(
            pltpu.make_async_remote_copy(
                src_ref=lv_ref.at[low], dst_ref=far_ref.at[i],
                send_sem=pair_sems.at[0, i + 1], recv_sem=pair_sems.at[1, i + 1],
                device_id=(peer, me), device_id_type=MESH_ID,
            )
        )
    for copy in level_copies:
        copy.start()
    local = pltpu.make_async_copy(
        x_ref.at[:, pl.ds(me * width, width)], o_ref.at[:, pl.ds(me * width, width)],
        local_sems.at[0],
    )
    local.start()
    own = pltpu.make_async_copy(r_ref.at[me], got.at[me], local_sems.at[1])
    own.start()

    def piece(s, peer, slot):
        return pltpu.make_async_remote_copy(
            src_ref=x_ref.at[:, pl.ds(peer * width, width)],
            dst_ref=o_ref.at[:, pl.ds(slot * width, width)],
            send_sem=sems.at[0, s], recv_sem=sems.at[1, s],
            device_id=(row, peer), device_id_type=MESH_ID,
        )

    def share(s, peer, slot):
        return pltpu.make_async_remote_copy(
            src_ref=r_ref.at[peer], dst_ref=got.at[slot],
            send_sem=sems.at[2, s], recv_sem=sems.at[3, s],
            device_id=(row, peer), device_id_type=MESH_ID,
        )

    for s, peer, _ in col_peers(n):
        share(s, peer, me).start()
        piece(s, peer, me).start()
    d_ref[...] = jnp.dot(li_ref[...], y_ref[...], preferred_element_type=jnp.float32)
    for s, peer, source in col_peers(n):
        share(s, peer, me).wait_send()
        share(s, source, source).wait_recv()
    own.wait()
    share_ref[...] = jnp.sum(got[...], axis=0)
    for s, peer, source in col_peers(n):
        piece(s, peer, me).wait_send()
        piece(s, source, source).wait_recv()
    local.wait()
    for copy in level_copies:
        copy.wait()


def scatter(x, r, lv, staged, li, y):
    n = r.shape[0]
    return pl.pallas_call(
        functools.partial(scatter_kernel, n),
        out_shape=(
            jax.ShapeDtypeStruct(x.shape, x.dtype),
            jax.ShapeDtypeStruct(r.shape[1:], r.dtype),
            jax.ShapeDtypeStruct((lv.shape[0] - 1,) + lv.shape[1:], lv.dtype),
            jax.ShapeDtypeStruct((2,) + lv.shape[1:], lv.dtype),
            jax.ShapeDtypeStruct((li.shape[0], y.shape[1]), jnp.float32),
        ),
        in_specs=[
            pl.BlockSpec(memory_space=pl.ANY),
            pl.BlockSpec(memory_space=pltpu.VMEM),
            pl.BlockSpec(memory_space=pl.ANY),
            pl.BlockSpec(memory_space=pltpu.VMEM),
            pl.BlockSpec(memory_space=pltpu.VMEM),
            pl.BlockSpec(memory_space=pltpu.VMEM),
        ],
        out_specs=(
            pl.BlockSpec(memory_space=pl.ANY),
            pl.BlockSpec(memory_space=pltpu.VMEM),
            pl.BlockSpec(memory_space=pl.ANY),
            pl.BlockSpec(memory_space=pl.ANY),
            pl.BlockSpec(memory_space=pltpu.VMEM),
        ),
        scratch_shapes=[
            pltpu.VMEM(r.shape, r.dtype),
            pltpu.SemaphoreType.DMA((4, n)),
            pltpu.SemaphoreType.DMA((2,)),
            pltpu.SemaphoreType.DMA((2, 3)),
        ],
        compiler_params=pltpu.CompilerParams(
            collective_id=0, has_side_effects=True, vmem_limit_bytes=4 * 1024 * 1024
        ),
    )(x, r, lv, staged, li, y)


def gather_kernel(
    n, m, a_ref, w_ref, share_ref, c1_ref, p_ref, e2_ref, e3_ref, o_ref, full_ref, got1, got2,
    mixed, rows_got, total, rounded, sems, row_sems, local_sems, sib_sems,
):
    me = lax.axis_index("col")
    row = lax.axis_index("row")
    piece_rows = mixed.shape[1]
    row_peers = [(s, lax.rem(row + s, m), lax.rem(row + m - s, m)) for s in range(1, m)]
    barrier = pltpu.get_barrier_semaphore()
    for s, peer, _ in col_peers(n):
        pl.semaphore_signal(barrier, inc=1, device_id=(row, peer), device_id_type=MESH_ID)
    for s, peer, _ in row_peers:
        pl.semaphore_signal(barrier, inc=1, device_id=(peer, me), device_id_type=MESH_ID)
    pl.semaphore_wait(barrier, n - 1 + m - 1)

    own = pltpu.make_async_copy(share_ref, rows_got.at[row], local_sems.at[1])
    own.start()
    sends = [(c1_ref, got1, flipped(row, 2)), (p_ref, got2, flipped(row, 1))]
    sibs = []
    for i, (src_ref, dst_ref, peer) in enumerate(sends):
        sib = pltpu.make_async_remote_copy(
            src_ref=src_ref, dst_ref=dst_ref,
            send_sem=sib_sems.at[0, i], recv_sem=sib_sems.at[1, i],
            device_id=(peer, me), device_id_type=MESH_ID,
        )
        sib.start()
        sibs.append(sib)

    def part(s, peer, slot):
        return pltpu.make_async_remote_copy(
            src_ref=share_ref, dst_ref=rows_got.at[slot],
            send_sem=row_sems.at[0, s], recv_sem=row_sems.at[1, s],
            device_id=(peer, me), device_id_type=MESH_ID,
        )

    for s, peer, _ in row_peers:
        part(s, peer, row).start()

    def piece(s, peer, slot):
        return pltpu.make_async_remote_copy(
            src_ref=mixed.at[peer], dst_ref=o_ref.at[slot],
            send_sem=sems.at[0, s], recv_sem=sems.at[1, s],
            device_id=(row, peer), device_id_type=MESH_ID,
        )

    def compute(peer):
        first = pl.multiple_of(peer * piece_rows, piece_rows)
        mixed[peer] = lax.dot_general(
            w_ref[pl.ds(first, piece_rows), :], a_ref[...], (((1,), (1,)), ((), ())),
            preferred_element_type=jnp.float32,
        ).astype(mixed.dtype)

    def compute_and_send(s, carry):
        peer = lax.rem(me + s, n)
        compute(peer)
        piece(s, peer, me).start()
        return carry

    half = n - n // 4
    lax.fori_loop(1, half, compute_and_send, 0)

    def spread(s, peer, slot):
        return pltpu.make_async_remote_copy(
            src_ref=rounded, dst_ref=full_ref.at[slot],
            send_sem=sems.at[2, s], recv_sem=sems.at[3, s],
            device_id=(row, peer), device_id_type=MESH_ID,
        )

    for s, peer, source in row_peers:
        part(s, peer, row).wait_send()
        part(s, source, source).wait_recv()
    own.wait()
    total[...] = jnp.sum(rows_got[...], axis=0)
    rounded[...] = total[...].astype(rounded.dtype)
    mine = pltpu.make_async_copy(rounded, full_ref.at[me], local_sems.at[2])
    mine.start()
    for s, peer, _ in col_peers(n):
        spread(s, peer, me).start()

    lax.fori_loop(half, n, compute_and_send, 0)
    compute(me)
    local = pltpu.make_async_copy(mixed.at[me], o_ref.at[me], local_sems.at[0])
    local.start()

    for s, peer, source in col_peers(n):
        spread(s, peer, me).wait_send()
        spread(s, source, source).wait_recv()
        piece(s, peer, me).wait_send()
        piece(s, source, source).wait_recv()
    mine.wait()
    local.wait()
    for sib in sibs:
        sib.wait()


def gather(a, w, share, c1, p, staged, n, m):
    piece_rows = w.shape[0] // n
    columns = a.shape[0]
    return pl.pallas_call(
        functools.partial(gather_kernel, n, m),
        out_shape=(
            jax.ShapeDtypeStruct((n, piece_rows, columns), a.dtype),
            jax.ShapeDtypeStruct((n,) + share.shape, jnp.bfloat16),
            jax.ShapeDtypeStruct(c1.shape, c1.dtype),
            jax.ShapeDtypeStruct(p.shape, p.dtype),
        ),
        in_specs=[
            pl.BlockSpec(memory_space=pltpu.VMEM),
            pl.BlockSpec(memory_space=pltpu.VMEM),
            pl.BlockSpec(memory_space=pltpu.VMEM),
            pl.BlockSpec(memory_space=pl.ANY),
            pl.BlockSpec(memory_space=pl.ANY),
        ]
        + [pl.BlockSpec(memory_space=pltpu.VMEM)] * len(staged),
        out_specs=(
            pl.BlockSpec(memory_space=pl.ANY),
            pl.BlockSpec(memory_space=pltpu.VMEM),
            pl.BlockSpec(memory_space=pl.ANY),
            pl.BlockSpec(memory_space=pl.ANY),
        ),
        scratch_shapes=[
            pltpu.VMEM((n, piece_rows, columns), a.dtype),
            pltpu.VMEM((m,) + share.shape, share.dtype),
            pltpu.VMEM(share.shape, share.dtype),
            pltpu.VMEM(share.shape, jnp.bfloat16),
            pltpu.SemaphoreType.DMA((4, n)),
            pltpu.SemaphoreType.DMA((2, m)),
            pltpu.SemaphoreType.DMA((3,)),
            pltpu.SemaphoreType.DMA((2, 2)),
        ],
        compiler_params=pltpu.CompilerParams(
            collective_id=1, has_side_effects=True, vmem_limit_bytes=48 * 1024 * 1024
        ),
    )(a, w, share, c1, p, *staged)


def per_device(
    right_side,
    leaf_inverse,
    compress,
    middle,
    expand,
    row_project,
    row_expand,
    root_project,
    root_expand,
    owner_map,
):
    lowered = right_side.astype(jnp.bfloat16)
    columns = lowered.shape[1]
    root_term = lax.dot_general(
        lowered, root_project, contract_first, preferred_element_type=jnp.float32
    )
    level_coeffs = jnp.einsum(
        "lw,blr->bwr", lowered, row_project, preferred_element_type=jnp.float32
    )
    coeffs = lax.dot_general(
        lowered, compress, contract_first, preferred_element_type=jnp.float32
    ).astype(jnp.bfloat16)
    col_count = lax.axis_size("col")
    pieces = coeffs.reshape(columns, col_count, -1)
    chosen = (owner_map[:, None] == jnp.arange(col_count, dtype=owner_map.dtype)[None, :]).astype(
        jnp.bfloat16
    )
    outgoing = jnp.einsum(
        "kd,wkx->wdx", chosen, pieces, preferred_element_type=jnp.float32
    ).astype(jnp.bfloat16)
    root_shares = root_term.reshape(col_count, -1, root_term.shape[1])
    arrived, root_share, pair, far, dense_part = scatter(
        outgoing.reshape(columns, -1), root_shares, level_coeffs, expand, leaf_inverse, lowered
    )
    pair_sum = (level_coeffs[1] + pair[1]).astype(jnp.bfloat16)
    far_sum = far[0] + far[1]
    returned, root_full, quad_one, quad_two = gather(
        arrived, middle, root_share, pair_sum, far_sum, (row_expand, root_expand), col_count,
        lax.axis_size("row"),
    )
    ordered = jnp.einsum(
        "jd,dxw->jxw", chosen, returned, preferred_element_type=jnp.float32
    ).astype(jnp.bfloat16).reshape(-1, columns)
    cluster_part = jnp.dot(expand, ordered, preferred_element_type=jnp.float32)

    sibling_sum = jnp.stack(
        [pair[0], quad_one.astype(jnp.float32), far_sum + quad_two], axis=0
    )
    root_coeffs = root_full.reshape(columns, -1)
    coupled = jnp.einsum(
        "blr,bwr->lw",
        row_expand,
        sibling_sum.astype(jnp.bfloat16),
        preferred_element_type=jnp.float32,
    )
    root_part = lax.dot_general(
        root_expand, root_coeffs, (((1,), (1,)), ((), ())), preferred_element_type=jnp.float32
    )
    return dense_part + cluster_part + coupled + root_part


def solution(mesh):
    in_specs = (
        P(("row", "col"), None),
        P(("row", "col"), None),
        P(("row", "col"), None),
        P(("row", "col"), None),
        P(("row", "col"), None),
        P(None, ("row", "col"), None),
        P(None, ("row", "col"), None),
        P(("row", "col"), None),
        P(("row", "col"), None),
        P(),
    )
    out_specs = P(("row", "col"), None)
    return jax.shard_map(
        per_device, mesh=mesh, in_specs=in_specs, out_specs=out_specs, check_vma=False
    )
```

```python
import functools

import jax
import jax.numpy as jnp
from jax import lax
from jax.experimental import pallas as pl
from jax.experimental.pallas import tpu as pltpu
from jax.sharding import PartitionSpec as P

contract_first = (((0,), (0,)), ((), ()))
MESH_ID = pl.DeviceIdType.MESH


def swapped(x, axis, bit):
    return lax.ppermute(x, axis, [(i, i ^ 1 << bit) for i in range(lax.axis_size(axis))])


def flipped(index, bit):
    return index + bit - 2 * bit * lax.rem(index // bit, 2)


def col_peers(n):
    me = lax.axis_index("col")
    return [(s, lax.rem(me + s, n), lax.rem(me + n - s, n)) for s in range(1, n)]


def scatter_kernel(
    n, x_ref, r_ref, lv_ref, e0_ref, li_ref, y_ref, o_ref, share_ref, pair_ref, far_ref, d_ref,
    got, sems, local_sems, pair_sems,
):
    me = lax.axis_index("col")
    row = lax.axis_index("row")
    width = x_ref.shape[1] // n
    barrier = pltpu.get_barrier_semaphore()
    for s, peer, _ in col_peers(n):
        pl.semaphore_signal(barrier, inc=1, device_id=(row, peer), device_id_type=MESH_ID)
    partner = flipped(row, 1)
    far = [flipped(row, 4), flipped(flipped(row, 4), 2)]
    for peer in [partner] + far:
        pl.semaphore_signal(barrier, inc=1, device_id=(peer, me), device_id_type=MESH_ID)
    pl.semaphore_wait(barrier, n + 2)

    low = pair_ref.shape[0]
    level_copies = [
        pltpu.make_async_remote_copy(
            src_ref=lv_ref.at[pl.ds(0, low)], dst_ref=pair_ref,
            send_sem=pair_sems.at[0, 0], recv_sem=pair_sems.at[1, 0],
            device_id=(partner, me), device_id_type=MESH_ID,
        )
    ]
    for i, peer in enumerate(far):
        level_copies.append(
            pltpu.make_async_remote_copy(
                src_ref=lv_ref.at[low], dst_ref=far_ref.at[i],
                send_sem=pair_sems.at[0, i + 1], recv_sem=pair_sems.at[1, i + 1],
                device_id=(peer, me), device_id_type=MESH_ID,
            )
        )
    for copy in level_copies:
        copy.start()
    local = pltpu.make_async_copy(
        x_ref.at[:, pl.ds(me * width, width)], o_ref.at[:, pl.ds(me * width, width)],
        local_sems.at[0],
    )
    local.start()
    own = pltpu.make_async_copy(r_ref.at[me], got.at[me], local_sems.at[1])
    own.start()

    def piece(s, peer, slot):
        return pltpu.make_async_remote_copy(
            src_ref=x_ref.at[:, pl.ds(peer * width, width)],
            dst_ref=o_ref.at[:, pl.ds(slot * width, width)],
            send_sem=sems.at[0, s], recv_sem=sems.at[1, s],
            device_id=(row, peer), device_id_type=MESH_ID,
        )

    def share(s, peer, slot):
        return pltpu.make_async_remote_copy(
            src_ref=r_ref.at[peer], dst_ref=got.at[slot],
            send_sem=sems.at[2, s], recv_sem=sems.at[3, s],
            device_id=(row, peer), device_id_type=MESH_ID,
        )

    for s, peer, _ in col_peers(n):
        share(s, peer, me).start()
        piece(s, peer, me).start()
    d_ref[...] = jnp.dot(li_ref[...], y_ref[...], preferred_element_type=jnp.float32)
    for s, peer, source in col_peers(n):
        share(s, peer, me).wait_send()
        share(s, source, source).wait_recv()
    own.wait()
    share_ref[...] = jnp.sum(got[...], axis=0)
    for s, peer, source in col_peers(n):
        piece(s, peer, me).wait_send()
        piece(s, source, source).wait_recv()
    local.wait()
    for copy in level_copies:
        copy.wait()


def scatter(x, r, lv, staged, li, y):
    n = r.shape[0]
    return pl.pallas_call(
        functools.partial(scatter_kernel, n),
        out_shape=(
            jax.ShapeDtypeStruct(x.shape, x.dtype),
            jax.ShapeDtypeStruct(r.shape[1:], r.dtype),
            jax.ShapeDtypeStruct((lv.shape[0] - 1,) + lv.shape[1:], lv.dtype),
            jax.ShapeDtypeStruct((2,) + lv.shape[1:], lv.dtype),
            jax.ShapeDtypeStruct((li.shape[0], y.shape[1]), jnp.float32),
        ),
        in_specs=[
            pl.BlockSpec(memory_space=pl.ANY),
            pl.BlockSpec(memory_space=pltpu.VMEM),
            pl.BlockSpec(memory_space=pl.ANY),
            pl.BlockSpec(memory_space=pltpu.VMEM),
            pl.BlockSpec(memory_space=pltpu.VMEM),
            pl.BlockSpec(memory_space=pltpu.VMEM),
        ],
        out_specs=(
            pl.BlockSpec(memory_space=pl.ANY),
            pl.BlockSpec(memory_space=pltpu.VMEM),
            pl.BlockSpec(memory_space=pl.ANY),
            pl.BlockSpec(memory_space=pl.ANY),
            pl.BlockSpec(memory_space=pltpu.VMEM),
        ),
        scratch_shapes=[
            pltpu.VMEM(r.shape, r.dtype),
            pltpu.SemaphoreType.DMA((4, n)),
            pltpu.SemaphoreType.DMA((2,)),
            pltpu.SemaphoreType.DMA((2, 3)),
        ],
        compiler_params=pltpu.CompilerParams(
            collective_id=0, has_side_effects=True, vmem_limit_bytes=4 * 1024 * 1024
        ),
    )(x, r, lv, staged, li, y)


def gather_kernel(
    n, m, a_ref, w_ref, share_ref, c1_ref, p_ref, e2_ref, e3_ref, o_ref, full_ref, got1, got2,
    mixed, rows_got, total, rounded, sems, row_sems, local_sems, sib_sems,
):
    me = lax.axis_index("col")
    row = lax.axis_index("row")
    piece_rows = mixed.shape[1]
    row_peers = [(s, lax.rem(row + s, m), lax.rem(row + m - s, m)) for s in range(1, m)]
    barrier = pltpu.get_barrier_semaphore()
    for s, peer, _ in col_peers(n):
        pl.semaphore_signal(barrier, inc=1, device_id=(row, peer), device_id_type=MESH_ID)
    for s, peer, _ in row_peers:
        pl.semaphore_signal(barrier, inc=1, device_id=(peer, me), device_id_type=MESH_ID)
    pl.semaphore_wait(barrier, n - 1 + m - 1)

    own = pltpu.make_async_copy(share_ref, rows_got.at[row], local_sems.at[1])
    own.start()
    sends = [(c1_ref, got1, flipped(row, 2)), (p_ref, got2, flipped(row, 1))]
    sibs = []
    for i, (src_ref, dst_ref, peer) in enumerate(sends):
        sib = pltpu.make_async_remote_copy(
            src_ref=src_ref, dst_ref=dst_ref,
            send_sem=sib_sems.at[0, i], recv_sem=sib_sems.at[1, i],
            device_id=(peer, me), device_id_type=MESH_ID,
        )
        sib.start()
        sibs.append(sib)

    def part(s, peer, slot):
        return pltpu.make_async_remote_copy(
            src_ref=share_ref, dst_ref=rows_got.at[slot],
            send_sem=row_sems.at[0, s], recv_sem=row_sems.at[1, s],
            device_id=(peer, me), device_id_type=MESH_ID,
        )

    for s, peer, _ in row_peers:
        part(s, peer, row).start()

    def piece(s, peer, slot):
        return pltpu.make_async_remote_copy(
            src_ref=mixed.at[peer], dst_ref=o_ref.at[slot],
            send_sem=sems.at[0, s], recv_sem=sems.at[1, s],
            device_id=(row, peer), device_id_type=MESH_ID,
        )

    def compute(peer):
        first = pl.multiple_of(peer * piece_rows, piece_rows)
        mixed[peer] = lax.dot_general(
            w_ref[pl.ds(first, piece_rows), :], a_ref[...], (((1,), (1,)), ((), ())),
            preferred_element_type=jnp.float32,
        ).astype(mixed.dtype)

    def compute_and_send(s, carry):
        peer = lax.rem(me + s, n)
        compute(peer)
        piece(s, peer, me).start()
        return carry

    half = n
    lax.fori_loop(1, half, compute_and_send, 0)

    def spread(s, peer, slot):
        return pltpu.make_async_remote_copy(
            src_ref=rounded, dst_ref=full_ref.at[slot],
            send_sem=sems.at[2, s], recv_sem=sems.at[3, s],
            device_id=(row, peer), device_id_type=MESH_ID,
        )

    for s, peer, source in row_peers:
        part(s, peer, row).wait_send()
        part(s, source, source).wait_recv()
    own.wait()
    total[...] = jnp.sum(rows_got[...], axis=0)
    rounded[...] = total[...].astype(rounded.dtype)
    mine = pltpu.make_async_copy(rounded, full_ref.at[me], local_sems.at[2])
    mine.start()
    for s, peer, _ in col_peers(n):
        spread(s, peer, me).start()

    lax.fori_loop(half, n, compute_and_send, 0)
    compute(me)
    local = pltpu.make_async_copy(mixed.at[me], o_ref.at[me], local_sems.at[0])
    local.start()

    for s, peer, source in col_peers(n):
        spread(s, peer, me).wait_send()
        spread(s, source, source).wait_recv()
        piece(s, peer, me).wait_send()
        piece(s, source, source).wait_recv()
    mine.wait()
    local.wait()
    for sib in sibs:
        sib.wait()


def gather(a, w, share, c1, p, staged, n, m):
    piece_rows = w.shape[0] // n
    columns = a.shape[0]
    return pl.pallas_call(
        functools.partial(gather_kernel, n, m),
        out_shape=(
            jax.ShapeDtypeStruct((n, piece_rows, columns), a.dtype),
            jax.ShapeDtypeStruct((n,) + share.shape, jnp.bfloat16),
            jax.ShapeDtypeStruct(c1.shape, c1.dtype),
            jax.ShapeDtypeStruct(p.shape, p.dtype),
        ),
        in_specs=[
            pl.BlockSpec(memory_space=pltpu.VMEM),
            pl.BlockSpec(memory_space=pltpu.VMEM),
            pl.BlockSpec(memory_space=pltpu.VMEM),
            pl.BlockSpec(memory_space=pl.ANY),
            pl.BlockSpec(memory_space=pl.ANY),
        ]
        + [pl.BlockSpec(memory_space=pltpu.VMEM)] * len(staged),
        out_specs=(
            pl.BlockSpec(memory_space=pl.ANY),
            pl.BlockSpec(memory_space=pltpu.VMEM),
            pl.BlockSpec(memory_space=pl.ANY),
            pl.BlockSpec(memory_space=pl.ANY),
        ),
        scratch_shapes=[
            pltpu.VMEM((n, piece_rows, columns), a.dtype),
            pltpu.VMEM((m,) + share.shape, share.dtype),
            pltpu.VMEM(share.shape, share.dtype),
            pltpu.VMEM(share.shape, jnp.bfloat16),
            pltpu.SemaphoreType.DMA((4, n)),
            pltpu.SemaphoreType.DMA((2, m)),
            pltpu.SemaphoreType.DMA((3,)),
            pltpu.SemaphoreType.DMA((2, 2)),
        ],
        compiler_params=pltpu.CompilerParams(
            collective_id=1, has_side_effects=True, vmem_limit_bytes=48 * 1024 * 1024
        ),
    )(a, w, share, c1, p, *staged)


def per_device(
    right_side,
    leaf_inverse,
    compress,
    middle,
    expand,
    row_project,
    row_expand,
    root_project,
    root_expand,
    owner_map,
):
    lowered = right_side.astype(jnp.bfloat16)
    columns = lowered.shape[1]
    root_term = lax.dot_general(
        lowered, root_project, contract_first, preferred_element_type=jnp.float32
    )
    level_coeffs = jnp.einsum(
        "lw,blr->bwr", lowered, row_project, preferred_element_type=jnp.float32
    )
    coeffs = lax.dot_general(
        lowered, compress, contract_first, preferred_element_type=jnp.float32
    ).astype(jnp.bfloat16)
    col_count = lax.axis_size("col")
    pieces = coeffs.reshape(columns, col_count, -1)
    chosen = (owner_map[:, None] == jnp.arange(col_count, dtype=owner_map.dtype)[None, :]).astype(
        jnp.bfloat16
    )
    outgoing = jnp.einsum(
        "kd,wkx->wdx", chosen, pieces, preferred_element_type=jnp.float32
    ).astype(jnp.bfloat16)
    root_shares = root_term.reshape(col_count, -1, root_term.shape[1])
    arrived, root_share, pair, far, dense_part = scatter(
        outgoing.reshape(columns, -1), root_shares, level_coeffs, expand, leaf_inverse, lowered
    )
    pair_sum = (level_coeffs[1] + pair[1]).astype(jnp.bfloat16)
    far_sum = far[0] + far[1]
    returned, root_full, quad_one, quad_two = gather(
        arrived, middle, root_share, pair_sum, far_sum, (row_expand, root_expand), col_count,
        lax.axis_size("row"),
    )
    ordered = jnp.einsum(
        "jd,dxw->jxw", chosen, returned, preferred_element_type=jnp.float32
    ).astype(jnp.bfloat16).reshape(-1, columns)
    cluster_part = jnp.dot(expand, ordered, preferred_element_type=jnp.float32)

    sibling_sum = jnp.stack(
        [pair[0], quad_one.astype(jnp.float32), far_sum + quad_two], axis=0
    )
    root_coeffs = root_full.reshape(columns, -1)
    coupled = jnp.einsum(
        "blr,bwr->lw",
        row_expand,
        sibling_sum.astype(jnp.bfloat16),
        preferred_element_type=jnp.float32,
    )
    root_part = lax.dot_general(
        root_expand, root_coeffs, (((1,), (1,)), ((), ())), preferred_element_type=jnp.float32
    )
    return dense_part + cluster_part + coupled + root_part


def solution(mesh):
    in_specs = (
        P(("row", "col"), None),
        P(("row", "col"), None),
        P(("row", "col"), None),
        P(("row", "col"), None),
        P(("row", "col"), None),
        P(None, ("row", "col"), None),
        P(None, ("row", "col"), None),
        P(("row", "col"), None),
        P(("row", "col"), None),
        P(),
    )
    out_specs = P(("row", "col"), None)
    return jax.shard_map(
        per_device, mesh=mesh, in_specs=in_specs, out_specs=out_specs, check_vma=False
    )
```

```python
import functools

import jax
import jax.numpy as jnp
from jax import lax
from jax.experimental import pallas as pl
from jax.experimental.pallas import tpu as pltpu
from jax.sharding import PartitionSpec as P

contract_first = (((0,), (0,)), ((), ()))
MESH_ID = pl.DeviceIdType.MESH


def swapped(x, axis, bit):
    return lax.ppermute(x, axis, [(i, i ^ 1 << bit) for i in range(lax.axis_size(axis))])


def flipped(index, bit):
    return index + bit - 2 * bit * lax.rem(index // bit, 2)


def col_peers(n):
    me = lax.axis_index("col")
    return [(s, lax.rem(me + s, n), lax.rem(me + n - s, n)) for s in range(1, n)]


def scatter_kernel(
    n, x_ref, r_ref, lv_ref, e0_ref, li_ref, y_ref, o_ref, share_ref, pair_ref, far_ref, d_ref,
    got, sems, local_sems, pair_sems,
):
    me = lax.axis_index("col")
    row = lax.axis_index("row")
    width = x_ref.shape[1] // n
    barrier = pltpu.get_barrier_semaphore()
    for s, peer, _ in col_peers(n):
        pl.semaphore_signal(barrier, inc=1, device_id=(row, peer), device_id_type=MESH_ID)
    partner = flipped(row, 1)
    far = [flipped(row, 4), flipped(flipped(row, 4), 2)]
    for peer in [partner] + far:
        pl.semaphore_signal(barrier, inc=1, device_id=(peer, me), device_id_type=MESH_ID)
    pl.semaphore_wait(barrier, n + 2)

    low = pair_ref.shape[0]
    level_copies = [
        pltpu.make_async_remote_copy(
            src_ref=lv_ref.at[pl.ds(0, low)], dst_ref=pair_ref,
            send_sem=pair_sems.at[0, 0], recv_sem=pair_sems.at[1, 0],
            device_id=(partner, me), device_id_type=MESH_ID,
        )
    ]
    for i, peer in enumerate(far):
        level_copies.append(
            pltpu.make_async_remote_copy(
                src_ref=lv_ref.at[low], dst_ref=far_ref.at[i],
                send_sem=pair_sems.at[0, i + 1], recv_sem=pair_sems.at[1, i + 1],
                device_id=(peer, me), device_id_type=MESH_ID,
            )
        )
    for copy in level_copies:
        copy.start()
    local = pltpu.make_async_copy(
        x_ref.at[:, pl.ds(me * width, width)], o_ref.at[:, pl.ds(me * width, width)],
        local_sems.at[0],
    )
    local.start()
    own = pltpu.make_async_copy(r_ref.at[me], got.at[me], local_sems.at[1])
    own.start()

    def piece(s, peer, slot):
        return pltpu.make_async_remote_copy(
            src_ref=x_ref.at[:, pl.ds(peer * width, width)],
            dst_ref=o_ref.at[:, pl.ds(slot * width, width)],
            send_sem=sems.at[0, s], recv_sem=sems.at[1, s],
            device_id=(row, peer), device_id_type=MESH_ID,
        )

    def share(s, peer, slot):
        return pltpu.make_async_remote_copy(
            src_ref=r_ref.at[peer], dst_ref=got.at[slot],
            send_sem=sems.at[2, s], recv_sem=sems.at[3, s],
            device_id=(row, peer), device_id_type=MESH_ID,
        )

    for s, peer, _ in col_peers(n):
        share(s, peer, me).start()
        piece(s, peer, me).start()
    d_ref[...] = jnp.dot(li_ref[...], y_ref[...], preferred_element_type=jnp.float32)
    for s, peer, source in col_peers(n):
        share(s, peer, me).wait_send()
        share(s, source, source).wait_recv()
    own.wait()
    share_ref[...] = jnp.sum(got[...], axis=0)
    for s, peer, source in col_peers(n):
        piece(s, peer, me).wait_send()
        piece(s, source, source).wait_recv()
    local.wait()
    for copy in level_copies:
        copy.wait()


def scatter(x, r, lv, staged, li, y):
    n = r.shape[0]
    return pl.pallas_call(
        functools.partial(scatter_kernel, n),
        out_shape=(
            jax.ShapeDtypeStruct(x.shape, x.dtype),
            jax.ShapeDtypeStruct(r.shape[1:], r.dtype),
            jax.ShapeDtypeStruct((lv.shape[0] - 1,) + lv.shape[1:], lv.dtype),
            jax.ShapeDtypeStruct((2,) + lv.shape[1:], lv.dtype),
            jax.ShapeDtypeStruct((li.shape[0], y.shape[1]), jnp.float32),
        ),
        in_specs=[
            pl.BlockSpec(memory_space=pl.ANY),
            pl.BlockSpec(memory_space=pltpu.VMEM),
            pl.BlockSpec(memory_space=pl.ANY),
            pl.BlockSpec(memory_space=pltpu.VMEM),
            pl.BlockSpec(memory_space=pltpu.VMEM),
            pl.BlockSpec(memory_space=pltpu.VMEM),
        ],
        out_specs=(
            pl.BlockSpec(memory_space=pl.ANY),
            pl.BlockSpec(memory_space=pltpu.VMEM),
            pl.BlockSpec(memory_space=pl.ANY),
            pl.BlockSpec(memory_space=pl.ANY),
            pl.BlockSpec(memory_space=pltpu.VMEM),
        ),
        scratch_shapes=[
            pltpu.VMEM(r.shape, r.dtype),
            pltpu.SemaphoreType.DMA((4, n)),
            pltpu.SemaphoreType.DMA((2,)),
            pltpu.SemaphoreType.DMA((2, 3)),
        ],
        compiler_params=pltpu.CompilerParams(
            collective_id=0, has_side_effects=True, vmem_limit_bytes=4 * 1024 * 1024
        ),
    )(x, r, lv, staged, li, y)


def gather_kernel(
    n, m, a_ref, w_ref, share_ref, c1_ref, p_ref, e2_ref, e3_ref, o_ref, full_ref, got1, got2,
    mixed, rows_got, total, rounded, sems, row_sems, local_sems, sib_sems,
):
    me = lax.axis_index("col")
    row = lax.axis_index("row")
    piece_rows = mixed.shape[1]
    row_peers = [(s, lax.rem(row + s, m), lax.rem(row + m - s, m)) for s in range(1, m)]
    barrier = pltpu.get_barrier_semaphore()
    for s, peer, _ in col_peers(n):
        pl.semaphore_signal(barrier, inc=1, device_id=(row, peer), device_id_type=MESH_ID)
    for s, peer, _ in row_peers:
        pl.semaphore_signal(barrier, inc=1, device_id=(peer, me), device_id_type=MESH_ID)
    pl.semaphore_wait(barrier, n - 1 + m - 1)

    own = pltpu.make_async_copy(share_ref, rows_got.at[row], local_sems.at[1])
    own.start()
    sends = [(c1_ref, got1, flipped(row, 2)), (p_ref, got2, flipped(row, 1))]
    sibs = []
    for i, (src_ref, dst_ref, peer) in enumerate(sends):
        sib = pltpu.make_async_remote_copy(
            src_ref=src_ref, dst_ref=dst_ref,
            send_sem=sib_sems.at[0, i], recv_sem=sib_sems.at[1, i],
            device_id=(peer, me), device_id_type=MESH_ID,
        )
        sib.start()
        sibs.append(sib)

    def part(s, peer, slot):
        return pltpu.make_async_remote_copy(
            src_ref=share_ref, dst_ref=rows_got.at[slot],
            send_sem=row_sems.at[0, s], recv_sem=row_sems.at[1, s],
            device_id=(peer, me), device_id_type=MESH_ID,
        )

    for s, peer, _ in row_peers:
        part(s, peer, row).start()

    def piece(s, peer, slot):
        return pltpu.make_async_remote_copy(
            src_ref=mixed.at[peer], dst_ref=o_ref.at[slot],
            send_sem=sems.at[0, s], recv_sem=sems.at[1, s],
            device_id=(row, peer), device_id_type=MESH_ID,
        )

    def compute(peer):
        first = pl.multiple_of(peer * piece_rows, piece_rows)
        mixed[peer] = lax.dot_general(
            w_ref[pl.ds(first, piece_rows), :], a_ref[...], (((1,), (1,)), ((), ())),
            preferred_element_type=jnp.float32,
        ).astype(mixed.dtype)

    def compute_and_send(s, carry):
        peer = lax.rem(me + s, n)
        compute(peer)
        piece(s, peer, me).start()
        return carry

    lax.fori_loop(1, n, compute_and_send, 0)
    compute(me)
    local = pltpu.make_async_copy(mixed.at[me], o_ref.at[me], local_sems.at[0])
    local.start()

    def spread(s, peer, slot):
        return pltpu.make_async_remote_copy(
            src_ref=rounded, dst_ref=full_ref.at[slot],
            send_sem=sems.at[2, s], recv_sem=sems.at[3, s],
            device_id=(row, peer), device_id_type=MESH_ID,
        )

    for s, peer, source in row_peers:
        part(s, peer, row).wait_send()
        part(s, source, source).wait_recv()
    own.wait()
    total[...] = jnp.sum(rows_got[...], axis=0)
    rounded[...] = total[...].astype(rounded.dtype)
    mine = pltpu.make_async_copy(rounded, full_ref.at[me], local_sems.at[2])
    mine.start()
    for s, peer, _ in col_peers(n):
        spread(s, peer, me).start()


    for s, peer, source in col_peers(n):
        spread(s, peer, me).wait_send()
        spread(s, source, source).wait_recv()
        piece(s, peer, me).wait_send()
        piece(s, source, source).wait_recv()
    mine.wait()
    local.wait()
    for sib in sibs:
        sib.wait()


def gather(a, w, share, c1, p, staged, n, m):
    piece_rows = w.shape[0] // n
    columns = a.shape[0]
    return pl.pallas_call(
        functools.partial(gather_kernel, n, m),
        out_shape=(
            jax.ShapeDtypeStruct((n, piece_rows, columns), a.dtype),
            jax.ShapeDtypeStruct((n,) + share.shape, jnp.bfloat16),
            jax.ShapeDtypeStruct(c1.shape, c1.dtype),
            jax.ShapeDtypeStruct(p.shape, p.dtype),
        ),
        in_specs=[
            pl.BlockSpec(memory_space=pltpu.VMEM),
            pl.BlockSpec(memory_space=pltpu.VMEM),
            pl.BlockSpec(memory_space=pltpu.VMEM),
            pl.BlockSpec(memory_space=pl.ANY),
            pl.BlockSpec(memory_space=pl.ANY),
        ]
        + [pl.BlockSpec(memory_space=pltpu.VMEM)] * len(staged),
        out_specs=(
            pl.BlockSpec(memory_space=pl.ANY),
            pl.BlockSpec(memory_space=pltpu.VMEM),
            pl.BlockSpec(memory_space=pl.ANY),
            pl.BlockSpec(memory_space=pl.ANY),
        ),
        scratch_shapes=[
            pltpu.VMEM((n, piece_rows, columns), a.dtype),
            pltpu.VMEM((m,) + share.shape, share.dtype),
            pltpu.VMEM(share.shape, share.dtype),
            pltpu.VMEM(share.shape, jnp.bfloat16),
            pltpu.SemaphoreType.DMA((4, n)),
            pltpu.SemaphoreType.DMA((2, m)),
            pltpu.SemaphoreType.DMA((3,)),
            pltpu.SemaphoreType.DMA((2, 2)),
        ],
        compiler_params=pltpu.CompilerParams(
            collective_id=1, has_side_effects=True, vmem_limit_bytes=48 * 1024 * 1024
        ),
    )(a, w, share, c1, p, *staged)


def per_device(
    right_side,
    leaf_inverse,
    compress,
    middle,
    expand,
    row_project,
    row_expand,
    root_project,
    root_expand,
    owner_map,
):
    lowered = right_side.astype(jnp.bfloat16)
    columns = lowered.shape[1]
    root_term = lax.dot_general(
        lowered, root_project, contract_first, preferred_element_type=jnp.float32
    )
    level_coeffs = jnp.einsum(
        "lw,blr->bwr", lowered, row_project, preferred_element_type=jnp.float32
    )
    coeffs = lax.dot_general(
        lowered, compress, contract_first, preferred_element_type=jnp.float32
    ).astype(jnp.bfloat16)
    col_count = lax.axis_size("col")
    pieces = coeffs.reshape(columns, col_count, -1)
    chosen = (owner_map[:, None] == jnp.arange(col_count, dtype=owner_map.dtype)[None, :]).astype(
        jnp.bfloat16
    )
    outgoing = jnp.einsum(
        "kd,wkx->wdx", chosen, pieces, preferred_element_type=jnp.float32
    ).astype(jnp.bfloat16)
    root_shares = root_term.reshape(col_count, -1, root_term.shape[1])
    arrived, root_share, pair, far, dense_part = scatter(
        outgoing.reshape(columns, -1), root_shares, level_coeffs, expand, leaf_inverse, lowered
    )
    pair_sum = (level_coeffs[1] + pair[1]).astype(jnp.bfloat16)
    far_sum = far[0] + far[1]
    returned, root_full, quad_one, quad_two = gather(
        arrived, middle, root_share, pair_sum, far_sum, (row_expand, root_expand), col_count,
        lax.axis_size("row"),
    )
    ordered = jnp.einsum(
        "jd,dxw->jxw", chosen, returned, preferred_element_type=jnp.float32
    ).astype(jnp.bfloat16).reshape(-1, columns)
    cluster_part = jnp.dot(expand, ordered, preferred_element_type=jnp.float32)

    sibling_sum = jnp.stack(
        [pair[0], quad_one.astype(jnp.float32), far_sum + quad_two], axis=0
    )
    root_coeffs = root_full.reshape(columns, -1)
    coupled = jnp.einsum(
        "blr,bwr->lw",
        row_expand,
        sibling_sum.astype(jnp.bfloat16),
        preferred_element_type=jnp.float32,
    )
    root_part = lax.dot_general(
        root_expand, root_coeffs, (((1,), (1,)), ((), ())), preferred_element_type=jnp.float32
    )
    return dense_part + cluster_part + coupled + root_part


def solution(mesh):
    in_specs = (
        P(("row", "col"), None),
        P(("row", "col"), None),
        P(("row", "col"), None),
        P(("row", "col"), None),
        P(("row", "col"), None),
        P(None, ("row", "col"), None),
        P(None, ("row", "col"), None),
        P(("row", "col"), None),
        P(("row", "col"), None),
        P(),
    )
    out_specs = P(("row", "col"), None)
    return jax.shard_map(
        per_device, mesh=mesh, in_specs=in_specs, out_specs=out_specs, check_vma=False
    )
```

```python
import functools

import jax
import jax.numpy as jnp
from jax import lax
from jax.experimental import pallas as pl
from jax.experimental.pallas import tpu as pltpu
from jax.sharding import PartitionSpec as P

contract_first = (((0,), (0,)), ((), ()))
MESH_ID = pl.DeviceIdType.MESH


def swapped(x, axis, bit):
    return lax.ppermute(x, axis, [(i, i ^ 1 << bit) for i in range(lax.axis_size(axis))])


def flipped(index, bit):
    return index + bit - 2 * bit * lax.rem(index // bit, 2)


def col_peers(n):
    me = lax.axis_index("col")
    return [(s, lax.rem(me + s, n), lax.rem(me + n - s, n)) for s in range(1, n)]


def scatter_kernel(
    n, x_ref, r_ref, lv_ref, e0_ref, li_ref, y_ref, o_ref, share_ref, pair_ref, far_ref, d_ref,
    got, sems, local_sems, pair_sems,
):
    me = lax.axis_index("col")
    row = lax.axis_index("row")
    width = x_ref.shape[1] // n
    barrier = pltpu.get_barrier_semaphore()
    for s, peer, _ in col_peers(n):
        pl.semaphore_signal(barrier, inc=1, device_id=(row, peer), device_id_type=MESH_ID)
    partner = flipped(row, 1)
    far = [flipped(row, 4), flipped(flipped(row, 4), 2)]
    for peer in [partner] + far:
        pl.semaphore_signal(barrier, inc=1, device_id=(peer, me), device_id_type=MESH_ID)
    pl.semaphore_wait(barrier, n + 2)

    low = pair_ref.shape[0]
    level_copies = [
        pltpu.make_async_remote_copy(
            src_ref=lv_ref.at[pl.ds(0, low)], dst_ref=pair_ref,
            send_sem=pair_sems.at[0, 0], recv_sem=pair_sems.at[1, 0],
            device_id=(partner, me), device_id_type=MESH_ID,
        )
    ]
    for i, peer in enumerate(far):
        level_copies.append(
            pltpu.make_async_remote_copy(
                src_ref=lv_ref.at[low], dst_ref=far_ref.at[i],
                send_sem=pair_sems.at[0, i + 1], recv_sem=pair_sems.at[1, i + 1],
                device_id=(peer, me), device_id_type=MESH_ID,
            )
        )
    for copy in level_copies:
        copy.start()
    local = pltpu.make_async_copy(
        x_ref.at[:, pl.ds(me * width, width)], o_ref.at[:, pl.ds(me * width, width)],
        local_sems.at[0],
    )
    local.start()
    own = pltpu.make_async_copy(r_ref.at[me], got.at[me], local_sems.at[1])
    own.start()

    def piece(s, peer, slot):
        return pltpu.make_async_remote_copy(
            src_ref=x_ref.at[:, pl.ds(peer * width, width)],
            dst_ref=o_ref.at[:, pl.ds(slot * width, width)],
            send_sem=sems.at[0, s], recv_sem=sems.at[1, s],
            device_id=(row, peer), device_id_type=MESH_ID,
        )

    def share(s, peer, slot):
        return pltpu.make_async_remote_copy(
            src_ref=r_ref.at[peer], dst_ref=got.at[slot],
            send_sem=sems.at[2, s], recv_sem=sems.at[3, s],
            device_id=(row, peer), device_id_type=MESH_ID,
        )

    for s, peer, _ in col_peers(n):
        piece(s, peer, me).start()
    for s, peer, _ in col_peers(n):
        share(s, peer, me).start()
    d_ref[...] = jnp.dot(li_ref[...], y_ref[...], preferred_element_type=jnp.float32)
    for s, peer, source in col_peers(n):
        share(s, peer, me).wait_send()
        share(s, source, source).wait_recv()
    own.wait()
    share_ref[...] = jnp.sum(got[...], axis=0)
    for s, peer, source in col_peers(n):
        piece(s, peer, me).wait_send()
        piece(s, source, source).wait_recv()
    local.wait()
    for copy in level_copies:
        copy.wait()


def scatter(x, r, lv, staged, li, y):
    n = r.shape[0]
    return pl.pallas_call(
        functools.partial(scatter_kernel, n),
        out_shape=(
            jax.ShapeDtypeStruct(x.shape, x.dtype),
            jax.ShapeDtypeStruct(r.shape[1:], r.dtype),
            jax.ShapeDtypeStruct((lv.shape[0] - 1,) + lv.shape[1:], lv.dtype),
            jax.ShapeDtypeStruct((2,) + lv.shape[1:], lv.dtype),
            jax.ShapeDtypeStruct((li.shape[0], y.shape[1]), jnp.float32),
        ),
        in_specs=[
            pl.BlockSpec(memory_space=pl.ANY),
            pl.BlockSpec(memory_space=pltpu.VMEM),
            pl.BlockSpec(memory_space=pl.ANY),
            pl.BlockSpec(memory_space=pltpu.VMEM),
            pl.BlockSpec(memory_space=pltpu.VMEM),
            pl.BlockSpec(memory_space=pltpu.VMEM),
        ],
        out_specs=(
            pl.BlockSpec(memory_space=pl.ANY),
            pl.BlockSpec(memory_space=pltpu.VMEM),
            pl.BlockSpec(memory_space=pl.ANY),
            pl.BlockSpec(memory_space=pl.ANY),
            pl.BlockSpec(memory_space=pltpu.VMEM),
        ),
        scratch_shapes=[
            pltpu.VMEM(r.shape, r.dtype),
            pltpu.SemaphoreType.DMA((4, n)),
            pltpu.SemaphoreType.DMA((2,)),
            pltpu.SemaphoreType.DMA((2, 3)),
        ],
        compiler_params=pltpu.CompilerParams(
            collective_id=0, has_side_effects=True, vmem_limit_bytes=4 * 1024 * 1024
        ),
    )(x, r, lv, staged, li, y)


def gather_kernel(
    n, m, a_ref, w_ref, share_ref, c1_ref, p_ref, e2_ref, e3_ref, o_ref, full_ref, got1, got2,
    mixed, rows_got, total, rounded, sems, row_sems, local_sems, sib_sems,
):
    me = lax.axis_index("col")
    row = lax.axis_index("row")
    piece_rows = mixed.shape[1]
    row_peers = [(s, lax.rem(row + s, m), lax.rem(row + m - s, m)) for s in range(1, m)]
    barrier = pltpu.get_barrier_semaphore()
    for s, peer, _ in col_peers(n):
        pl.semaphore_signal(barrier, inc=1, device_id=(row, peer), device_id_type=MESH_ID)
    for s, peer, _ in row_peers:
        pl.semaphore_signal(barrier, inc=1, device_id=(peer, me), device_id_type=MESH_ID)
    pl.semaphore_wait(barrier, n - 1 + m - 1)

    own = pltpu.make_async_copy(share_ref, rows_got.at[row], local_sems.at[1])
    own.start()
    sends = [(c1_ref, got1, flipped(row, 2)), (p_ref, got2, flipped(row, 1))]
    sibs = []
    for i, (src_ref, dst_ref, peer) in enumerate(sends):
        sib = pltpu.make_async_remote_copy(
            src_ref=src_ref, dst_ref=dst_ref,
            send_sem=sib_sems.at[0, i], recv_sem=sib_sems.at[1, i],
            device_id=(peer, me), device_id_type=MESH_ID,
        )
        sib.start()
        sibs.append(sib)

    def part(s, peer, slot):
        return pltpu.make_async_remote_copy(
            src_ref=share_ref, dst_ref=rows_got.at[slot],
            send_sem=row_sems.at[0, s], recv_sem=row_sems.at[1, s],
            device_id=(peer, me), device_id_type=MESH_ID,
        )

    for s, peer, _ in row_peers:
        part(s, peer, row).start()

    def piece(s, peer, slot):
        return pltpu.make_async_remote_copy(
            src_ref=mixed.at[peer], dst_ref=o_ref.at[slot],
            send_sem=sems.at[0, s], recv_sem=sems.at[1, s],
            device_id=(row, peer), device_id_type=MESH_ID,
        )

    def compute(peer):
        first = pl.multiple_of(peer * piece_rows, piece_rows)
        mixed[peer] = lax.dot_general(
            w_ref[pl.ds(first, piece_rows), :], a_ref[...], (((1,), (1,)), ((), ())),
            preferred_element_type=jnp.float32,
        ).astype(mixed.dtype)

    def compute_and_send(s, carry):
        peer = lax.rem(me + s, n)
        compute(peer)
        piece(s, peer, me).start()
        return carry

    half = n
    lax.fori_loop(1, half, compute_and_send, 0)

    def spread(s, peer, slot):
        return pltpu.make_async_remote_copy(
            src_ref=rounded, dst_ref=full_ref.at[slot],
            send_sem=sems.at[2, s], recv_sem=sems.at[3, s],
            device_id=(row, peer), device_id_type=MESH_ID,
        )

    for s, peer, source in row_peers:
        part(s, peer, row).wait_send()
        part(s, source, source).wait_recv()
    own.wait()
    total[...] = jnp.sum(rows_got[...], axis=0)
    rounded[...] = total[...].astype(rounded.dtype)
    mine = pltpu.make_async_copy(rounded, full_ref.at[me], local_sems.at[2])
    mine.start()
    for s, peer, _ in col_peers(n):
        spread(s, peer, me).start()

    lax.fori_loop(half, n, compute_and_send, 0)
    compute(me)
    local = pltpu.make_async_copy(mixed.at[me], o_ref.at[me], local_sems.at[0])
    local.start()

    for s, peer, source in col_peers(n):
        spread(s, peer, me).wait_send()
        spread(s, source, source).wait_recv()
        piece(s, peer, me).wait_send()
        piece(s, source, source).wait_recv()
    mine.wait()
    local.wait()
    for sib in sibs:
        sib.wait()


def gather(a, w, share, c1, p, staged, n, m):
    piece_rows = w.shape[0] // n
    columns = a.shape[0]
    return pl.pallas_call(
        functools.partial(gather_kernel, n, m),
        out_shape=(
            jax.ShapeDtypeStruct((n, piece_rows, columns), a.dtype),
            jax.ShapeDtypeStruct((n,) + share.shape, jnp.bfloat16),
            jax.ShapeDtypeStruct(c1.shape, c1.dtype),
            jax.ShapeDtypeStruct(p.shape, p.dtype),
        ),
        in_specs=[
            pl.BlockSpec(memory_space=pltpu.VMEM),
            pl.BlockSpec(memory_space=pltpu.VMEM),
            pl.BlockSpec(memory_space=pltpu.VMEM),
            pl.BlockSpec(memory_space=pl.ANY),
            pl.BlockSpec(memory_space=pl.ANY),
        ]
        + [pl.BlockSpec(memory_space=pltpu.VMEM)] * len(staged),
        out_specs=(
            pl.BlockSpec(memory_space=pl.ANY),
            pl.BlockSpec(memory_space=pltpu.VMEM),
            pl.BlockSpec(memory_space=pl.ANY),
            pl.BlockSpec(memory_space=pl.ANY),
        ),
        scratch_shapes=[
            pltpu.VMEM((n, piece_rows, columns), a.dtype),
            pltpu.VMEM((m,) + share.shape, share.dtype),
            pltpu.VMEM(share.shape, share.dtype),
            pltpu.VMEM(share.shape, jnp.bfloat16),
            pltpu.SemaphoreType.DMA((4, n)),
            pltpu.SemaphoreType.DMA((2, m)),
            pltpu.SemaphoreType.DMA((3,)),
            pltpu.SemaphoreType.DMA((2, 2)),
        ],
        compiler_params=pltpu.CompilerParams(
            collective_id=1, has_side_effects=True, vmem_limit_bytes=48 * 1024 * 1024
        ),
    )(a, w, share, c1, p, *staged)


def per_device(
    right_side,
    leaf_inverse,
    compress,
    middle,
    expand,
    row_project,
    row_expand,
    root_project,
    root_expand,
    owner_map,
):
    lowered = right_side.astype(jnp.bfloat16)
    columns = lowered.shape[1]
    root_term = lax.dot_general(
        lowered, root_project, contract_first, preferred_element_type=jnp.float32
    )
    level_coeffs = jnp.einsum(
        "lw,blr->bwr", lowered, row_project, preferred_element_type=jnp.float32
    )
    coeffs = lax.dot_general(
        lowered, compress, contract_first, preferred_element_type=jnp.float32
    ).astype(jnp.bfloat16)
    col_count = lax.axis_size("col")
    pieces = coeffs.reshape(columns, col_count, -1)
    chosen = (owner_map[:, None] == jnp.arange(col_count, dtype=owner_map.dtype)[None, :]).astype(
        jnp.bfloat16
    )
    outgoing = jnp.einsum(
        "kd,wkx->wdx", chosen, pieces, preferred_element_type=jnp.float32
    ).astype(jnp.bfloat16)
    root_shares = root_term.reshape(col_count, -1, root_term.shape[1])
    arrived, root_share, pair, far, dense_part = scatter(
        outgoing.reshape(columns, -1), root_shares, level_coeffs, expand, leaf_inverse, lowered
    )
    pair_sum = (level_coeffs[1] + pair[1]).astype(jnp.bfloat16)
    far_sum = far[0] + far[1]
    returned, root_full, quad_one, quad_two = gather(
        arrived, middle, root_share, pair_sum, far_sum, (row_expand, root_expand), col_count,
        lax.axis_size("row"),
    )
    ordered = jnp.einsum(
        "jd,dxw->jxw", chosen, returned, preferred_element_type=jnp.float32
    ).astype(jnp.bfloat16).reshape(-1, columns)
    cluster_part = jnp.dot(expand, ordered, preferred_element_type=jnp.float32)

    sibling_sum = jnp.stack(
        [pair[0], quad_one.astype(jnp.float32), far_sum + quad_two], axis=0
    )
    root_coeffs = root_full.reshape(columns, -1)
    coupled = jnp.einsum(
        "blr,bwr->lw",
        row_expand,
        sibling_sum.astype(jnp.bfloat16),
        preferred_element_type=jnp.float32,
    )
    root_part = lax.dot_general(
        root_expand, root_coeffs, (((1,), (1,)), ((), ())), preferred_element_type=jnp.float32
    )
    return dense_part + cluster_part + coupled + root_part


def solution(mesh):
    in_specs = (
        P(("row", "col"), None),
        P(("row", "col"), None),
        P(("row", "col"), None),
        P(("row", "col"), None),
        P(("row", "col"), None),
        P(None, ("row", "col"), None),
        P(None, ("row", "col"), None),
        P(("row", "col"), None),
        P(("row", "col"), None),
        P(),
    )
    out_specs = P(("row", "col"), None)
    return jax.shard_map(
        per_device, mesh=mesh, in_specs=in_specs, out_specs=out_specs, check_vma=False
    )
```

```python
import functools

import jax
import jax.numpy as jnp
from jax import lax
from jax.experimental import pallas as pl
from jax.experimental.pallas import tpu as pltpu
from jax.sharding import PartitionSpec as P

contract_first = (((0,), (0,)), ((), ()))
MESH_ID = pl.DeviceIdType.MESH


def swapped(x, axis, bit):
    return lax.ppermute(x, axis, [(i, i ^ 1 << bit) for i in range(lax.axis_size(axis))])


def flipped(index, bit):
    return index + bit - 2 * bit * lax.rem(index // bit, 2)


def col_peers(n):
    me = lax.axis_index("col")
    return [(s, lax.rem(me + s, n), lax.rem(me + n - s, n)) for s in range(1, n)]


def scatter_kernel(
    n, x_ref, r_ref, lv_ref, e0_ref, li_ref, y_ref, o_ref, share_ref, pair_ref, far_ref, d_ref,
    got, sems, local_sems, pair_sems,
):
    me = lax.axis_index("col")
    row = lax.axis_index("row")
    width = x_ref.shape[1] // n
    barrier = pltpu.get_barrier_semaphore()
    for s, peer, _ in col_peers(n):
        pl.semaphore_signal(barrier, inc=1, device_id=(row, peer), device_id_type=MESH_ID)
    partner = flipped(row, 1)
    far = [flipped(row, 4), flipped(flipped(row, 4), 2)]
    for peer in [partner] + far:
        pl.semaphore_signal(barrier, inc=1, device_id=(peer, me), device_id_type=MESH_ID)
    pl.semaphore_wait(barrier, n + 2)

    low = pair_ref.shape[0]
    level_copies = [
        pltpu.make_async_remote_copy(
            src_ref=lv_ref.at[pl.ds(0, low)], dst_ref=pair_ref,
            send_sem=pair_sems.at[0, 0], recv_sem=pair_sems.at[1, 0],
            device_id=(partner, me), device_id_type=MESH_ID,
        )
    ]
    for i, peer in enumerate(far):
        level_copies.append(
            pltpu.make_async_remote_copy(
                src_ref=lv_ref.at[low], dst_ref=far_ref.at[i],
                send_sem=pair_sems.at[0, i + 1], recv_sem=pair_sems.at[1, i + 1],
                device_id=(peer, me), device_id_type=MESH_ID,
            )
        )
    for copy in level_copies:
        copy.start()
    local = pltpu.make_async_copy(
        x_ref.at[:, pl.ds(me * width, width)], o_ref.at[:, pl.ds(me * width, width)],
        local_sems.at[0],
    )
    local.start()
    own = pltpu.make_async_copy(r_ref.at[me], got.at[me], local_sems.at[1])
    own.start()

    def piece(s, peer, slot):
        return pltpu.make_async_remote_copy(
            src_ref=x_ref.at[:, pl.ds(peer * width, width)],
            dst_ref=o_ref.at[:, pl.ds(slot * width, width)],
            send_sem=sems.at[0, s], recv_sem=sems.at[1, s],
            device_id=(row, peer), device_id_type=MESH_ID,
        )

    def share(s, peer, slot):
        return pltpu.make_async_remote_copy(
            src_ref=r_ref.at[peer], dst_ref=got.at[slot],
            send_sem=sems.at[2, s], recv_sem=sems.at[3, s],
            device_id=(row, peer), device_id_type=MESH_ID,
        )

    for s, peer, _ in col_peers(n):
        share(s, peer, me).start()
        piece(s, peer, me).start()
    d_ref[...] = jnp.dot(li_ref[...], y_ref[...], preferred_element_type=jnp.float32)
    for s, peer, source in col_peers(n):
        share(s, peer, me).wait_send()
        share(s, source, source).wait_recv()
    own.wait()
    share_ref[...] = jnp.sum(got[...], axis=0)
    for s, peer, source in col_peers(n):
        piece(s, peer, me).wait_send()
        piece(s, source, source).wait_recv()
    local.wait()
    for copy in level_copies:
        copy.wait()


def scatter(x, r, lv, staged, li, y):
    n = r.shape[0]
    return pl.pallas_call(
        functools.partial(scatter_kernel, n),
        out_shape=(
            jax.ShapeDtypeStruct(x.shape, x.dtype),
            jax.ShapeDtypeStruct(r.shape[1:], r.dtype),
            jax.ShapeDtypeStruct((lv.shape[0] - 1,) + lv.shape[1:], lv.dtype),
            jax.ShapeDtypeStruct((2,) + lv.shape[1:], lv.dtype),
            jax.ShapeDtypeStruct((li.shape[0], y.shape[1]), jnp.float32),
        ),
        in_specs=[
            pl.BlockSpec(memory_space=pl.ANY),
            pl.BlockSpec(memory_space=pltpu.VMEM),
            pl.BlockSpec(memory_space=pl.ANY),
            pl.BlockSpec(memory_space=pltpu.VMEM),
            pl.BlockSpec(memory_space=pltpu.VMEM),
            pl.BlockSpec(memory_space=pltpu.VMEM),
        ],
        out_specs=(
            pl.BlockSpec(memory_space=pl.ANY),
            pl.BlockSpec(memory_space=pltpu.VMEM),
            pl.BlockSpec(memory_space=pl.ANY),
            pl.BlockSpec(memory_space=pl.ANY),
            pl.BlockSpec(memory_space=pltpu.VMEM),
        ),
        scratch_shapes=[
            pltpu.VMEM(r.shape, r.dtype),
            pltpu.SemaphoreType.DMA((4, n)),
            pltpu.SemaphoreType.DMA((2,)),
            pltpu.SemaphoreType.DMA((2, 3)),
        ],
        compiler_params=pltpu.CompilerParams(
            collective_id=0, has_side_effects=True, vmem_limit_bytes=4 * 1024 * 1024
        ),
    )(x, r, lv, staged, li, y)


def gather_kernel(
    n, m, a_ref, w_ref, share_ref, c1_ref, p_ref, e2_ref, e3_ref, o_ref, full_ref, got1, got2,
    mixed, rows_got, total, rounded, sems, row_sems, local_sems, sib_sems,
):
    me = lax.axis_index("col")
    row = lax.axis_index("row")
    piece_rows = mixed.shape[1]
    row_peers = [(s, lax.rem(row + s, m), lax.rem(row + m - s, m)) for s in range(1, m)]
    barrier = pltpu.get_barrier_semaphore()
    for s, peer, _ in col_peers(n):
        pl.semaphore_signal(barrier, inc=1, device_id=(row, peer), device_id_type=MESH_ID)
    for s, peer, _ in row_peers:
        pl.semaphore_signal(barrier, inc=1, device_id=(peer, me), device_id_type=MESH_ID)
    pl.semaphore_wait(barrier, n - 1 + m - 1)

    own = pltpu.make_async_copy(share_ref, rows_got.at[row], local_sems.at[1])
    own.start()
    sends = [(c1_ref, got1, flipped(row, 2)), (p_ref, got2, flipped(row, 1))]
    sibs = []
    for i, (src_ref, dst_ref, peer) in enumerate(sends):
        sib = pltpu.make_async_remote_copy(
            src_ref=src_ref, dst_ref=dst_ref,
            send_sem=sib_sems.at[0, i], recv_sem=sib_sems.at[1, i],
            device_id=(peer, me), device_id_type=MESH_ID,
        )
        sib.start()
        sibs.append(sib)

    def part(s, peer, slot):
        return pltpu.make_async_remote_copy(
            src_ref=share_ref, dst_ref=rows_got.at[slot],
            send_sem=row_sems.at[0, s], recv_sem=row_sems.at[1, s],
            device_id=(peer, me), device_id_type=MESH_ID,
        )

    for s, peer, _ in row_peers:
        part(s, peer, row).start()

    def piece(s, peer, slot):
        return pltpu.make_async_remote_copy(
            src_ref=mixed.at[peer], dst_ref=o_ref.at[slot],
            send_sem=sems.at[0, s], recv_sem=sems.at[1, s],
            device_id=(row, peer), device_id_type=MESH_ID,
        )

    def compute(peer):
        first = pl.multiple_of(peer * piece_rows, piece_rows)
        mixed[peer] = lax.dot_general(
            w_ref[pl.ds(first, piece_rows), :], a_ref[...], (((1,), (1,)), ((), ())),
            preferred_element_type=jnp.float32,
        ).astype(mixed.dtype)

    def compute_and_send(s, carry):
        peer = lax.rem(me + s, n)
        compute(peer)
        piece(s, peer, me).start()
        return carry

    half = n
    lax.fori_loop(1, half, compute_and_send, 0)

    def spread(s, peer, slot):
        return pltpu.make_async_remote_copy(
            src_ref=rounded, dst_ref=full_ref.at[slot],
            send_sem=sems.at[2, s], recv_sem=sems.at[3, s],
            device_id=(row, peer), device_id_type=MESH_ID,
        )

    for s, peer, source in row_peers:
        part(s, peer, row).wait_send()
        part(s, source, source).wait_recv()
    own.wait()
    total[...] = jnp.sum(rows_got[...], axis=0)
    rounded[...] = total[...].astype(rounded.dtype)
    mine = pltpu.make_async_copy(rounded, full_ref.at[me], local_sems.at[2])
    mine.start()
    for s, peer, _ in col_peers(n):
        spread(s, peer, me).start()

    lax.fori_loop(half, n, compute_and_send, 0)
    compute(me)
    local = pltpu.make_async_copy(mixed.at[me], o_ref.at[me], local_sems.at[0])
    local.start()

    for s, peer, source in col_peers(n):
        spread(s, peer, me).wait_send()
        spread(s, source, source).wait_recv()
        piece(s, peer, me).wait_send()
        piece(s, source, source).wait_recv()
    mine.wait()
    local.wait()
    for sib in sibs:
        sib.wait()


def gather(a, w, share, c1, p, staged, n, m):
    piece_rows = w.shape[0] // n
    columns = a.shape[0]
    return pl.pallas_call(
        functools.partial(gather_kernel, n, m),
        out_shape=(
            jax.ShapeDtypeStruct((n, piece_rows, columns), a.dtype),
            jax.ShapeDtypeStruct((n,) + share.shape, jnp.bfloat16),
            jax.ShapeDtypeStruct(c1.shape, c1.dtype),
            jax.ShapeDtypeStruct(p.shape, p.dtype),
        ),
        in_specs=[
            pl.BlockSpec(memory_space=pltpu.VMEM),
            pl.BlockSpec(memory_space=pltpu.VMEM),
            pl.BlockSpec(memory_space=pltpu.VMEM),
            pl.BlockSpec(memory_space=pl.ANY),
            pl.BlockSpec(memory_space=pl.ANY),
        ]
        + [pl.BlockSpec(memory_space=pltpu.VMEM)] * len(staged),
        out_specs=(
            pl.BlockSpec(memory_space=pl.ANY),
            pl.BlockSpec(memory_space=pltpu.VMEM),
            pl.BlockSpec(memory_space=pl.ANY),
            pl.BlockSpec(memory_space=pl.ANY),
        ),
        scratch_shapes=[
            pltpu.VMEM((n, piece_rows, columns), a.dtype),
            pltpu.VMEM((m,) + share.shape, share.dtype),
            pltpu.VMEM(share.shape, share.dtype),
            pltpu.VMEM(share.shape, jnp.bfloat16),
            pltpu.SemaphoreType.DMA((4, n)),
            pltpu.SemaphoreType.DMA((2, m)),
            pltpu.SemaphoreType.DMA((3,)),
            pltpu.SemaphoreType.DMA((2, 2)),
        ],
        compiler_params=pltpu.CompilerParams(
            collective_id=1, has_side_effects=True, vmem_limit_bytes=16 * 1024 * 1024
        ),
    )(a, w, share, c1, p, *staged)


def per_device(
    right_side,
    leaf_inverse,
    compress,
    middle,
    expand,
    row_project,
    row_expand,
    root_project,
    root_expand,
    owner_map,
):
    lowered = right_side.astype(jnp.bfloat16)
    columns = lowered.shape[1]
    root_term = lax.dot_general(
        lowered, root_project, contract_first, preferred_element_type=jnp.float32
    )
    level_coeffs = jnp.einsum(
        "lw,blr->bwr", lowered, row_project, preferred_element_type=jnp.float32
    )
    coeffs = lax.dot_general(
        lowered, compress, contract_first, preferred_element_type=jnp.float32
    ).astype(jnp.bfloat16)
    col_count = lax.axis_size("col")
    pieces = coeffs.reshape(columns, col_count, -1)
    chosen = (owner_map[:, None] == jnp.arange(col_count, dtype=owner_map.dtype)[None, :]).astype(
        jnp.bfloat16
    )
    outgoing = jnp.einsum(
        "kd,wkx->wdx", chosen, pieces, preferred_element_type=jnp.float32
    ).astype(jnp.bfloat16)
    root_shares = root_term.reshape(col_count, -1, root_term.shape[1])
    arrived, root_share, pair, far, dense_part = scatter(
        outgoing.reshape(columns, -1), root_shares, level_coeffs, expand, leaf_inverse, lowered
    )
    pair_sum = (level_coeffs[1] + pair[1]).astype(jnp.bfloat16)
    far_sum = far[0] + far[1]
    returned, root_full, quad_one, quad_two = gather(
        arrived, middle, root_share, pair_sum, far_sum, (row_expand, root_expand), col_count,
        lax.axis_size("row"),
    )
    ordered = jnp.einsum(
        "jd,dxw->jxw", chosen, returned, preferred_element_type=jnp.float32
    ).astype(jnp.bfloat16).reshape(-1, columns)
    cluster_part = jnp.dot(expand, ordered, preferred_element_type=jnp.float32)

    sibling_sum = jnp.stack(
        [pair[0], quad_one.astype(jnp.float32), far_sum + quad_two], axis=0
    )
    root_coeffs = root_full.reshape(columns, -1)
    coupled = jnp.einsum(
        "blr,bwr->lw",
        row_expand,
        sibling_sum.astype(jnp.bfloat16),
        preferred_element_type=jnp.float32,
    )
    root_part = lax.dot_general(
        root_expand, root_coeffs, (((1,), (1,)), ((), ())), preferred_element_type=jnp.float32
    )
    return dense_part + cluster_part + coupled + root_part


def solution(mesh):
    in_specs = (
        P(("row", "col"), None),
        P(("row", "col"), None),
        P(("row", "col"), None),
        P(("row", "col"), None),
        P(("row", "col"), None),
        P(None, ("row", "col"), None),
        P(None, ("row", "col"), None),
        P(("row", "col"), None),
        P(("row", "col"), None),
        P(),
    )
    out_specs = P(("row", "col"), None)
    return jax.shard_map(
        per_device, mesh=mesh, in_specs=in_specs, out_specs=out_specs, check_vma=False
    )
```

```python
import functools

import jax
import jax.numpy as jnp
from jax import lax
from jax.experimental import pallas as pl
from jax.experimental.pallas import tpu as pltpu
from jax.sharding import PartitionSpec as P

contract_first = (((0,), (0,)), ((), ()))
MESH_ID = pl.DeviceIdType.MESH


def swapped(x, axis, bit):
    return lax.ppermute(x, axis, [(i, i ^ 1 << bit) for i in range(lax.axis_size(axis))])


def flipped(index, bit):
    return index + bit - 2 * bit * lax.rem(index // bit, 2)


def col_peers(n):
    me = lax.axis_index("col")
    return [(s, lax.rem(me + s, n), lax.rem(me + n - s, n)) for s in range(1, n)]


def scatter_kernel(
    n, x_ref, r_ref, lv_ref, e0_ref, li_ref, y_ref, o_ref, share_ref, pair_ref, far_ref, d_ref,
    got, sems, local_sems, pair_sems,
):
    me = lax.axis_index("col")
    row = lax.axis_index("row")
    width = x_ref.shape[1] // n
    barrier = pltpu.get_barrier_semaphore()
    for s, peer, _ in col_peers(n):
        pl.semaphore_signal(barrier, inc=1, device_id=(row, peer), device_id_type=MESH_ID)
    partner = flipped(row, 1)
    far = [flipped(row, 4), flipped(flipped(row, 4), 2)]
    for peer in [partner] + far:
        pl.semaphore_signal(barrier, inc=1, device_id=(peer, me), device_id_type=MESH_ID)
    pl.semaphore_wait(barrier, n + 2)

    low = pair_ref.shape[0]
    level_copies = [
        pltpu.make_async_remote_copy(
            src_ref=lv_ref.at[pl.ds(0, low)], dst_ref=pair_ref,
            send_sem=pair_sems.at[0, 0], recv_sem=pair_sems.at[1, 0],
            device_id=(partner, me), device_id_type=MESH_ID,
        )
    ]
    for i, peer in enumerate(far):
        level_copies.append(
            pltpu.make_async_remote_copy(
                src_ref=lv_ref.at[low], dst_ref=far_ref.at[i],
                send_sem=pair_sems.at[0, i + 1], recv_sem=pair_sems.at[1, i + 1],
                device_id=(peer, me), device_id_type=MESH_ID,
            )
        )
    for copy in level_copies:
        copy.start()
    local = pltpu.make_async_copy(
        x_ref.at[:, pl.ds(me * width, width)], o_ref.at[:, pl.ds(me * width, width)],
        local_sems.at[0],
    )
    local.start()
    own = pltpu.make_async_copy(r_ref.at[me], got.at[me], local_sems.at[1])
    own.start()

    def piece(s, peer, slot):
        return pltpu.make_async_remote_copy(
            src_ref=x_ref.at[:, pl.ds(peer * width, width)],
            dst_ref=o_ref.at[:, pl.ds(slot * width, width)],
            send_sem=sems.at[0, s], recv_sem=sems.at[1, s],
            device_id=(row, peer), device_id_type=MESH_ID,
        )

    def share(s, peer, slot):
        return pltpu.make_async_remote_copy(
            src_ref=r_ref.at[peer], dst_ref=got.at[slot],
            send_sem=sems.at[2, s], recv_sem=sems.at[3, s],
            device_id=(row, peer), device_id_type=MESH_ID,
        )

    for s, peer, _ in col_peers(n):
        share(s, peer, me).start()
        piece(s, peer, me).start()
    d_ref[...] = jnp.dot(li_ref[...], y_ref[...], preferred_element_type=jnp.float32)
    for s, peer, source in col_peers(n):
        share(s, peer, me).wait_send()
        share(s, source, source).wait_recv()
    own.wait()
    share_ref[...] = jnp.sum(got[...], axis=0)
    for s, peer, source in col_peers(n):
        piece(s, peer, me).wait_send()
        piece(s, source, source).wait_recv()
    local.wait()
    for copy in level_copies:
        copy.wait()


def scatter(x, r, lv, staged, li, y):
    n = r.shape[0]
    return pl.pallas_call(
        functools.partial(scatter_kernel, n),
        out_shape=(
            jax.ShapeDtypeStruct(x.shape, x.dtype),
            jax.ShapeDtypeStruct(r.shape[1:], r.dtype),
            jax.ShapeDtypeStruct((lv.shape[0] - 1,) + lv.shape[1:], lv.dtype),
            jax.ShapeDtypeStruct((2,) + lv.shape[1:], lv.dtype),
            jax.ShapeDtypeStruct((li.shape[0], y.shape[1]), jnp.float32),
        ),
        in_specs=[
            pl.BlockSpec(memory_space=pl.ANY),
            pl.BlockSpec(memory_space=pltpu.VMEM),
            pl.BlockSpec(memory_space=pl.ANY),
            pl.BlockSpec(memory_space=pltpu.VMEM),
            pl.BlockSpec(memory_space=pltpu.VMEM),
            pl.BlockSpec(memory_space=pltpu.VMEM),
        ],
        out_specs=(
            pl.BlockSpec(memory_space=pl.ANY),
            pl.BlockSpec(memory_space=pltpu.VMEM),
            pl.BlockSpec(memory_space=pl.ANY),
            pl.BlockSpec(memory_space=pl.ANY),
            pl.BlockSpec(memory_space=pltpu.VMEM),
        ),
        scratch_shapes=[
            pltpu.VMEM(r.shape, r.dtype),
            pltpu.SemaphoreType.DMA((4, n)),
            pltpu.SemaphoreType.DMA((2,)),
            pltpu.SemaphoreType.DMA((2, 3)),
        ],
        compiler_params=pltpu.CompilerParams(
            collective_id=0, has_side_effects=True, vmem_limit_bytes=4 * 1024 * 1024
        ),
    )(x, r, lv, staged, li, y)


def gather_kernel(
    n, m, a_ref, w_ref, share_ref, c1_ref, p_ref, e2_ref, e3_ref, o_ref, full_ref, got1, got2,
    mixed, rows_got, total, rounded, sems, row_sems, local_sems, sib_sems,
):
    me = lax.axis_index("col")
    row = lax.axis_index("row")
    piece_rows = mixed.shape[1]
    row_peers = [(s, lax.rem(row + s, m), lax.rem(row + m - s, m)) for s in range(1, m)]
    barrier = pltpu.get_barrier_semaphore()
    for s, peer, _ in col_peers(n):
        pl.semaphore_signal(barrier, inc=1, device_id=(row, peer), device_id_type=MESH_ID)
    for s, peer, _ in row_peers:
        pl.semaphore_signal(barrier, inc=1, device_id=(peer, me), device_id_type=MESH_ID)
    pl.semaphore_wait(barrier, n - 1 + m - 1)

    own = pltpu.make_async_copy(share_ref, rows_got.at[row], local_sems.at[1])
    own.start()
    sends = [(c1_ref, got1, flipped(row, 2)), (p_ref, got2, flipped(row, 1))]
    sibs = []
    for i, (src_ref, dst_ref, peer) in enumerate(sends):
        sib = pltpu.make_async_remote_copy(
            src_ref=src_ref, dst_ref=dst_ref,
            send_sem=sib_sems.at[0, i], recv_sem=sib_sems.at[1, i],
            device_id=(peer, me), device_id_type=MESH_ID,
        )
        sib.start()
        sibs.append(sib)

    def part(s, peer, slot):
        return pltpu.make_async_remote_copy(
            src_ref=share_ref, dst_ref=rows_got.at[slot],
            send_sem=row_sems.at[0, s], recv_sem=row_sems.at[1, s],
            device_id=(peer, me), device_id_type=MESH_ID,
        )

    for s, peer, _ in row_peers:
        part(s, peer, row).start()

    def piece(s, peer, slot):
        return pltpu.make_async_remote_copy(
            src_ref=mixed.at[peer], dst_ref=o_ref.at[slot],
            send_sem=sems.at[0, s], recv_sem=sems.at[1, s],
            device_id=(row, peer), device_id_type=MESH_ID,
        )

    def compute(peer):
        first = pl.multiple_of(peer * piece_rows, piece_rows)
        mixed[peer] = lax.dot_general(
            w_ref[pl.ds(first, piece_rows), :], a_ref[...], (((1,), (1,)), ((), ())),
            preferred_element_type=jnp.float32,
        ).astype(mixed.dtype)

    def compute_and_send(s, carry):
        peer = lax.rem(me + s, n)
        compute(peer)
        piece(s, peer, me).start()
        return carry

    half = n
    lax.fori_loop(1, half, compute_and_send, 0)

    def spread(s, peer, slot):
        return pltpu.make_async_remote_copy(
            src_ref=rounded, dst_ref=full_ref.at[slot],
            send_sem=sems.at[2, s], recv_sem=sems.at[3, s],
            device_id=(row, peer), device_id_type=MESH_ID,
        )

    for s, peer, source in row_peers:
        part(s, peer, row).wait_send()
        part(s, source, source).wait_recv()
    own.wait()
    total[...] = jnp.sum(rows_got[...], axis=0)
    rounded[...] = total[...].astype(rounded.dtype)
    mine = pltpu.make_async_copy(rounded, full_ref.at[me], local_sems.at[2])
    mine.start()
    for s, peer, _ in col_peers(n):
        spread(s, peer, me).start()

    lax.fori_loop(half, n, compute_and_send, 0)
    compute(me)
    local = pltpu.make_async_copy(mixed.at[me], o_ref.at[me], local_sems.at[0])
    local.start()

    for s, peer, source in col_peers(n):
        spread(s, peer, me).wait_send()
        spread(s, source, source).wait_recv()
        piece(s, peer, me).wait_send()
        piece(s, source, source).wait_recv()
    mine.wait()
    local.wait()
    for sib in sibs:
        sib.wait()


def gather(a, w, share, c1, p, staged, n, m):
    piece_rows = w.shape[0] // n
    columns = a.shape[0]
    return pl.pallas_call(
        functools.partial(gather_kernel, n, m),
        out_shape=(
            jax.ShapeDtypeStruct((n, piece_rows, columns), a.dtype),
            jax.ShapeDtypeStruct((n,) + share.shape, jnp.bfloat16),
            jax.ShapeDtypeStruct(c1.shape, c1.dtype),
            jax.ShapeDtypeStruct(p.shape, p.dtype),
        ),
        in_specs=[
            pl.BlockSpec(memory_space=pltpu.VMEM),
            pl.BlockSpec(memory_space=pltpu.VMEM),
            pl.BlockSpec(memory_space=pltpu.VMEM),
            pl.BlockSpec(memory_space=pl.ANY),
            pl.BlockSpec(memory_space=pl.ANY),
        ]
        + [pl.BlockSpec(memory_space=pltpu.VMEM)] * len(staged),
        out_specs=(
            pl.BlockSpec(memory_space=pl.ANY),
            pl.BlockSpec(memory_space=pltpu.VMEM),
            pl.BlockSpec(memory_space=pl.ANY),
            pl.BlockSpec(memory_space=pl.ANY),
        ),
        scratch_shapes=[
            pltpu.VMEM((n, piece_rows, columns), a.dtype),
            pltpu.VMEM((m,) + share.shape, share.dtype),
            pltpu.VMEM(share.shape, share.dtype),
            pltpu.VMEM(share.shape, jnp.bfloat16),
            pltpu.SemaphoreType.DMA((4, n)),
            pltpu.SemaphoreType.DMA((2, m)),
            pltpu.SemaphoreType.DMA((3,)),
            pltpu.SemaphoreType.DMA((2, 2)),
        ],
        compiler_params=pltpu.CompilerParams(
            collective_id=1, has_side_effects=True, vmem_limit_bytes=8 * 1024 * 1024
        ),
    )(a, w, share, c1, p, *staged)


def per_device(
    right_side,
    leaf_inverse,
    compress,
    middle,
    expand,
    row_project,
    row_expand,
    root_project,
    root_expand,
    owner_map,
):
    lowered = right_side.astype(jnp.bfloat16)
    columns = lowered.shape[1]
    root_term = lax.dot_general(
        lowered, root_project, contract_first, preferred_element_type=jnp.float32
    )
    level_coeffs = jnp.einsum(
        "lw,blr->bwr", lowered, row_project, preferred_element_type=jnp.float32
    )
    coeffs = lax.dot_general(
        lowered, compress, contract_first, preferred_element_type=jnp.float32
    ).astype(jnp.bfloat16)
    col_count = lax.axis_size("col")
    pieces = coeffs.reshape(columns, col_count, -1)
    chosen = (owner_map[:, None] == jnp.arange(col_count, dtype=owner_map.dtype)[None, :]).astype(
        jnp.bfloat16
    )
    outgoing = jnp.einsum(
        "kd,wkx->wdx", chosen, pieces, preferred_element_type=jnp.float32
    ).astype(jnp.bfloat16)
    root_shares = root_term.reshape(col_count, -1, root_term.shape[1])
    arrived, root_share, pair, far, dense_part = scatter(
        outgoing.reshape(columns, -1), root_shares, level_coeffs, expand, leaf_inverse, lowered
    )
    pair_sum = (level_coeffs[1] + pair[1]).astype(jnp.bfloat16)
    far_sum = far[0] + far[1]
    returned, root_full, quad_one, quad_two = gather(
        arrived, middle, root_share, pair_sum, far_sum, (row_expand, root_expand), col_count,
        lax.axis_size("row"),
    )
    ordered = jnp.einsum(
        "jd,dxw->jxw", chosen, returned, preferred_element_type=jnp.float32
    ).astype(jnp.bfloat16).reshape(-1, columns)
    cluster_part = jnp.dot(expand, ordered, preferred_element_type=jnp.float32)

    sibling_sum = jnp.stack(
        [pair[0], quad_one.astype(jnp.float32), far_sum + quad_two], axis=0
    )
    root_coeffs = root_full.reshape(columns, -1)
    coupled = jnp.einsum(
        "blr,bwr->lw",
        row_expand,
        sibling_sum.astype(jnp.bfloat16),
        preferred_element_type=jnp.float32,
    )
    root_part = lax.dot_general(
        root_expand, root_coeffs, (((1,), (1,)), ((), ())), preferred_element_type=jnp.float32
    )
    return dense_part + cluster_part + coupled + root_part


def solution(mesh):
    in_specs = (
        P(("row", "col"), None),
        P(("row", "col"), None),
        P(("row", "col"), None),
        P(("row", "col"), None),
        P(("row", "col"), None),
        P(None, ("row", "col"), None),
        P(None, ("row", "col"), None),
        P(("row", "col"), None),
        P(("row", "col"), None),
        P(),
    )
    out_specs = P(("row", "col"), None)
    return jax.shard_map(
        per_device, mesh=mesh, in_specs=in_specs, out_specs=out_specs, check_vma=False
    )
```
